32 devices in a mesh: dp: 16 (over z, x, core), seq: 2 (over y).
Axes of the slice: x: 2, y: 2, z: 4, core: 2. Of those that a mesh axis runs over, the one named last changes fastest.
Arguments:
- tokens: bfloat16 [16, 1024, 768], P('dp', 'seq'), may hold values from -6 to 6
- lengths: int32 [16], P('dp'), may hold values from 513 to 1024, as said below
- cotangent: bfloat16 [16, 1024, 768], P('dp', 'seq'), may hold values from -6 to 6
- norm1_gain: bfloat16 [768], P(('dp', 'seq')), may hold values from 0.099609375 to 1.8984375
- norm1_bias: bfloat16 [768], P(('dp', 'seq')), may hold values from -2 to 2
- w_query: bfloat16 [768, 768], P(('dp', 'seq')), may hold values from -0.21875 to 0.21875
- w_key: bfloat16 [768, 768], P(('dp', 'seq')), may hold values from -0.21875 to 0.21875
- w_value: bfloat16 [768, 768], P(('dp', 'seq')), may hold values from -0.21875 to 0.21875
- shift_taps: bfloat16 [768, 4], P(('dp', 'seq')), may hold values from -3 to 3
- ssm_coef: bfloat16 [768, 64], P(('dp', 'seq')), may hold values from -0.75 to 0.75
- ssm_rate: bfloat16 [768, 64], P(('dp', 'seq')), may hold values from 0.5 to 60
- skip_gain: bfloat16 [768], P(('dp', 'seq')), may hold values from -4 to 4
- w_out: bfloat16 [768, 768], P(('dp', 'seq')), may hold values from -0.21875 to 0.21875
- norm2_gain: bfloat16 [768], P(('dp', 'seq')), may hold values from 0.099609375 to 1.8984375
- norm2_bias: bfloat16 [768], P(('dp', 'seq')), may hold values from -2 to 2
- w_up: bfloat16 [768, 3072], P(('dp', 'seq')), may hold values from -0.21875 to 0.21875
- up_bias: bfloat16 [3072], P(('dp', 'seq')), may hold values from -3 to 3
- w_down: bfloat16 [3072, 768], P(('dp', 'seq')), may hold values from -0.109375 to 0.109375
- down_bias: bfloat16 [768], P(('dp', 'seq')), may hold values from -2 to 2
Outputs:
- mixed: bfloat16 [16, 1024, 768], P('dp', 'seq')
- token_grad: float32 [16, 1024, 768], P('dp', 'seq')
- norm1_gain_grad: float32 [768], P(('dp', 'seq'))
- norm1_bias_grad: float32 [768], P(('dp', 'seq'))
- w_query_grad: float32 [768, 768], P(('dp', 'seq'))
- w_key_grad: float32 [768, 768], P(('dp', 'seq'))
- w_value_grad: float32 [768, 768], P(('dp', 'seq'))
- shift_taps_grad: float32 [768, 4], P(('dp', 'seq'))
- ssm_coef_grad: float32 [768, 64], P(('dp', 'seq'))
- ssm_rate_grad: float32 [768, 64], P(('dp', 'seq'))
- skip_gain_grad: float32 [768], P(('dp', 'seq'))
- w_out_grad: float32 [768, 768], P(('dp', 'seq'))
- norm2_gain_grad: float32 [768], P(('dp', 'seq'))
- norm2_bias_grad: float32 [768], P(('dp', 'seq'))
- w_up_grad: float32 [768, 3072], P(('dp', 'seq'))
- up_bias_grad: float32 [3072], P(('dp', 'seq'))
- w_down_grad: float32 [3072, 768], P(('dp', 'seq'))
- down_bias_grad: float32 [768], P(('dp', 'seq'))
The draws below stay inside these ranges and needn't reach their ends.
Inputs may be any that keep to these rules, and one draw needn't show every extreme that they name: lengths[s] counts the valid leading tokens of sequence s; the rest of its 1024 slots are padding. In every draw one sequence has 1024 valid tokens and another 1024 // 2 + 1.
All inputs are finite; a program needn't handle non-finite values.
Results may differ from the reference program's by a relative error of at most 0.014.
Values may be sent and summed in bfloat16 or wider, within the bound.
No kernel may reach another device: no remote copies, remote signals or barrier semaphores. Data moves between devices by JAX's collectives and lax.ppermute only.
A program may use at most 192 MiB of HBM per device.

```python
import math
import jax
import jax.numpy as jnp
from jax import lax

D = 768
FF = 3072
STATE = 64
SHIFT = 4
LEN = 1024
SEQUENCES = 16


def draw_lengths(key, part):
    first_key, second_key = jax.random.split(key)
    lengths_drawn = jax.random.randint(first_key, (SEQUENCES,), LEN // 2 + 1, LEN + 1, dtype=jnp.int32)
    ranking = jax.random.permutation(second_key, SEQUENCES)
    lengths_drawn = lengths_drawn.at[ranking[0]].set(LEN)
    return lengths_drawn.at[ranking[1]].set(LEN // 2 + 1)


def block_scale(rng, dims, cuts, least, high):
    def one(dim, parts):
        heights = jax.random.uniform(jax.random.fold_in(jax.random.fold_in(rng, 6), dim), (parts,), jnp.float32, least / len(cuts), high / len(cuts))
        return jnp.repeat(jnp.exp(heights), dims[dim] // parts).reshape((-1,) + (1,) * (len(dims) - dim - 1))

    loudness = one(*cuts[0])
    for cut in cuts[1:]:
        loudness = loudness * one(*cut)
    return loudness


def noise(own_key, shape, width, most, shards=(), held_as=jnp.bfloat16):
    drawn = width * jax.random.normal(own_key, shape, jnp.float32)
    if shards:
        drawn = drawn * block_scale(own_key, shape, shards, -0.22, 0.18)
    return jnp.clip(drawn, -most, most).astype(held_as)


def setup_inputs(seed: int = 0) -> dict:
    seeds = jax.random.split(jax.random.key(seed), 20)
    return {
        "tokens": noise(seeds[0], (SEQUENCES, LEN, D), 1.0, 6.0, ((0, 16), (1, 2))),
        "lengths": draw_lengths(jax.random.fold_in(seeds[19], 71), 0),
        "cotangent": noise(seeds[2], (SEQUENCES, LEN, D), 1.0, 6.0, ((0, 16), (1, 2))),
        "norm1_gain": jnp.clip(1.0 + 0.18 * jax.random.normal(seeds[3], (D,), jnp.float32), 0.099609375, 1.8984375).astype(jnp.bfloat16),
        "norm1_bias": noise(seeds[4], (D,), 0.3, 2.0, ((0, 32),)),
        "w_query": noise(seeds[5], (D, D), D ** -0.5, 0.21875, ((0, 32),)),
        "w_key": noise(seeds[6], (D, D), D ** -0.5, 0.21875, ((0, 32),)),
        "w_value": noise(seeds[7], (D, D), D ** -0.5, 0.21875, ((0, 32),)),
        "shift_taps": noise(seeds[8], (D, SHIFT), 0.5, 3.0, ((0, 32),)),
        "ssm_coef": noise(seeds[9], (D, STATE), STATE ** -0.5, 0.75, ((0, 32),)),
        "ssm_rate": jnp.clip(jnp.exp(math.log(60.0) - 4.787492 * jax.random.uniform(seeds[10], (D, STATE), jnp.float32) ** block_scale(seeds[10], (D, STATE), ((0, 32),), -0.2, 0.2)), 0.5, 60.0).astype(jnp.bfloat16),
        "skip_gain": noise(seeds[11], (D,), 1.0, 4.0, ((0, 32),)),
        "w_out": noise(seeds[12], (D, D), D ** -0.5, 0.21875, ((0, 32),)),
        "norm2_gain": jnp.clip(1.0 + 0.18 * jax.random.normal(seeds[13], (D,), jnp.float32), 0.099609375, 1.8984375).astype(jnp.bfloat16),
        "norm2_bias": noise(seeds[14], (D,), 0.3, 2.0, ((0, 32),)),
        "w_up": noise(seeds[15], (D, FF), D ** -0.5, 0.21875, ((0, 32),)),
        "up_bias": noise(seeds[16], (FF,), 0.5, 3.0, ((0, 32),)),
        "w_down": noise(seeds[17], (FF, D), FF ** -0.5, 0.109375, ((0, 32),)),
        "down_bias": noise(seeds[18], (D,), 0.3, 2.0, ((0, 32),)),
    }


EPS = 1e-05
HIGHEST = lax.Precision.HIGHEST

@jax.custom_vjp
def low(v):
    return lax.optimization_barrier(v.astype(jnp.bfloat16)).astype(jnp.float32)

@jax.custom_vjp
def low_back(v):
    return v

def low_keep(v):
    return (low(v), None)

def low_pass(kept, grad):
    return (grad,)

def back_keep(v):
    return (v, None)

def back_low(kept, grad):
    return (low(grad),)
low.defvjp(low_keep, low_pass)
low_back.defvjp(back_keep, back_low)

def layer_norm(values, norm_gain, norm_bias):
    row_mean = lax.optimization_barrier(jnp.mean(values, axis=-1, keepdims=True))
    centred = values - row_mean
    variance = lax.optimization_barrier(jnp.mean(centred * centred, axis=-1, keepdims=True))
    return centred * lax.rsqrt(variance + EPS) * norm_gain + norm_bias

def project(values, weight):
    flat_rows = values.reshape(-1, values.shape[-1])
    result = jnp.dot(flat_rows, weight, precision=HIGHEST, preferred_element_type=jnp.float32)
    return result.reshape(values.shape[:-1] + (weight.shape[1],))

def ssm_kernel(coef, rate):
    times = jnp.arange(LEN, dtype=jnp.float32) / LEN

    def one_block(pieces):
        coef_block, rate_block = pieces
        decay = jnp.exp(-rate_block[:, :, None] * times)
        return lax.optimization_barrier(jnp.sum(coef_block[:, :, None] * decay, axis=1))
    blocks = lax.map(jax.checkpoint(one_block), (coef.reshape(-1, 128, STATE), rate.reshape(-1, 128, STATE)))
    return blocks.reshape(D, LEN).T * LEN ** (-0.5)

def mixer_layer(group_tokens, weights, kernel):
    norm1_gain, norm1_bias, w_query, w_key, w_value, shift_taps, skip_gain, w_out, norm2_gain, norm2_bias, w_up, up_bias, w_down, down_bias = weights
    first_rows = low(layer_norm(group_tokens, norm1_gain, norm1_bias))
    queries = low_back(low(project(first_rows, w_query)))
    keys_all = low_back(low(project(first_rows, w_key)))
    values_all = low_back(low(project(first_rows, w_value)))
    padded = jnp.pad(keys_all, ((0, 0), (SHIFT - 1, 0), (0, 0)))
    shifted = jnp.zeros_like(keys_all)
    for tap_index in range(SHIFT):
        start_at = SHIFT - 1 - tap_index
        shifted = shifted + padded[:, start_at:start_at + LEN] * shift_taps[:, tap_index]
    products = shifted * values_all
    fft_size = 2 * LEN
    spectrum = jnp.fft.rfft(products, n=fft_size, axis=1) * jnp.fft.rfft(kernel, n=fft_size, axis=0)[None]
    convolved = jnp.fft.irfft(spectrum, n=fft_size, axis=1)[:, :LEN] + skip_gain * products
    mixer_out = low_back(low(queries * convolved))
    residual = group_tokens + low_back(project(mixer_out, w_out))
    second_rows = low(layer_norm(residual, norm2_gain, norm2_bias))
    preact = low_back(project(second_rows, w_up) + up_bias)
    activated = low(jax.nn.gelu(preact))
    return residual + project(activated, w_down) + down_bias

def reference(tokens, lengths, cotangent, norm1_gain, norm1_bias, w_query, w_key, w_value, shift_taps, ssm_coef, ssm_rate, skip_gain, w_out, norm2_gain, norm2_bias, w_up, up_bias, w_down, down_bias):
    weights = tuple((item.astype(jnp.float32) for item in (norm1_gain, norm1_bias, w_query, w_key, w_value, shift_taps, skip_gain, w_out, norm2_gain, norm2_bias, w_up, up_bias, w_down, down_bias)))
    kernel, kernel_back = jax.vjp(ssm_kernel, ssm_coef.astype(jnp.float32), ssm_rate.astype(jnp.float32))
    group_size = 4
    groups = SEQUENCES // group_size
    positions = jnp.arange(LEN, dtype=jnp.int32)

    def one_group(carry, pieces):
        weight_sums, kernel_sum = carry
        group_tokens, group_cot, group_lengths = pieces
        valid_mask = (positions[None, :] < group_lengths[:, None]).astype(jnp.float32)
        result, pullback = jax.vjp(mixer_layer, group_tokens.astype(jnp.float32), weights, kernel)
        token_part, weight_part, kernel_part = pullback(group_cot.astype(jnp.float32) * valid_mask[:, :, None])
        new_sums = jax.tree.map(lambda total, extra: total + extra, weight_sums, weight_part)
        return ((new_sums, kernel_sum + kernel_part), (result.astype(jnp.bfloat16), token_part))
    start_sums = jax.tree.map(jnp.zeros_like, weights)
    (weight_sums, kernel_sum), (mixed, token_grad) = lax.scan(one_group, (start_sums, jnp.zeros_like(kernel)), (tokens.reshape(groups, group_size, LEN, D), cotangent.reshape(groups, group_size, LEN, D), lengths.reshape(groups, group_size)))
    coef_grad, rate_grad = kernel_back(kernel_sum)
    g1_grad, b1_grad, query_grad, key_grad, value_grad, taps_grad, skip_grad, out_grad, g2_grad, b2_grad, up_grad, up_bias_grad, down_grad, down_bias_grad = weight_sums
    return (mixed.reshape(SEQUENCES, LEN, D), token_grad.reshape(SEQUENCES, LEN, D), g1_grad, b1_grad, query_grad, key_grad, value_grad, taps_grad, coef_grad, rate_grad, skip_grad, out_grad, g2_grad, b2_grad, up_grad, up_bias_grad, down_grad, down_bias_grad)
```

```python
import functools
import math

import jax
import jax.numpy as jnp
from jax import lax
from jax.experimental import pallas as pl
from jax.experimental.pallas import tpu as pltpu
from jax.sharding import Mesh, PartitionSpec as P

EPS = 1e-05
BF = jnp.bfloat16
F32 = jnp.float32
SQRT_2_PI = math.sqrt(2.0 / math.pi)
MISC = ("r", "x", "y")


def flip(value, axis):
    return lax.ppermute(value, axis, [(0, 1), (1, 0)])


def ordered(mine, other, place, axis):
    first = jnp.where(place == 0, mine, other)
    second = jnp.where(place == 0, other, mine)
    return jnp.stack([first, second], axis=axis)


def swap_cy(value):
    return lax.ppermute(value, ("c", "y"), [(0, 0), (1, 2), (2, 1), (3, 3)])


def ring_gather(block, ring):
    place = lax.axis_index("r")
    whole = jnp.zeros((ring,) + block.shape, block.dtype)
    whole = lax.dynamic_update_slice_in_dim(whole, block[None], place, 0)
    perm = [(i, (i + 1) % ring) for i in range(ring)]
    for step in range(1, ring):
        block = lax.ppermute(block, "r", perm)
        whole = lax.dynamic_update_slice_in_dim(
            whole, block[None], lax.rem(place - step + ring, ring), 0
        )
    return whole


def gather_yxr(block, ring):
    pair = ordered(block, flip(block, "y"), lax.axis_index("y"), 0)
    quad = ordered(pair, flip(pair, "x"), lax.axis_index("x"), 0)
    return ring_gather(quad, ring)


def gather_rxy(block, ring):
    whole = ring_gather(block, ring)
    pair = ordered(whole, flip(whole, "x"), lax.axis_index("x"), 1)
    return ordered(pair, flip(pair, "y"), lax.axis_index("y"), 2)


def ring_scatter(parts, ring):
    place = lax.axis_index("r")
    perm = [(i, (i + 1) % ring) for i in range(ring)]

    def own(back):
        return lax.dynamic_index_in_dim(
            parts, lax.rem(place - back + ring, ring), 0, keepdims=False
        ).astype(F32)

    total = own(1)
    for step in range(1, ring):
        moved = lax.ppermute(total.astype(parts.dtype), "r", perm)
        back = (step + 1) % ring
        total = moved.astype(F32) + own(back)
    return total


def half_scatter(parts, axis, dim):
    place = lax.axis_index(axis)
    keep = lax.dynamic_index_in_dim(parts, place, dim, keepdims=False)
    send = lax.dynamic_index_in_dim(parts, 1 - place, dim, keepdims=False)
    return keep.astype(F32) + flip(send, axis).astype(F32)


def scatter_yxr(parts, ring):
    kind = parts.dtype
    parts = half_scatter(parts, "y", 2).astype(kind)
    parts = half_scatter(parts, "x", 1).astype(kind)
    return ring_scatter(parts, ring)


def scatter_rxy(parts, ring):
    kind = parts.dtype
    parts = ring_scatter(parts, ring).astype(kind)
    parts = half_scatter(parts, "x", 0).astype(kind)
    return half_scatter(parts, "y", 0)


def own_columns(rows, core, groups):
    count, cols = rows.shape
    grid = rows.reshape(count, groups, 2, cols // (2 * groups))
    keep = jnp.where(core == 0, grid[:, :, 0], grid[:, :, 1])
    send = jnp.where(core == 0, grid[:, :, 1], grid[:, :, 0])
    return keep.reshape(count, -1), send.reshape(count, -1)


def split_columns(rows, core, groups):
    keep, send = own_columns(rows, core, groups)
    return ordered(keep, flip(send, "c"), core, 0)


def merge_columns(parts, core, groups):
    keep = lax.dynamic_index_in_dim(parts, core, 0, keepdims=False)
    send = lax.dynamic_index_in_dim(parts, 1 - core, 0, keepdims=False)
    count, cols = keep.shape
    other = flip(send.astype(BF), "c").astype(F32)
    grid = ordered(
        keep.reshape(count, groups, -1), other.reshape(count, groups, -1), core, 2
    )
    return grid.reshape(count, 2 * cols)


def mm(left, right):
    return jnp.dot(left, right, preferred_element_type=F32)


def mm_tn(left, right):
    return lax.dot_general(
        left, right, (((0,), (0,)), ((), ())), preferred_element_type=F32
    )


def mm_nt(left, right):
    return lax.dot_general(
        left, right, (((1,), (1,)), ((), ())), preferred_element_type=F32
    )


def norm_stats(values):
    mean = jnp.mean(values, axis=-1, keepdims=True)
    centred = values - mean
    variance = jnp.mean(centred * centred, axis=-1, keepdims=True)
    scale = lax.rsqrt(variance + EPS)
    return centred * scale, scale


def norm_back(grad, unit, scale, gain):
    inner = grad * gain
    mean_one = jnp.mean(inner, axis=-1, keepdims=True)
    mean_two = jnp.mean(inner * unit, axis=-1, keepdims=True)
    return scale * (inner - mean_one - unit * mean_two)


def dft_tables(length):
    part = 32
    blocks = length // part
    step = math.pi / (2.0 * length)
    times = lax.broadcasted_iota(jnp.int32, (blocks, length), 1)
    high = lax.broadcasted_iota(jnp.int32, (blocks, length), 0)
    low = lax.broadcasted_iota(jnp.int32, (part, length), 0)
    low_times = lax.broadcasted_iota(jnp.int32, (part, length), 1)
    high, low = lax.optimization_barrier((high, low))
    period = 4 * length
    angle_high = (2 * part * high * times % period).astype(F32) * step
    angle_low = ((2 * low + 1) * low_times % period).astype(F32) * step
    cos_high, sin_high = jnp.cos(angle_high)[:, None], jnp.sin(angle_high)[:, None]
    cos_low, sin_low = jnp.cos(angle_low)[None], jnp.sin(angle_low)[None]
    cos_all = (cos_high * cos_low - sin_high * sin_low).reshape(length, length)
    sin_all = (sin_high * cos_low + cos_high * sin_low).reshape(length, length)
    return cos_all.astype(BF), sin_all.astype(BF)


def kernel_body(part, coef_ref, rate_ref, out_ref, high_ref, low_ref):
    states = coef_ref.shape[0]
    length = out_ref.shape[0]
    blocks = length // part
    lanes = out_ref.shape[1]
    high_ids = lax.broadcasted_iota(jnp.int32, (blocks, lanes), 0).astype(F32) * (part / length)
    low_ids = lax.broadcasted_iota(jnp.int32, (part, lanes), 0).astype(F32) * (1.0 / length)

    def fill(state, carry):
        rate = rate_ref[pl.ds(state, 1), :]
        coef = coef_ref[pl.ds(state, 1), :] * (length ** (-0.5))
        high_ref[state] = coef * jnp.exp(-rate * high_ids)
        low_ref[state] = jnp.exp(-rate * low_ids)
        return carry

    lax.fori_loop(0, states, fill, 0)
    for start in range(0, blocks, 8):

        def add(state, sums):
            low = low_ref[state]
            return tuple(
                total + high_ref[state, pl.ds(start + index, 1), :] * low
                for index, total in enumerate(sums)
            )

        zero = jnp.zeros((part, lanes), F32)
        sums = lax.fori_loop(0, states, add, (zero,) * 8)
        for index, total in enumerate(sums):
            out_ref[pl.ds((start + index) * part, part), :] = total


def ssm_kernel(coef, rate, length):
    states, channels = coef.shape
    part = 32
    return pl.pallas_call(
        functools.partial(kernel_body, part),
        out_shape=jax.ShapeDtypeStruct((length, channels), F32),
        grid=(channels // 128,),
        in_specs=[pl.BlockSpec((states, 128), lambda i: (0, i))] * 2,
        out_specs=pl.BlockSpec((length, 128), lambda i: (0, i)),
        scratch_shapes=[
            pltpu.VMEM((states, length // part, 128), F32),
            pltpu.VMEM((states, part, 128), F32),
        ],
        cost_estimate=pl.CostEstimate(
            flops=2 * length * states * channels, bytes_accessed=2 * length * channels * 4, transcendentals=0
        ),
        name="ssm_kernel",
    )(coef, rate)


def kernel_grad_body(grad_ref, coef_ref, rate_ref, coef_out, rate_out):
    length = grad_ref.shape[0]
    ratio = jnp.exp(rate_ref[...] * (-1.0 / length))
    scale = length ** (-0.5)

    def step(index, carry):
        value, slope = carry
        base = pl.multiple_of(length - 8 - index * 8, 8)
        rows = grad_ref[pl.ds(base, 8), :]
        for sub in range(7, -1, -1):
            slope = slope * ratio + value
            value = value * ratio + rows[sub : sub + 1, :]
        return value, slope

    zero = jnp.zeros(ratio.shape, F32)
    value, slope = lax.fori_loop(0, length // 8, step, (zero, zero))
    coef_out[...] = value * scale
    rate_out[...] = slope * ratio * coef_ref[...] * (-scale / length)


def ssm_kernel_grads(grad, coef, rate):
    states, channels = coef.shape
    length = grad.shape[0]
    small = pl.BlockSpec((states, 128), lambda i: (0, i))
    return pl.pallas_call(
        kernel_grad_body,
        out_shape=(jax.ShapeDtypeStruct((states, channels), F32),) * 2,
        grid=(channels // 128,),
        in_specs=[pl.BlockSpec((length, 128), lambda i: (0, i)), small, small],
        out_specs=(small, small),
        cost_estimate=pl.CostEstimate(
            flops=4 * length * states * channels, bytes_accessed=length * channels * 4, transcendentals=0
        ),
        name="ssm_kernel_grads",
    )(grad, coef, rate)


def body(
    ring,
    tokens,
    lengths,
    cotangent,
    norm1_gain,
    norm1_bias,
    w_query,
    w_key,
    w_value,
    shift_taps,
    ssm_coef,
    ssm_rate,
    skip_gain,
    w_out,
    norm2_gain,
    norm2_bias,
    w_up,
    up_bias,
    w_down,
    down_bias,
):
    core = lax.axis_index("c")
    groups = 2 * ring
    _, block_len, width = tokens.shape
    length = 2 * block_len
    rows = w_query.shape[0]
    up_rows = up_bias.shape[0]
    hidden = w_up.shape[1]
    states = ssm_coef.shape[1]
    tap_count = shift_taps.shape[1]
    channels = width // 2

    vectors = jnp.stack([norm1_gain, norm1_bias, norm2_gain, norm2_bias, down_bias])
    misc = jnp.concatenate(
        [
            ssm_coef.reshape(-1),
            ssm_rate.reshape(-1),
            shift_taps.reshape(-1),
            skip_gain,
            up_bias,
            vectors.reshape(-1),
        ]
    )
    misc_len = misc.shape[0]
    misc_pad = -misc_len % 1024
    misc = jnp.pad(misc, (0, misc_pad)).reshape(-1, 128)
    misc_all = gather_yxr(misc, ring).reshape(groups * 2, -1)
    cuts = []
    offset = 0
    for size in (rows * states, rows * states, rows * tap_count, rows, up_rows, 5 * rows):
        cuts.append(misc_all[:, offset : offset + size].astype(F32))
        offset += size
    coef = cuts[0].reshape(channels, states).T
    rate = cuts[1].reshape(channels, states).T
    taps = cuts[2].reshape(channels, tap_count).T
    skip = cuts[3].reshape(1, channels)
    up_bias_own = cuts[4].reshape(1, hidden // 2)
    vec_own = cuts[5].astype(BF).reshape(groups, 2, 5, rows)
    vec_all = ordered(vec_own, flip(vec_own, "c"), core, 1)
    vec_all = vec_all.transpose(3, 0, 1, 2, 4).reshape(5, 1, width).astype(F32)
    gain_one, bias_one, gain_two, bias_two, down_bias_all = [vec_all[i] for i in range(5)]

    start = lax.axis_index("y") * block_len
    valid = start + lax.broadcasted_iota(jnp.int32, (block_len, 1), 0) < lengths[0]
    masked = jnp.where(valid, cotangent[0], jnp.zeros((), BF))
    token_half = swap_cy(tokens[0])
    grad_half = swap_cy(masked)
    token_all = ordered(token_half, flip(token_half, "c"), core, 0).reshape(length, width)
    grad_all = ordered(grad_half, flip(grad_half, "c"), core, 0).reshape(length, width)

    qkv = jnp.concatenate(
        [split_columns(w, core, groups).reshape(2 * rows, channels) for w in (w_query, w_key, w_value)],
        axis=1,
    ).reshape(2, rows, 3, channels)
    qkv = qkv.transpose(2, 0, 1, 3)
    qkv_all = jnp.concatenate(
        [
            gather_rxy(qkv[:, :, : rows // 2], ring),
            gather_yxr(qkv[:, :, rows // 2 :], ring),
        ],
        axis=5,
    )
    qkv_all = qkv_all.transpose(3, 0, 1, 4, 2, 5, 6).reshape(3, width, channels)
    w_q, w_k, w_v = qkv_all[0], qkv_all[1], qkv_all[2]
    out_own = lax.all_gather(w_out, MISC, axis=0, tiled=True)
    up_parts = split_columns(w_up, core, groups)
    up_own = lax.all_gather(up_parts, MISC, axis=0, tiled=False)
    up_own = up_own.reshape(groups, 2, 2, rows, hidden // 2).transpose(0, 2, 1, 3, 4)
    up_own = up_own.reshape(width, hidden // 2)
    down_own = lax.all_gather(w_down, MISC, axis=0, tiled=True)

    cos_t, sin_t = dft_tables(length)
    kernel = ssm_kernel(coef, rate, length)
    inputs = token_all.astype(F32)
    unit_one, _ = norm_stats(inputs)
    first_rows = (unit_one * gain_one + bias_one).astype(BF)
    query = mm(first_rows, w_q).astype(BF)
    key = mm(first_rows, w_k).astype(BF)
    value = mm(first_rows, w_v).astype(BF)
    query_f, key_f, value_f = query.astype(F32), key.astype(F32), value.astype(F32)
    padded = jnp.pad(key_f, ((tap_count - 1, 0), (0, 0)))
    shifted = jnp.zeros_like(key_f)
    for tap in range(tap_count):
        at = tap_count - 1 - tap
        shifted = shifted + padded[at : at + length] * taps[tap : tap + 1]
    products = shifted * value_f
    both = jnp.concatenate([products.astype(BF), kernel.astype(BF)], axis=1)
    both_re = mm(cos_t, both)
    both_im = mm(sin_t, both)
    prod_re, kern_re = both_re[:, :channels], both_re[:, channels:]
    prod_im, kern_im = both_im[:, :channels], both_im[:, channels:]
    spec_re = (prod_re * kern_re - prod_im * kern_im).astype(BF)
    spec_im = (prod_re * kern_im + prod_im * kern_re).astype(BF)
    convolved = (mm_tn(cos_t, spec_re) + mm_tn(sin_t, spec_im)) * (1.0 / length)
    convolved = convolved + skip * products
    mixed_heads = (query_f * convolved).astype(BF)
    mixed_other = flip(mixed_heads, "c")
    out_other = flip(out_own, "c")
    residual = inputs + mm(mixed_heads, out_own) + mm(mixed_other, out_other)
    unit_two, scale_two = norm_stats(residual)
    second_rows = (unit_two * gain_two + bias_two).astype(BF)
    preact = mm(second_rows, up_own) + up_bias_own
    bend = jnp.tanh(SQRT_2_PI * (preact + 0.044715 * preact * preact * preact))
    activated = (0.5 * preact * (1.0 + bend)).astype(BF)
    slope = 0.5 * (1.0 + bend) + 0.5 * preact * (1.0 - bend * bend) * SQRT_2_PI * (
        1.0 + 3.0 * 0.044715 * preact * preact
    )
    slope = slope.astype(BF)

    def mine(array):
        return lax.dynamic_slice_in_dim(array, core * block_len, block_len, 0)

    def theirs(array):
        return lax.dynamic_slice_in_dim(array, (1 - core) * block_len, block_len, 0)

    down_part = mm(activated, down_own)
    down_other = flip(theirs(down_part).astype(BF), "c").astype(F32)
    mixed = mine(residual) + mine(down_part) + down_other + down_bias_all
    mixed = swap_cy(mixed.astype(BF))[None]

    def tree(parts):
        return parts.reshape((ring, 2, 2) + parts.shape[1:])

    down_grad = mm_tn(activated, grad_all).astype(BF)
    act_grad = mm_nt(grad_all, down_own)
    pre_grad_f = act_grad * slope.astype(F32)
    pre_grad = pre_grad_f.astype(BF)
    up_grad = mm_tn(second_rows, pre_grad).astype(BF)
    up_bias_grad = jnp.sum(pre_grad.astype(F32), axis=0)
    second_part = mm_nt(pre_grad, up_own)
    second_other = flip(theirs(second_part).astype(BF), "c").astype(F32)
    second_grad = mine(second_part) + second_other
    unit_two_h, scale_two_h = mine(unit_two), mine(scale_two)
    grad_half_f = grad_half.astype(F32)
    gain_two_grad = jnp.sum(second_grad * unit_two_h, axis=0)
    bias_two_grad = jnp.sum(second_grad, axis=0)
    down_bias_grad = jnp.sum(grad_half_f, axis=0)
    resid_grad = grad_half_f + norm_back(second_grad, unit_two_h, scale_two_h, gain_two)
    mix_half = resid_grad.astype(BF)
    mix_grad = ordered(mix_half, flip(mix_half, "c"), core, 0).reshape(length, width)

    down_sum = down_grad.reshape(groups, 2, up_rows, width)
    down_one = scatter_yxr(
        down_sum[:, :, : up_rows // 2].reshape(ring, 2, 2, up_rows // 2, width), ring
    )
    down_two = scatter_rxy(
        down_sum[:, :, up_rows // 2 :].reshape(ring, 2, 2, up_rows // 2, width), ring
    )
    down_s = jnp.concatenate([down_one, down_two], axis=0)
    up_sum = up_grad.reshape(ring, 2, 2, 2, rows, hidden // 2).transpose(0, 1, 3, 2, 4, 5)
    up_one = scatter_yxr(up_sum[:, :, :, :, : rows // 2], ring)
    up_two = scatter_rxy(up_sum[:, :, :, :, rows // 2 :], ring)
    up_s = merge_columns(jnp.concatenate([up_one, up_two], axis=1), core, groups)

    out_grad = mm_tn(mixed_heads, mix_grad).astype(BF)
    head_grad = mm_nt(mix_grad, out_own).astype(BF).astype(F32)
    query_grad = (head_grad * convolved).astype(BF)
    conv_grad = head_grad * query_f
    skip_grad = jnp.sum(conv_grad * products, axis=0)
    conv_low = conv_grad.astype(BF)
    grad_re = mm(cos_t, conv_low)
    grad_im = mm(sin_t, conv_low)
    back_re = jnp.concatenate(
        [grad_re * kern_re + grad_im * kern_im, grad_re * prod_re + grad_im * prod_im], axis=1
    ).astype(BF)
    back_im = jnp.concatenate(
        [grad_im * kern_re - grad_re * kern_im, grad_im * prod_re - grad_re * prod_im], axis=1
    ).astype(BF)
    back = (mm_tn(cos_t, back_re) + mm_tn(sin_t, back_im)) * (1.0 / length)
    product_grad = back[:, :channels] + skip * conv_grad
    kernel_grad = back[:, channels:]
    shifted_grad = product_grad * value_f
    value_grad = (product_grad * shifted).astype(BF)
    padded_grad = jnp.pad(shifted_grad, ((0, tap_count - 1), (0, 0)))
    key_grad = jnp.zeros_like(key_f)
    tap_rows = []
    for tap in range(tap_count):
        at = tap_count - 1 - tap
        key_grad = key_grad + padded_grad[tap : tap + length] * taps[tap : tap + 1]
        tap_rows.append(jnp.sum(shifted_grad * padded[at : at + length], axis=0))
    key_grad = key_grad.astype(BF)
    coef_grad, rate_grad = ssm_kernel_grads(kernel_grad, coef, rate)
    qkv_grad = jnp.stack(
        [mm_tn(first_rows, g).astype(BF) for g in (query_grad, key_grad, value_grad)]
    )
    first_part = mm_nt(query_grad, w_q) + mm_nt(key_grad, w_k) + mm_nt(value_grad, w_v)
    first_other = flip(theirs(first_part).astype(BF), "c").astype(F32)
    first_grad = mine(first_part) + first_other
    unit_one_h, scale_one_h = norm_stats(token_half.astype(F32))
    gain_one_grad = jnp.sum(first_grad * unit_one_h, axis=0)
    bias_one_grad = jnp.sum(first_grad, axis=0)
    token_grad = resid_grad + norm_back(first_grad, unit_one_h, scale_one_h, gain_one)
    token_grad = swap_cy(token_grad.astype(BF)).astype(F32)[None]

    qkv_sum = qkv_grad.reshape(3, ring, 2, 2, 2, rows, channels).transpose(1, 2, 4, 0, 3, 5, 6)
    out_sum = out_grad.reshape(ring, 2, 2, 1, rows, width)
    out_sum = out_sum.reshape(ring, 2, 2, 1, rows, 2, channels).transpose(0, 1, 2, 3, 5, 4, 6)
    mix_sum = jnp.concatenate([qkv_sum, out_sum], axis=3)
    mix_one = scatter_yxr(mix_sum[:, :, :, :, :, : rows // 2], ring)
    mix_two = scatter_rxy(mix_sum[:, :, :, :, :, rows // 2 :], ring)
    mix_s = jnp.concatenate([mix_one, mix_two], axis=2)
    query_s = merge_columns(mix_s[0], core, groups)
    key_s = merge_columns(mix_s[1], core, groups)
    value_s = merge_columns(mix_s[2], core, groups)
    out_s = mix_s[3].transpose(1, 0, 2).reshape(rows, width)

    vec_grads = jnp.stack(
        [gain_one_grad, bias_one_grad, gain_two_grad, bias_two_grad, down_bias_grad]
    )
    vec_grads = vec_grads.reshape(5, ring, 2, 2, 2, rows)
    vec_keep = lax.dynamic_index_in_dim(vec_grads, core, 3, keepdims=False)
    vec_send = lax.dynamic_index_in_dim(vec_grads, 1 - core, 3, keepdims=False)
    vec_sum = (vec_keep + flip(vec_send, "c")).transpose(1, 2, 3, 0, 4)

    def flat(array):
        return array.reshape(ring, 2, 2, -1)

    small = jnp.concatenate(
        [
            flat(coef_grad.T),
            flat(rate_grad.T),
            flat(jnp.stack(tap_rows, axis=1)),
            flat(skip_grad),
            flat(up_bias_grad),
            flat(vec_sum),
        ],
        axis=3,
    )
    small = jnp.pad(small, ((0, 0), (0, 0), (0, 0), (0, misc_pad)))
    small = small.reshape(ring, 2, 2, -1, 128)
    small = scatter_yxr(small, ring).reshape(-1)
    pieces = []
    offset = 0
    for size in (rows * states, rows * states, rows * tap_count, rows, up_rows, 5 * rows):
        pieces.append(small[offset : offset + size])
        offset += size
    vec_s = pieces[5].reshape(5, rows)
    return (
        mixed,
        token_grad,
        vec_s[0],
        vec_s[1],
        query_s,
        key_s,
        value_s,
        pieces[2].reshape(rows, tap_count),
        pieces[0].reshape(rows, states),
        pieces[1].reshape(rows, states),
        pieces[3],
        out_s,
        vec_s[2],
        vec_s[3],
        up_s,
        pieces[4],
        down_s,
        vec_s[4],
    )


def solution(mesh):
    dp_size, seq_size = mesh.devices.shape
    ring = dp_size // 4
    grid = Mesh(mesh.devices.reshape(ring, 2, 2, seq_size), ("r", "x", "c", "y"))
    dp = ("r", "x", "c")
    act = P(dp, "y", None)
    vec = P(dp + ("y",))
    mat = P(dp + ("y",), None)
    return jax.shard_map(
        functools.partial(body, ring),
        mesh=grid,
        in_specs=(
            act, P(dp), act, vec, vec, mat, mat, mat, mat, mat, mat, vec, mat, vec, vec, mat, vec, mat, vec,
        ),
        out_specs=(
            act, act, vec, vec, mat, mat, mat, mat, mat, mat, vec, mat, vec, vec, mat, vec, mat, vec,
        ),
        check_vma=False,
    )
```

```python
import functools
import math

import jax
import jax.numpy as jnp
from jax import lax
from jax.experimental import pallas as pl
from jax.experimental.pallas import tpu as pltpu
from jax.sharding import Mesh, PartitionSpec as P

EPS = 1e-05
BF = jnp.bfloat16
F32 = jnp.float32
SQRT_2_PI = math.sqrt(2.0 / math.pi)
MISC = ("r", "x", "y")


def flip(value, axis):
    return lax.ppermute(value, axis, [(0, 1), (1, 0)])


def ordered(mine, other, place, axis):
    first = jnp.where(place == 0, mine, other)
    second = jnp.where(place == 0, other, mine)
    return jnp.stack([first, second], axis=axis)


def swap_cy(value):
    moved = lax.ppermute(value, ("c", "y"), [(1, 2), (2, 1)])
    return jnp.where(lax.axis_index("c") == lax.axis_index("y"), value, moved)


def shift_ring(value, distance, ring):
    return lax.ppermute(value, "r", [(i, (i + distance) % ring) for i in range(ring)])


def flip_xy(value):
    return lax.ppermute(value, ("x", "y"), [(i, 3 - i) for i in range(4)])


def place(whole, part, starts):
    return lax.dynamic_update_slice(whole, part, starts)


def gather_ring(block, ring):
    here = lax.axis_index("r")
    rest = (0,) * block.ndim
    whole = jnp.zeros((ring,) + block.shape, block.dtype)
    whole = place(whole, block[None], (here,) + rest)
    for distance in range(1, ring):
        moved = shift_ring(block, distance, ring)
        whole = place(whole, moved[None], (lax.rem(here - distance + ring, ring),) + rest)
    return whole


def gather_near(block):
    half = block.shape[-1] // 256 * 128
    one, two = block[..., :half], block[..., half:]
    x, y = lax.axis_index("x"), lax.axis_index("y")
    return (
        lambda: (flip(one, "y"), flip(two, "x")),
        lambda moved: (ordered(one, moved[0], y, 0), ordered(two, moved[1], x, 0)),
        lambda pair: (flip(pair[0], "x"), flip(pair[1], "y")),
        lambda pair, moved: (ordered(pair[0], moved[0], x, 0), ordered(pair[1], moved[1], y, 1)),
    )


def place_near(quads):
    both = [quad.transpose(2, 0, 3, 1, 4, 5) for quad in quads]
    return jnp.concatenate(both, axis=5)


def split_half(parts):
    half = parts.shape[-1] // 256 * 128
    return parts[..., :half], parts[..., half:]


def take(parts, axis, index):
    return lax.dynamic_index_in_dim(parts, index, axis, keepdims=False)


def cut(parts, starts, sizes):
    full = tuple(1 if size is None else size for size in sizes)
    block = lax.dynamic_slice(parts, starts, full)
    return block.reshape(tuple(size for size in sizes if size is not None)).astype(F32)


def scatter_one(parts):
    x, y = lax.axis_index("x"), lax.axis_index("y")
    one, two = split_half(parts)
    return flip(take(one, 3, 1 - y), "y"), flip(take(two, 1, 1 - x), "x")


def scatter_two(parts, moved):
    x, y = lax.axis_index("x"), lax.axis_index("y")
    one, two = split_half(parts)
    ring, _, cores, _, rows, half = one.shape
    other = two.shape[-1]
    send_one = cut(one, (0, 1 - x, 0, y, 0, 0), (ring, None, cores, None, rows, half))
    send_one = send_one + cut(moved[0], (0, 1 - x, 0, 0, 0), (ring, None, cores, rows, half))
    send_two = cut(two, (0, x, 0, 1 - y, 0, 0), (ring, None, cores, None, rows, other))
    send_two = send_two + cut(moved[1], (0, 0, 1 - y, 0, 0), (ring, cores, None, rows, other))
    return flip(send_one.astype(BF), "x"), flip(send_two.astype(BF), "y")


def scatter_held(parts, moved_one, moved_two, place_r):
    x, y = lax.axis_index("x"), lax.axis_index("y")
    one, two = split_half(parts)
    _, _, cores, _, rows, half = one.shape
    other = two.shape[-1]
    held_one = cut(one, (place_r, x, 0, y, 0, 0), (None, None, cores, None, rows, half))
    held_one = held_one + cut(moved_one[0], (place_r, x, 0, 0, 0), (None, None, cores, rows, half))
    held_one = held_one + cut(moved_two[0], (place_r, 0, 0, 0), (None, cores, rows, half))
    held_two = cut(two, (place_r, x, 0, y, 0, 0), (None, None, cores, None, rows, other))
    held_two = held_two + cut(moved_one[1], (place_r, 0, y, 0, 0), (None, cores, None, rows, other))
    held_two = held_two + cut(moved_two[1], (place_r, 0, 0, 0), (None, cores, rows, other))
    return jnp.concatenate([held_one, held_two], axis=-1)


def scatter_three(parts, moved_one, moved_two, ring):
    here = lax.axis_index("r")
    moved = []
    for distance in range(1, ring):
        held = scatter_held(parts, moved_one, moved_two, lax.rem(here + distance, ring))
        moved.append(shift_ring(held.astype(BF), distance, ring))
    return scatter_held(parts, moved_one, moved_two, here), tuple(moved)


def scatter_sum(held, moved):
    total = held
    for part in moved:
        total = total + part.astype(F32)
    return total


def scatter_near(pick):
    x, y = lax.axis_index("x"), lax.axis_index("y")
    total = pick(x, y).astype(F32)
    total = total + flip(pick(x, 1 - y), "y").astype(F32)
    total = total + flip(pick(1 - x, y), "x").astype(F32)
    return total + flip_xy(pick(1 - x, 1 - y)).astype(F32)


def gather_small(block, ring):
    x, y = lax.axis_index("x"), lax.axis_index("y")
    whole = gather_ring(block, ring)
    rest = (0,) * block.ndim
    parts = ((whole, x, y), (flip(whole, "y"), x, 1 - y), (flip(whole, "x"), 1 - x, y), (flip_xy(whole), 1 - x, 1 - y))
    full = jnp.zeros((ring, 2, 2) + block.shape, block.dtype)
    for part, at_x, at_y in parts:
        full = place(full, part[:, None, None], (0, at_x, at_y) + rest)
    return full, whole


def fence(*values):
    return lax.optimization_barrier(values)


def merge_columns(parts, core, groups):
    keep = lax.dynamic_index_in_dim(parts, core, 0, keepdims=False)
    send = lax.dynamic_index_in_dim(parts, 1 - core, 0, keepdims=False)
    count, cols = keep.shape
    other = flip(send.astype(BF), "c").astype(F32)
    grid = ordered(
        keep.reshape(count, groups, -1), other.reshape(count, groups, -1), core, 2
    )
    return grid.reshape(count, 2 * cols)


def mm(left, right):
    return jnp.dot(left, right, preferred_element_type=F32)


def mm_tn(left, right):
    return lax.dot_general(
        left, right, (((0,), (0,)), ((), ())), preferred_element_type=F32
    )


def mm_nt(left, right):
    return lax.dot_general(
        left, right, (((1,), (1,)), ((), ())), preferred_element_type=F32
    )


def norm_stats(values):
    mean = jnp.mean(values, axis=-1, keepdims=True)
    centred = values - mean
    variance = jnp.mean(centred * centred, axis=-1, keepdims=True)
    scale = lax.rsqrt(variance + EPS)
    return centred * scale, scale


def norm_back(grad, unit, scale, gain):
    inner = grad * gain
    mean_one = jnp.mean(inner, axis=-1, keepdims=True)
    mean_two = jnp.mean(inner * unit, axis=-1, keepdims=True)
    return scale * (inner - mean_one - unit * mean_two)


def dft_tables(length):
    part = 32
    blocks = length // part
    step = math.pi / (2.0 * length)
    times = lax.broadcasted_iota(jnp.int32, (blocks, length), 1)
    high = lax.broadcasted_iota(jnp.int32, (blocks, length), 0)
    low = lax.broadcasted_iota(jnp.int32, (part, length), 0)
    low_times = lax.broadcasted_iota(jnp.int32, (part, length), 1)
    high, low = lax.optimization_barrier((high, low))
    period = 4 * length
    angle_high = (2 * part * high * times % period).astype(F32) * step
    angle_low = ((2 * low + 1) * low_times % period).astype(F32) * step
    cos_high, sin_high = jnp.cos(angle_high)[:, None], jnp.sin(angle_high)[:, None]
    cos_low, sin_low = jnp.cos(angle_low)[None], jnp.sin(angle_low)[None]
    cos_all = (cos_high * cos_low - sin_high * sin_low).reshape(length, length)
    sin_all = (sin_high * cos_low + cos_high * sin_low).reshape(length, length)
    return cos_all.astype(BF), sin_all.astype(BF)


def kernel_body(part, coef_ref, rate_ref, out_ref, high_ref, low_ref):
    states = coef_ref.shape[0]
    length = out_ref.shape[0]
    blocks = length // part
    lanes = out_ref.shape[1]
    high_ids = lax.broadcasted_iota(jnp.int32, (blocks, lanes), 0).astype(F32) * (part / length)
    low_ids = lax.broadcasted_iota(jnp.int32, (part, lanes), 0).astype(F32) * (1.0 / length)

    def fill(state, carry):
        rate = rate_ref[pl.ds(state, 1), :]
        coef = coef_ref[pl.ds(state, 1), :] * (length ** (-0.5))
        high_ref[state] = coef * jnp.exp(-rate * high_ids)
        low_ref[state] = jnp.exp(-rate * low_ids)
        return carry

    lax.fori_loop(0, states, fill, 0)
    for start in range(0, blocks, 8):

        def add(state, sums):
            low = low_ref[state]
            return tuple(
                total + high_ref[state, pl.ds(start + index, 1), :] * low
                for index, total in enumerate(sums)
            )

        zero = jnp.zeros((part, lanes), F32)
        sums = lax.fori_loop(0, states, add, (zero,) * 8, unroll=4)
        for index, total in enumerate(sums):
            out_ref[pl.ds((start + index) * part, part), :] = total


def ssm_kernel(coef, rate, length):
    states, channels = coef.shape
    part = 32
    return pl.pallas_call(
        functools.partial(kernel_body, part),
        out_shape=jax.ShapeDtypeStruct((length, channels), F32),
        grid=(channels // 128,),
        in_specs=[pl.BlockSpec((states, 128), lambda i: (0, i))] * 2,
        out_specs=pl.BlockSpec((length, 128), lambda i: (0, i)),
        scratch_shapes=[
            pltpu.VMEM((states, length // part, 128), F32),
            pltpu.VMEM((states, part, 128), F32),
        ],
        cost_estimate=pl.CostEstimate(
            flops=2 * length * states * channels, bytes_accessed=2 * length * channels * 4, transcendentals=0
        ),
        name="ssm_kernel",
    )(coef, rate)


def ssm_kernel_grads(grad, coef, rate):
    length = grad.shape[1]
    times = lax.broadcasted_iota(jnp.int32, (1, 1, length), 2).astype(F32) * (1.0 / length)
    weighted = grad[:, None] * jnp.exp(-rate[:, :, None] * times)
    scale = length ** (-0.5)
    return jnp.sum(weighted, axis=2) * scale, -coef * jnp.sum(weighted * times, axis=2) * scale


def body(
    ring,
    tokens,
    lengths,
    cotangent,
    norm1_gain,
    norm1_bias,
    w_query,
    w_key,
    w_value,
    shift_taps,
    ssm_coef,
    ssm_rate,
    skip_gain,
    w_out,
    norm2_gain,
    norm2_bias,
    w_up,
    up_bias,
    w_down,
    down_bias,
):
    core = lax.axis_index("c")
    groups = 2 * ring
    _, block_len, width = tokens.shape
    length = 2 * block_len
    rows = w_query.shape[0]
    up_rows = up_bias.shape[0]
    hidden = w_up.shape[1]
    states = ssm_coef.shape[1]
    tap_count = shift_taps.shape[1]
    channels = width // 2

    def columns(weight, which):
        grid = weight.reshape(rows, groups, 2, -1)
        return jnp.where(which == 0, grid[:, :, 0], grid[:, :, 1]).reshape(rows, -1)

    matrices = (w_query, w_key, w_value, w_up)
    keep = jnp.concatenate([columns(w, core) for w in matrices], axis=1)
    send = jnp.concatenate([columns(w, 1 - core) for w in matrices], axis=1)
    packed = ordered(keep, flip(send, "c"), core, 0)
    up_parts = packed[:, :, 3 * channels :]
    up_own = lax.all_gather(up_parts, MISC, axis=0, tiled=False)
    out_halves = w_out.reshape(rows, 2, channels).transpose(1, 0, 2)
    first_pack = jnp.concatenate([packed[:, :, : 3 * channels], out_halves], axis=2)

    vectors = jnp.stack([norm1_gain, norm1_bias, norm2_gain, norm2_bias, down_bias])
    misc = jnp.concatenate(
        [
            ssm_coef.reshape(-1),
            ssm_rate.reshape(-1),
            shift_taps.reshape(-1),
            skip_gain,
            up_bias,
            vectors.reshape(-1),
        ]
    )
    misc_pad = -misc.shape[0] % 1024
    misc = jnp.pad(misc, (0, misc_pad)).reshape(-1, 128)
    misc, first_pack = fence(misc, first_pack)
    misc_all, misc_ring = gather_small(misc, ring)
    misc_all = misc_all.reshape(groups * 2, -1)
    cuts = []
    offset = 0
    for size in (rows * states, rows * states, rows * tap_count, rows, up_rows, 5 * rows):
        cuts.append(misc_all[:, offset : offset + size].astype(F32))
        offset += size
    coef = cuts[0].reshape(channels, states).T
    rate = cuts[1].reshape(channels, states).T
    taps = cuts[2].reshape(channels, tap_count).T
    skip = cuts[3].reshape(1, channels)
    up_bias_own = cuts[4].reshape(1, hidden // 2)
    vec_own = cuts[5].astype(BF).reshape(groups, 2, 5, rows)
    vec_all = ordered(vec_own, flip(vec_own, "c"), core, 1)
    vec_all = vec_all.transpose(3, 0, 1, 2, 4).reshape(5, 1, width).astype(F32)
    gain_one, bias_one, gain_two, bias_two, down_bias_all = [vec_all[i] for i in range(5)]

    first_pack, misc_ring = fence(first_pack, misc_ring)
    first_ring = gather_ring(first_pack, ring)
    own_tokens, misc_all = fence(tokens[0], misc_all)
    token_half = swap_cy(own_tokens)
    token_all = ordered(token_half, flip(token_half, "c"), core, 0).reshape(length, width)
    kernel = ssm_kernel(coef, rate, length)
    first_ring, kernel, token_all = fence(first_ring, kernel, token_all)
    start_one, pair_up, start_two, finish = gather_near(first_ring)
    moved = start_one()
    down_pack, first_ring = fence(w_down[None], first_ring)
    down_ring = gather_ring(down_pack, ring)
    cos_t, sin_t = dft_tables(length)
    pair = pair_up(moved)
    pair, cos_t, sin_t = fence(pair, cos_t, sin_t)
    moved = start_two(pair)
    inputs = token_all.astype(F32)
    unit_one, _ = norm_stats(inputs)
    first_rows = (unit_one * gain_one + bias_one).astype(BF)
    first_rows, down_ring, moved = fence(first_rows, down_ring, moved)
    weights = place_near(finish(pair, moved))
    w_qkv = weights[..., : 3 * channels].reshape(width, 3 * channels)
    out_own = weights[..., 3 * channels :].transpose(0, 1, 3, 4, 2, 5).reshape(channels, width)
    start_one, pair_up, start_two, finish = gather_near(down_ring)
    down_moved = start_one()

    start = lax.axis_index("y") * block_len
    valid = start + lax.broadcasted_iota(jnp.int32, (block_len, 1), 0) < lengths[0]
    masked = jnp.where(valid, cotangent[0], jnp.zeros((), BF))
    masked, w_qkv = fence(masked, w_qkv)
    grad_half = swap_cy(masked)
    grad_all = ordered(grad_half, flip(grad_half, "c"), core, 0).reshape(length, width)

    heads = mm(first_rows, w_qkv).astype(BF)
    query, key, value = [heads[:, i * channels : (i + 1) * channels] for i in range(3)]
    query_f, key_f, value_f = query.astype(F32), key.astype(F32), value.astype(F32)
    padded = jnp.pad(key_f, ((tap_count - 1, 0), (0, 0)))
    shifted = jnp.zeros_like(key_f)
    for tap in range(tap_count):
        at = tap_count - 1 - tap
        shifted = shifted + padded[at : at + length] * taps[tap : tap + 1]
    products = shifted * value_f
    both = jnp.concatenate([products.astype(BF), kernel.astype(BF)], axis=1)
    both_re = mm(cos_t, both)
    both_im = mm(sin_t, both)
    pair = pair_up(down_moved)
    pair, both_re, both_im = fence(pair, both_re, both_im)
    down_moved = start_two(pair)
    prod_re, kern_re = both_re[:, :channels], both_re[:, channels:]
    prod_im, kern_im = both_im[:, :channels], both_im[:, channels:]
    spec_re = (prod_re * kern_re - prod_im * kern_im).astype(BF)
    spec_im = (prod_re * kern_im + prod_im * kern_re).astype(BF)
    convolved = (mm_tn(cos_t, spec_re) + mm_tn(sin_t, spec_im)) * (1.0 / length)
    convolved = convolved + skip * products
    mixed_heads = (query_f * convolved).astype(BF)
    mixed_other = flip(mixed_heads, "c")
    out_other = flip(out_own, "c")
    residual = inputs + mm(mixed_heads, out_own) + mm(mixed_other, out_other)
    residual, down_moved = fence(residual, down_moved)
    down_own = place_near(finish(pair, down_moved)).reshape(hidden // 2, width)
    up_own = up_own.reshape(groups, 2, 2, rows, hidden // 2).transpose(0, 2, 1, 3, 4)
    up_own = up_own.reshape(width, hidden // 2)
    unit_two, scale_two = norm_stats(residual)
    second_rows = (unit_two * gain_two + bias_two).astype(BF)
    preact = mm(second_rows, up_own) + up_bias_own
    bend = jnp.tanh(SQRT_2_PI * (preact + 0.044715 * preact * preact * preact))
    activated = (0.5 * preact * (1.0 + bend)).astype(BF)
    slope = 0.5 * (1.0 + bend) + 0.5 * preact * (1.0 - bend * bend) * SQRT_2_PI * (
        1.0 + 3.0 * 0.044715 * preact * preact
    )
    slope = slope.astype(BF)

    def mine(array):
        return lax.dynamic_slice_in_dim(array, core * block_len, block_len, 0)

    def theirs(array):
        return lax.dynamic_slice_in_dim(array, (1 - core) * block_len, block_len, 0)

    down_part = mm(activated, down_own)
    down_other = flip(theirs(down_part).astype(BF), "c").astype(F32)
    mixed = mine(residual) + mine(down_part) + down_other + down_bias_all
    mixed = mixed.astype(BF)

    down_sum = mm_tn(activated, grad_all).astype(BF).reshape(ring, 2, 1, 2, up_rows, width)
    grad_in, down_sum = fence(grad_all, down_sum)
    down_one = scatter_one(down_sum)
    act_grad = mm_nt(grad_in, down_own)
    pre_grad = (act_grad * slope.astype(F32)).astype(BF)
    second_part = mm_nt(pre_grad, up_own)
    second_other = flip(theirs(second_part).astype(BF), "c").astype(F32)
    up_sum = mm_tn(second_rows, pre_grad).astype(BF).reshape(ring, 2, 2, 2, rows, hidden // 2)
    up_bias_grad = jnp.sum(pre_grad.astype(F32), axis=0)
    second_grad = mine(second_part) + second_other
    down_one, up_sum, second_grad = fence(down_one, up_sum, second_grad)

    down_two = scatter_two(down_sum, down_one)
    up_one = scatter_one(up_sum)
    unit_two_h, scale_two_h = mine(unit_two), mine(scale_two)
    grad_half_f = grad_half.astype(F32)
    gain_two_grad = jnp.sum(second_grad * unit_two_h, axis=0)
    bias_two_grad = jnp.sum(second_grad, axis=0)
    down_bias_grad = jnp.sum(grad_half_f, axis=0)
    resid_grad = grad_half_f + norm_back(second_grad, unit_two_h, scale_two_h, gain_two)
    mix_half = resid_grad.astype(BF)
    mix_grad = ordered(mix_half, flip(mix_half, "c"), core, 0).reshape(length, width)

    head_grad = mm_nt(mix_grad, out_own).astype(BF).astype(F32)
    query_grad = (head_grad * convolved).astype(BF)
    conv_grad = head_grad * query_f
    conv_low = conv_grad.astype(BF)
    skip_grad = jnp.sum(conv_grad * products, axis=0)
    grad_re = mm(cos_t, conv_low)
    grad_im = mm(sin_t, conv_low)
    grad_re, grad_im, down_two, up_one, mixed = fence(grad_re, grad_im, down_two, up_one, mixed)

    down_held, down_three = scatter_three(down_sum, down_one, down_two, ring)
    up_two = scatter_two(up_sum, up_one)
    back_re = (grad_re * kern_re + grad_im * kern_im).astype(BF)
    back_im = (grad_im * kern_re - grad_re * kern_im).astype(BF)
    lag_re = (grad_re * prod_re + grad_im * prod_im).astype(BF)
    lag_im = (grad_im * prod_re - grad_re * prod_im).astype(BF)
    back = (mm_tn(cos_t, back_re) + mm_tn(sin_t, back_im)) * (1.0 / length)
    product_grad = back + skip * conv_grad
    out_grad = mm_tn(mixed_heads, mix_grad).astype(BF)
    out_grad = out_grad.reshape(ring, 2, 2, rows, 2, channels).transpose(0, 1, 4, 2, 3, 5)
    q_grad = mm_tn(first_rows, query_grad).astype(BF).reshape(ring, 2, 2, 2, rows, channels)
    outq_sum = jnp.concatenate([q_grad, out_grad], axis=5)
    product_grad, up_two, outq_sum = fence(product_grad, up_two, outq_sum)

    up_held, up_three = scatter_three(up_sum, up_one, up_two, ring)
    outq_one = scatter_one(outq_sum)
    shifted_grad = product_grad * value_f
    value_grad = (product_grad * shifted).astype(BF)
    padded_grad = jnp.pad(shifted_grad, ((0, tap_count - 1), (0, 0)))
    key_grad = jnp.zeros_like(key_f)
    tap_rows = []
    for tap in range(tap_count):
        at = tap_count - 1 - tap
        key_grad = key_grad + padded_grad[tap : tap + length] * taps[tap : tap + 1]
        tap_rows.append(jnp.sum(shifted_grad * padded[at : at + length], axis=0))
    key_grad = key_grad.astype(BF)
    kv_grad = jnp.concatenate([key_grad, value_grad], axis=1)
    kv_sum = mm_tn(first_rows, kv_grad).astype(BF).reshape(ring, 2, 2, 2, rows, 2 * channels)
    lag_grad = (mm_tn(lag_re, cos_t) + mm_tn(lag_im, sin_t)) * (1.0 / length)
    lag_sum = lag_grad.astype(BF).reshape(ring, 2, 2, rows, 2, block_len).transpose(0, 1, 4, 2, 3, 5)
    kv_sum = jnp.concatenate([kv_sum, lag_sum], axis=5)
    kv_sum, kv_grad, outq_one, up_three, down_three = fence(kv_sum, kv_grad, outq_one, up_three, down_three)

    outq_two = scatter_two(outq_sum, outq_one)
    kv_one = scatter_one(kv_sum)
    first_part = mm_nt(jnp.concatenate([query_grad, kv_grad], axis=1), w_qkv)
    first_other = flip(theirs(first_part).astype(BF), "c").astype(F32)
    first_grad = mine(first_part) + first_other
    unit_one_h, scale_one_h = norm_stats(token_half.astype(F32))
    gain_one_grad = jnp.sum(first_grad * unit_one_h, axis=0)
    bias_one_grad = jnp.sum(first_grad, axis=0)
    token_grad = resid_grad + norm_back(first_grad, unit_one_h, scale_one_h, gain_one)
    outq_two, kv_one, token_grad = fence(outq_two, kv_one, token_grad)

    outq_held, outq_three = scatter_three(outq_sum, outq_one, outq_two, ring)
    kv_two = scatter_two(kv_sum, kv_one)
    token_grad = swap_cy(token_grad.astype(BF)).astype(F32)[None]
    mixed = swap_cy(mixed)[None]
    down_s = scatter_sum(down_held, down_three)[0]
    up_s = merge_columns(scatter_sum(up_held, up_three), core, groups)
    up_s, down_s, kv_two = fence(up_s, down_s, kv_two)
    kv_held, kv_three = scatter_three(kv_sum, kv_one, kv_two, ring)
    outq_s = scatter_sum(outq_held, outq_three)
    out_s = outq_s[..., channels:].transpose(1, 0, 2).reshape(rows, width)
    query_s = merge_columns(outq_s[..., :channels], core, groups)
    query_s, out_s, kv_three = fence(query_s, out_s, kv_three)
    kv_s = scatter_sum(kv_held, kv_three)
    key_s = merge_columns(kv_s[..., :channels], core, groups)
    value_s = merge_columns(kv_s[..., channels : 2 * channels], core, groups)
    lag_s = kv_s[..., 2 * channels :].transpose(1, 0, 2).reshape(rows, length)
    coef_s, rate_s = ssm_kernel_grads(lag_s, ssm_coef.astype(F32), ssm_rate.astype(F32))

    vec_grads = jnp.stack(
        [gain_one_grad, bias_one_grad, gain_two_grad, bias_two_grad, down_bias_grad]
    )
    vec_grads = vec_grads.reshape(5, ring, 2, 2, 2, rows)
    vec_keep = lax.dynamic_index_in_dim(vec_grads, core, 3, keepdims=False)
    vec_send = lax.dynamic_index_in_dim(vec_grads, 1 - core, 3, keepdims=False)
    vec_sum = (vec_keep + flip(vec_send, "c")).transpose(1, 2, 3, 0, 4)

    def flat(array):
        return array.reshape(ring, 2, 2, -1)

    small = jnp.concatenate(
        [
            flat(jnp.stack(tap_rows, axis=1)),
            flat(skip_grad),
            flat(up_bias_grad),
            flat(vec_sum),
        ],
        axis=3,
    )
    small_pad = -small.shape[3] % 1024
    small = jnp.pad(small, ((0, 0), (0, 0), (0, 0), (0, small_pad)))
    small = small.reshape(ring, 2, 2, -1, 128)

    def pick_small(x, y):
        return lax.dynamic_slice(
            small, (0, x, y, 0, 0), (ring, 1, 1) + small.shape[3:]
        ).reshape((ring,) + small.shape[3:])

    near_small = scatter_near(pick_small)
    here = lax.axis_index("r")
    small = take(near_small, 0, here)
    for distance in range(1, ring):
        small = small + shift_ring(
            take(near_small, 0, lax.rem(here + distance, ring)), distance, ring
        )
    small = small.reshape(-1)
    pieces = []
    offset = 0
    for size in (rows * tap_count, rows, up_rows, 5 * rows):
        pieces.append(small[offset : offset + size])
        offset += size
    vec_s = pieces[3].reshape(5, rows)
    return (
        mixed,
        token_grad,
        vec_s[0],
        vec_s[1],
        query_s,
        key_s,
        value_s,
        pieces[0].reshape(rows, tap_count),
        coef_s,
        rate_s,
        pieces[1],
        out_s,
        vec_s[2],
        vec_s[3],
        up_s,
        pieces[2],
        down_s,
        vec_s[4],
    )


def solution(mesh):
    dp_size, seq_size = mesh.devices.shape
    ring = dp_size // 4
    grid = Mesh(mesh.devices.reshape(ring, 2, 2, seq_size), ("r", "x", "c", "y"))
    dp = ("r", "x", "c")
    act = P(dp, "y", None)
    vec = P(dp + ("y",))
    mat = P(dp + ("y",), None)
    return jax.shard_map(
        functools.partial(body, ring),
        mesh=grid,
        in_specs=(
            act, P(dp), act, vec, vec, mat, mat, mat, mat, mat, mat, vec, mat, vec, vec, mat, vec, mat, vec,
        ),
        out_specs=(
            act, act, vec, vec, mat, mat, mat, mat, mat, mat, vec, mat, vec, vec, mat, vec, mat, vec,
        ),
        check_vma=False,
    )
```

```python
import functools
import math

import jax
import jax.numpy as jnp
from jax import lax
from jax.experimental import pallas as pl
from jax.experimental.pallas import tpu as pltpu
from jax.sharding import Mesh, PartitionSpec as P

EPS = 1e-05
BF = jnp.bfloat16
F32 = jnp.float32
SQRT_2_PI = math.sqrt(2.0 / math.pi)
MISC = ("r", "x", "y")


def flip(value, axis):
    return lax.ppermute(value, axis, [(0, 1), (1, 0)])


def ordered(mine, other, place, axis):
    first = jnp.where(place == 0, mine, other)
    second = jnp.where(place == 0, other, mine)
    return jnp.stack([first, second], axis=axis)


def swap_cy(value):
    moved = lax.ppermute(value, ("c", "y"), [(1, 2), (2, 1)])
    return jnp.where(lax.axis_index("c") == lax.axis_index("y"), value, moved)


def shift_ring(value, distance, ring):
    return lax.ppermute(value, "r", [(i, (i + distance) % ring) for i in range(ring)])


def flip_xy(value):
    return lax.ppermute(value, ("x", "y"), [(i, 3 - i) for i in range(4)])


def place(whole, part, starts):
    return lax.dynamic_update_slice(whole, part, starts)


def gather_ring(block, ring):
    here = lax.axis_index("r")
    rest = (0,) * block.ndim
    whole = jnp.zeros((ring,) + block.shape, block.dtype)
    whole = place(whole, block[None], (here,) + rest)
    for distance in range(1, ring):
        moved = shift_ring(block, distance, ring)
        whole = place(whole, moved[None], (lax.rem(here - distance + ring, ring),) + rest)
    return whole


def ring_pieces(block, ring):
    blocks = [block] + [shift_ring(block, d, ring) for d in range(1, ring)]
    return tuple(jnp.stack([part[half] for part in blocks]) for half in range(2))


def near_one(halves):
    return flip(halves[0], "y"), flip(halves[1], "x")


def near_two(halves, moved):
    first = flip(jnp.concatenate([halves[0], moved[0]]), "x")
    second = flip(jnp.concatenate([halves[1], moved[1]]), "y")
    return first, second


def chip_ids():
    return jnp.stack([lax.axis_index("r"), lax.axis_index("x"), lax.axis_index("y")]).astype(jnp.int32)


def grant(*blocks):
    total = 0
    for shape, kind in blocks:
        rows = -(-shape[-2] // 16) * 16
        total += math.prod(shape[:-2]) * rows * shape[-1] * jnp.dtype(kind).itemsize
    return pltpu.CompilerParams(vmem_limit_bytes=2 * total + (2 << 20))


def assemble_body(write, ids, *refs):
    ins, outs = refs[:8], refs[8:]
    for half in range(2):
        for index in range(4):
            x = lax.rem(ids[1] + index // 2, 2)
            y = lax.rem(ids[2] + index % 2, 2)
            write(outs, ins[4 * half + index], half, x, y)


def assemble(halves, one, two, ring, shapes, write, name):
    sources = (
        (halves[0], 0), (one[0], 0), (two[0], 0), (two[0], ring),
        (halves[1], 0), (two[1], 0), (one[1], 0), (two[1], ring),
    )
    tail = halves[0].shape[1:]
    zeros = (0,) * len(tail)
    specs = [
        pl.BlockSpec((None,) + tail, lambda i, ids, base=base: (i + base,) + zeros) for _, base in sources
    ]
    moved = 32 * math.prod(tail) * ring
    return pl.pallas_call(
        functools.partial(assemble_body, write),
        out_shape=tuple(jax.ShapeDtypeStruct(shape, halves[0].dtype) for shape in shapes),
        grid_spec=pltpu.PrefetchScalarGridSpec(
            num_scalar_prefetch=1,
            grid=(ring,),
            in_specs=specs,
            out_specs=tuple(
                pl.BlockSpec(
                    (None,) + shape[1:],
                    lambda i, ids, rank=len(shape): (lax.rem(ids[0] + ring - i, ring),) + (0,) * (rank - 1),
                )
                for shape in shapes
            ),
        ),
        compiler_params=grant(*[(tail, BF)] * 8, *[(shape[1:], BF) for shape in shapes]),
        cost_estimate=pl.CostEstimate(flops=0, bytes_accessed=moved, transcendentals=0),
        name=name,
    )(chip_ids(), *[array for array, _ in sources])


def write_heads(outs, part, half, x, y):
    outs[0][x, half, y] = part[0]


def write_up(outs, part, half, x, y):
    lanes = part.shape[-1]
    count = part.shape[0] - 1
    for index in range(count):
        outs[0][x, half, y, :, index * lanes : (index + 1) * lanes] = part[index]
    outs[1][x, y, :, half * lanes : (half + 1) * lanes] = part[count]


def here_x(i, ids):
    return ids[1]


def other_x(i, ids):
    return 1 - ids[1]


def here_y(i, ids):
    return ids[2]


def other_y(i, ids):
    return 1 - ids[2]


def step_r(i, ids):
    return i


def turn_r(ring):
    return lambda i, ids: lax.rem(ids[0] + i, ring)


def sums_body(plan, ids, *refs):
    ins, outs = refs[: len(refs) - len(plan)], refs[len(refs) - len(plan) :]
    for out, columns in zip(outs, plan):
        width = out.shape[2]
        at = 0
        for terms in columns:
            first = ins[terms[0]]
            cores, extra, _, lanes = first.shape
            index = 0
            for core in range(cores):
                for more in range(extra):
                    for low in range(0, lanes, width):
                        total = None
                        for term in terms:
                            ref = ins[term]
                            if len(ref.shape) == 4:
                                value = ref[core, more, :, low : low + width]
                            else:
                                value = ref[at + index]
                            value = value.astype(F32)
                            total = value if total is None else total + value
                        out[at + index] = total.astype(out.dtype)
                        index += 1
            at += index


def sums(ring, jobs):
    arrays, specs, plan, shapes = [], [], [], []
    for width, columns in jobs:
        pieces = 0
        numbers = []
        for terms in columns:
            mine = []
            for count, (array, picks) in enumerate(terms):
                tail = array.shape[len(picks) :]
                block = tuple(
                    size if pick is None else None for size, pick in zip(array.shape, picks)
                ) + tail

                def index_map(i, ids, picks=picks, tail=tail):
                    return tuple(0 if pick is None else pick(i, ids) for pick in picks) + (0,) * len(tail)

                if count == 0:
                    held = [size for size in block if size is not None]
                    pieces += held[0] * held[1] * (held[3] // width)
                mine.append(len(arrays))
                arrays.append(array)
                specs.append(pl.BlockSpec(block, index_map))
            numbers.append(mine)
        plan.append(numbers)
        rows = columns[0][0][0].shape[-2]
        shapes.append(jax.ShapeDtypeStruct((ring, pieces, rows, width), BF))
    moved = sum(2 * math.prod(shape.shape) * 2 for shape in shapes)
    return pl.pallas_call(
        functools.partial(sums_body, plan),
        out_shape=tuple(shapes),
        grid_spec=pltpu.PrefetchScalarGridSpec(
            num_scalar_prefetch=1,
            grid=(ring,),
            in_specs=specs,
            out_specs=tuple(
                pl.BlockSpec((None,) + shape.shape[1:], lambda i, ids: (i, 0, 0, 0)) for shape in shapes
            ),
        ),
        compiler_params=grant(
            *[
                (tuple(size for size in spec.block_shape if size is not None), BF)
                for spec in specs
            ],
            *[(shape.shape[1:], BF) for shape in shapes],
        ),
        cost_estimate=pl.CostEstimate(flops=0, bytes_accessed=2 * moved, transcendentals=0),
        name="sums",
    )(chip_ids(), *arrays)


def take(parts, axis, index):
    return lax.dynamic_index_in_dim(parts, index, axis, keepdims=False)


def pair_one(y_first, x_first):
    x, y = lax.axis_index("x"), lax.axis_index("y")
    return flip(take(y_first, 3, 1 - y), "y"), flip(take(x_first, 1, 1 - x), "x")


def pair_two(y_first, x_first, moved, ring):
    one = [
        (y_first, (step_r, other_x, None, here_y)),
        (moved[0], (step_r, other_x, None)),
    ]
    two = [
        (x_first, (step_r, here_x, None, other_y)),
        (moved[1], (step_r, None, other_y)),
    ]
    send_one, send_two = sums(ring, [(y_first.shape[-1], [one]), (x_first.shape[-1], [two])])
    shape_one = (ring, y_first.shape[2]) + y_first.shape[4:]
    shape_two = (ring, x_first.shape[2]) + x_first.shape[4:]
    return flip(send_one, "x").reshape(shape_one), flip(send_two, "y").reshape(shape_two)


def pair_three(y_first, x_first, moved_one, moved_two, ring, width):
    turn = turn_r(ring)
    one = [
        (y_first, (turn, here_x, None, here_y)),
        (moved_one[0], (turn, here_x, None)),
        (moved_two[0], (turn, None)),
    ]
    two = [
        (x_first, (turn, here_x, None, here_y)),
        (moved_one[1], (turn, None, here_y)),
        (moved_two[1], (turn, None)),
    ]
    return sums(ring, [(width, [one, two])])[0]


def direct_one(arrays, ring, width):
    spots = ((here_x, other_y), (other_x, here_y), (other_x, other_y))
    along_y, along_x, across = sums(
        ring, [(width, [[(array, (step_r, x, None, y))] for array in arrays]) for x, y in spots]
    )
    return flip(along_y, "y"), flip(along_x, "x"), flip_xy(across)


def direct_two(arrays, moved, ring, width):
    turn = turn_r(ring)
    columns = [
        [(array, (turn, here_x, None, here_y))] + [(part, (turn,)) for part in moved] for array in arrays
    ]
    return sums(ring, [(width, columns)])[0]


def ring_send(held, ring):
    return tuple(shift_ring(held[distance], distance, ring) for distance in range(1, ring))


def ring_sum(held, moved):
    total = held[0].astype(F32)
    for part in moved:
        total = total + part.astype(F32)
    return total


def join(pieces):
    return jnp.concatenate([pieces[i] for i in range(pieces.shape[0])], axis=1)


def scatter_near(pick):
    x, y = lax.axis_index("x"), lax.axis_index("y")
    total = pick(x, y).astype(F32)
    total = total + flip(pick(x, 1 - y), "y").astype(F32)
    total = total + flip(pick(1 - x, y), "x").astype(F32)
    return total + flip_xy(pick(1 - x, 1 - y)).astype(F32)


def gather_quad(block):
    x, y = lax.axis_index("x"), lax.axis_index("y")
    parts = ((block, x, y), (flip(block, "y"), x, 1 - y), (flip(block, "x"), 1 - x, y), (flip_xy(block), 1 - x, 1 - y))
    full = jnp.zeros((2, 2) + block.shape, block.dtype)
    for part, at_x, at_y in parts:
        full = place(full, part[None, None], (at_x, at_y) + (0,) * block.ndim)
    return full


def fence(*values):
    return lax.optimization_barrier(values)


def merge_columns(parts, core, groups):
    keep = lax.dynamic_index_in_dim(parts, core, 0, keepdims=False)
    send = lax.dynamic_index_in_dim(parts, 1 - core, 0, keepdims=False)
    count, cols = keep.shape
    other = flip(send.astype(BF), "c").astype(F32)
    grid = ordered(
        keep.reshape(count, groups, -1), other.reshape(count, groups, -1), core, 2
    )
    return grid.reshape(count, 2 * cols)


def mm(left, right):
    return jnp.dot(left, right, preferred_element_type=F32)


def mm_tn(left, right):
    return lax.dot_general(
        left, right, (((0,), (0,)), ((), ())), preferred_element_type=F32
    )


def mm_nt(left, right):
    return lax.dot_general(
        left, right, (((1,), (1,)), ((), ())), preferred_element_type=F32
    )


def norm_stats(values):
    mean = jnp.mean(values, axis=-1, keepdims=True)
    centred = values - mean
    variance = jnp.mean(centred * centred, axis=-1, keepdims=True)
    scale = lax.rsqrt(variance + EPS)
    return centred * scale, scale


def norm_back(grad, unit, scale, gain):
    inner = grad * gain
    mean_one = jnp.mean(inner, axis=-1, keepdims=True)
    mean_two = jnp.mean(inner * unit, axis=-1, keepdims=True)
    return scale * (inner - mean_one - unit * mean_two)


def dft_tables(length, token):
    part = 32
    blocks = length // part
    step = math.pi / (2.0 * length)
    times = lax.broadcasted_iota(jnp.int32, (blocks, length), 1)
    high = lax.broadcasted_iota(jnp.int32, (blocks, length), 0)
    low = lax.broadcasted_iota(jnp.int32, (part, length), 0)
    low_times = lax.broadcasted_iota(jnp.int32, (part, length), 1)
    high, low, token = lax.optimization_barrier((high, low, token))
    period = 4 * length
    angle_high = (2 * part * high * times % period).astype(F32) * step
    angle_low = ((2 * low + 1) * low_times % period).astype(F32) * step
    cos_high, sin_high = jnp.cos(angle_high)[:, None], jnp.sin(angle_high)[:, None]
    cos_low, sin_low = jnp.cos(angle_low)[None], jnp.sin(angle_low)[None]
    cos_all = (cos_high * cos_low - sin_high * sin_low).reshape(length, length)
    sin_all = (sin_high * cos_low + cos_high * sin_low).reshape(length, length)
    return cos_all.astype(BF), sin_all.astype(BF)


def kernel_body(part, coef_ref, rate_ref, out_ref, high_ref, low_ref):
    states = coef_ref.shape[0]
    length = out_ref.shape[0]
    blocks = length // part
    lanes = out_ref.shape[1]
    high_ids = lax.broadcasted_iota(jnp.int32, (blocks, lanes), 0).astype(F32) * (part / length)
    low_ids = lax.broadcasted_iota(jnp.int32, (part, lanes), 0).astype(F32) * (1.0 / length)

    def fill(state, carry):
        rate = rate_ref[pl.ds(state, 1), :]
        coef = coef_ref[pl.ds(state, 1), :] * (length ** (-0.5))
        high_ref[state] = coef * jnp.exp(-rate * high_ids)
        low_ref[state] = jnp.exp(-rate * low_ids)
        return carry

    lax.fori_loop(0, states, fill, 0)
    for start in range(0, blocks, 8):

        def add(state, sums):
            low = low_ref[state]
            return tuple(
                total + high_ref[state, pl.ds(start + index, 1), :] * low
                for index, total in enumerate(sums)
            )

        zero = jnp.zeros((part, lanes), F32)
        sums = lax.fori_loop(0, states, add, (zero,) * 8, unroll=4)
        for index, total in enumerate(sums):
            out_ref[pl.ds((start + index) * part, part), :] = total


def ssm_kernel(coef, rate, length):
    states, channels = coef.shape
    part = 32
    return pl.pallas_call(
        functools.partial(kernel_body, part),
        out_shape=jax.ShapeDtypeStruct((length, channels), F32),
        grid=(channels // 128,),
        in_specs=[pl.BlockSpec((states, 128), lambda i: (0, i))] * 2,
        out_specs=pl.BlockSpec((length, 128), lambda i: (0, i)),
        scratch_shapes=[
            pltpu.VMEM((states, length // part, 128), F32),
            pltpu.VMEM((states, part, 128), F32),
        ],
        cost_estimate=pl.CostEstimate(
            flops=600 * length * states * channels, bytes_accessed=2 * length * channels * 4, transcendentals=0
        ),
        compiler_params=pltpu.CompilerParams(vmem_limit_bytes=6 << 20),
        name="ssm_kernel",
    )(coef, rate)


def ssm_kernel_grads(grad, coef, rate):
    length = grad.shape[1]
    times = lax.broadcasted_iota(jnp.int32, (1, 1, length), 2).astype(F32) * (1.0 / length)
    weighted = grad[:, None] * jnp.exp(-rate[:, :, None] * times)
    scale = length ** (-0.5)
    return jnp.sum(weighted, axis=2) * scale, -coef * jnp.sum(weighted * times, axis=2) * scale


def body(
    ring,
    tokens,
    lengths,
    cotangent,
    norm1_gain,
    norm1_bias,
    w_query,
    w_key,
    w_value,
    shift_taps,
    ssm_coef,
    ssm_rate,
    skip_gain,
    w_out,
    norm2_gain,
    norm2_bias,
    w_up,
    up_bias,
    w_down,
    down_bias,
):
    core = lax.axis_index("c")
    groups = 2 * ring
    _, block_len, width = tokens.shape
    length = 2 * block_len
    rows = w_query.shape[0]
    up_rows = up_bias.shape[0]
    hidden = w_up.shape[1]
    states = ssm_coef.shape[1]
    tap_count = shift_taps.shape[1]
    channels = width // 2

    def columns(weight, which):
        grid = weight.reshape(rows, groups, 2, -1)
        return jnp.where(which == 0, grid[:, :, 0], grid[:, :, 1]).reshape(rows, -1)

    down_own = lax.all_gather(w_down, MISC, axis=0, tiled=True)
    matrices = (w_query, w_key, w_value, w_up)
    keep = jnp.concatenate([columns(w, core) for w in matrices], axis=1)
    send = jnp.concatenate([columns(w, 1 - core) for w in matrices], axis=1)
    norm1_gain, ssm_coef, ssm_rate, send = fence(norm1_gain, ssm_coef, ssm_rate, send)
    packed = ordered(keep, flip(send, "c"), core, 0)
    first_pack = packed[:, None, :, : 3 * channels]
    first_ring = ring_pieces(first_pack, ring)
    up_lanes = packed[:, :, 3 * channels :]
    up_pack = jnp.stack(
        [up_lanes[:, :, i * channels : (i + 1) * channels] for i in range(hidden // width)]
        + [jnp.stack([w_out[:, :channels], w_out[:, channels:]])],
        axis=1,
    )

    vectors = jnp.stack([norm1_gain, norm1_bias, norm2_gain, norm2_bias, down_bias])
    misc = jnp.concatenate(
        [
            ssm_coef.reshape(-1),
            ssm_rate.reshape(-1),
            shift_taps.reshape(-1),
            skip_gain,
            up_bias,
            vectors.reshape(-1),
        ]
    )
    misc_pad = -misc.shape[0] % 1024
    misc = jnp.pad(misc, (0, misc_pad)).reshape(-1, 128)
    misc_near = gather_quad(misc)
    misc_near, *first_ring = fence(misc_near, *first_ring)
    misc_all = gather_ring(misc_near, ring)
    misc_all = misc_all.reshape(groups * 2, -1)
    cuts = []
    offset = 0
    for size in (rows * states, rows * states, rows * tap_count, rows, up_rows, 5 * rows):
        cuts.append(misc_all[:, offset : offset + size].astype(F32))
        offset += size
    coef = cuts[0].reshape(channels, states).T
    rate = cuts[1].reshape(channels, states).T
    taps = cuts[2].reshape(channels, tap_count).T
    skip = cuts[3].reshape(1, channels)
    up_bias_own = cuts[4].reshape(1, hidden // 2)
    vec_own = cuts[5].astype(BF).reshape(groups, 2, 5, rows)
    vec_all = ordered(vec_own, flip(vec_own, "c"), core, 1)
    vec_all = vec_all.transpose(3, 0, 1, 2, 4).reshape(5, 1, width).astype(F32)
    gain_one, bias_one, gain_two, bias_two, down_bias_all = [vec_all[i] for i in range(5)]

    token_half = swap_cy(tokens[0])
    token_all = ordered(token_half, flip(token_half, "c"), core, 0).reshape(length, width)
    first_one = near_one(first_ring)
    cos_t, sin_t = dft_tables(length, first_ring[0])
    inputs = token_all.astype(F32)
    unit_one, _ = norm_stats(inputs)
    first_rows = (unit_one * gain_one + bias_one).astype(BF)
    first_rows, cos_t, sin_t, coef, up_pack, *first_one = fence(
        first_rows, cos_t, sin_t, coef, up_pack, *first_one
    )
    first_two = near_two(first_ring, first_one)
    up_ring = ring_pieces(up_pack, ring)
    kernel = ssm_kernel(coef, rate, length)
    kernel, *first_two = fence(kernel, *first_two)
    w_qkv = assemble(
        first_ring, first_one, first_two, ring, ((ring, 2, 2, 2, rows, 3 * channels),), write_heads, "place_heads"
    )[0].reshape(width, 3 * channels)
    w_qkv, *up_ring = fence(w_qkv, *up_ring)
    up_one = near_one(up_ring)

    start = lax.axis_index("y") * block_len
    valid = start + lax.broadcasted_iota(jnp.int32, (block_len, 1), 0) < lengths[0]
    masked = jnp.where(valid, cotangent[0], jnp.zeros((), BF))
    masked, w_qkv = fence(masked, w_qkv)
    grad_half = swap_cy(masked)
    grad_all = ordered(grad_half, flip(grad_half, "c"), core, 0).reshape(length, width)

    heads = mm(first_rows, w_qkv).astype(BF)
    query, key, value = [heads[:, i * channels : (i + 1) * channels] for i in range(3)]
    query_f, key_f, value_f = query.astype(F32), key.astype(F32), value.astype(F32)
    padded = jnp.pad(key_f, ((tap_count - 1, 0), (0, 0)))
    shifted = jnp.zeros_like(key_f)
    for tap in range(tap_count):
        at = tap_count - 1 - tap
        shifted = shifted + padded[at : at + length] * taps[tap : tap + 1]
    products = shifted * value_f
    kernel, *up_one = fence(kernel, *up_one)
    up_two = near_two(up_ring, up_one)
    both = jnp.concatenate([products.astype(BF), kernel.astype(BF)], axis=1)
    both_re = mm(cos_t, both)
    both_im = mm(sin_t, both)
    prod_re, kern_re = both_re[:, :channels], both_re[:, channels:]
    prod_im, kern_im = both_im[:, :channels], both_im[:, channels:]
    spec_re = (prod_re * kern_re - prod_im * kern_im).astype(BF)
    spec_im = (prod_re * kern_im + prod_im * kern_re).astype(BF)
    convolved = (mm_tn(cos_t, spec_re) + mm_tn(sin_t, spec_im)) * (1.0 / length)
    convolved = convolved + skip * products
    mixed_heads = (query_f * convolved).astype(BF)
    mixed_other = flip(mixed_heads, "c")
    mixed_other, *up_two = fence(mixed_other, *up_two)
    up_own, out_own = assemble(
        up_ring,
        up_one,
        up_two,
        ring,
        ((ring, 2, 2, 2, rows, hidden // 2), (ring, 2, 2, rows, width)),
        write_up,
        "place_up",
    )
    up_own = up_own.reshape(width, hidden // 2)
    out_own = out_own.reshape(channels, width)
    out_other = flip(out_own, "c")
    residual = inputs + mm(mixed_heads, out_own) + mm(mixed_other, out_other)
    unit_two, scale_two = norm_stats(residual)
    second_rows = (unit_two * gain_two + bias_two).astype(BF)
    preact = mm(second_rows, up_own) + up_bias_own
    bend = jnp.tanh(SQRT_2_PI * (preact + 0.044715 * preact * preact * preact))
    activated = (0.5 * preact * (1.0 + bend)).astype(BF)
    slope = 0.5 * (1.0 + bend) + 0.5 * preact * (1.0 - bend * bend) * SQRT_2_PI * (
        1.0 + 3.0 * 0.044715 * preact * preact
    )
    activated, slope = fence(activated, slope.astype(BF))

    def mine(array):
        return lax.dynamic_slice_in_dim(array, core * block_len, block_len, 0)

    def theirs(array):
        return lax.dynamic_slice_in_dim(array, (1 - core) * block_len, block_len, 0)

    down_part = mm(activated, down_own)
    down_other = flip(theirs(down_part).astype(BF), "c").astype(F32)
    mixed = mine(residual) + mine(down_part) + down_other + down_bias_all
    mixed = mixed.astype(BF)

    act_grad = mm_nt(grad_all, down_own)
    pre_grad = (act_grad * slope.astype(F32)).astype(BF)
    second_part = mm_nt(pre_grad, up_own)
    second_other = flip(theirs(second_part).astype(BF), "c").astype(F32)
    down_sum = mm_tn(activated, grad_all).astype(BF).reshape(ring, 2, 1, 2, -1, rows, width)
    up_sum = mm_tn(second_rows, pre_grad).astype(BF).reshape(ring, 2, 2, 2, 1, rows, hidden // 2)
    up_bias_grad = mm(jnp.ones((8, length), BF), pre_grad)[0]
    second_part, down_sum, up_sum, second_other = fence(second_part, down_sum, up_sum, second_other)

    ffn_one = pair_one(down_sum, up_sum)
    second_grad = mine(second_part) + second_other
    unit_two_h, scale_two_h = mine(unit_two), mine(scale_two)
    grad_half_f = grad_half.astype(F32)
    gain_two_grad = jnp.sum(second_grad * unit_two_h, axis=0)
    bias_two_grad = jnp.sum(second_grad, axis=0)
    down_bias_grad = jnp.sum(grad_half_f, axis=0)
    resid_grad = grad_half_f + norm_back(second_grad, unit_two_h, scale_two_h, gain_two)
    mix_half = resid_grad.astype(BF)
    mix_grad = ordered(mix_half, flip(mix_half, "c"), core, 0).reshape(length, width)

    head_grad = mm_nt(mix_grad, out_own).astype(BF).astype(F32)
    query_grad = (head_grad * convolved).astype(BF)
    conv_grad = head_grad * query_f
    conv_low = conv_grad.astype(BF)
    skip_grad = jnp.sum(conv_grad * products, axis=0)
    grad_re = mm(cos_t, conv_low)
    grad_im = mm(sin_t, conv_low)
    out_grad = mm_tn(mixed_heads, mix_grad).astype(BF)
    q_grad = mm_tn(first_rows, query_grad).astype(BF)
    grad_re, grad_im, q_grad, out_grad = fence(grad_re, grad_im, q_grad, out_grad)

    back_re = (grad_re * kern_re + grad_im * kern_im).astype(BF)
    back_im = (grad_im * kern_re - grad_re * kern_im).astype(BF)
    lag_re = (grad_re * prod_re + grad_im * prod_im).astype(BF)
    lag_im = (grad_im * prod_re - grad_re * prod_im).astype(BF)
    lag_grad = (mm_tn(lag_re, cos_t) + mm_tn(lag_im, sin_t)) * (1.0 / length)
    lag_sum = lag_grad.astype(BF).reshape(ring, 2, 1, 2, 1, rows, length)
    back = (mm_tn(cos_t, back_re) + mm_tn(sin_t, back_im)) * (1.0 / length)
    product_grad = back + skip * conv_grad
    out_sum = out_grad.reshape(ring, 2, 1, 2, 1, rows, width)
    q_sum = q_grad.reshape(ring, 2, 2, 2, 1, rows, channels)
    product_grad, lag_sum, *ffn_one = fence(product_grad, lag_sum, *ffn_one)
    ffn_two = pair_two(down_sum, up_sum, ffn_one, ring)
    outq_one = direct_one((q_sum, out_sum, lag_sum), ring, length // 8)
    shifted_grad = product_grad * value_f
    value_grad = (product_grad * shifted).astype(BF)
    padded_grad = jnp.pad(shifted_grad, ((0, tap_count - 1), (0, 0)))
    key_grad = jnp.zeros_like(key_f)
    tap_rows = []
    for tap in range(tap_count):
        at = tap_count - 1 - tap
        key_grad = key_grad + padded_grad[tap : tap + length] * taps[tap : tap + 1]
        tap_rows.append(jnp.sum(shifted_grad * padded[at : at + length], axis=0))
    key_grad = key_grad.astype(BF)
    kv_grad = jnp.concatenate([key_grad, value_grad], axis=1)
    kv_sum = mm_tn(first_rows, kv_grad).astype(BF).reshape(ring, 2, 2, 2, 1, rows, 2 * channels)
    first_part = mm_nt(jnp.concatenate([query_grad, kv_grad], axis=1), w_qkv)
    kv_sum, first_part, *ffn_two = fence(kv_sum, first_part, *ffn_two)

    first_other = flip(theirs(first_part).astype(BF), "c").astype(F32)
    ffn_held = pair_three(down_sum, up_sum, ffn_one, ffn_two, ring, width)
    ffn_three = ring_send(ffn_held, ring)
    kv_one = direct_one((kv_sum,), ring, channels)
    first_grad = mine(first_part) + first_other
    unit_one_h, scale_one_h = norm_stats(token_half.astype(F32))
    gain_one_grad = jnp.sum(first_grad * unit_one_h, axis=0)
    bias_one_grad = jnp.sum(first_grad, axis=0)
    token_grad = resid_grad + norm_back(first_grad, unit_one_h, scale_one_h, gain_one)
    token_grad, *outq_one = fence(token_grad, *outq_one)
    lag_width = length // 8
    outq_held = direct_two((q_sum, out_sum, lag_sum), outq_one, ring, lag_width)
    outq_three = ring_send(outq_held, ring)
    token_grad, mixed, *kv_one = fence(token_grad, mixed, *kv_one)

    kv_held = direct_two((kv_sum,), kv_one, ring, channels)
    kv_three = ring_send(kv_held, ring)
    token_grad = swap_cy(token_grad.astype(BF)).astype(F32)[None]
    mixed = swap_cy(mixed)[None]
    ffn_s = ring_sum(ffn_held, ffn_three)
    down_pieces = up_rows // rows
    down_s = ffn_s[:down_pieces].reshape(up_rows, width)
    up_half = (ffn_s.shape[0] - down_pieces) // 2
    up_s = jnp.stack([join(ffn_s[down_pieces : down_pieces + up_half]), join(ffn_s[down_pieces + up_half :])])
    up_s = merge_columns(up_s, core, groups)
    outq_s = ring_sum(outq_held, outq_three)
    q_pieces = channels // lag_width
    query_s = merge_columns(
        jnp.stack([join(outq_s[:q_pieces]), join(outq_s[q_pieces : 2 * q_pieces])]), core, groups
    )
    out_s = join(outq_s[2 * q_pieces : 4 * q_pieces])
    lag_s = join(outq_s[4 * q_pieces :])
    up_s, down_s, query_s, out_s, lag_s, *kv_three = fence(up_s, down_s, query_s, out_s, lag_s, *kv_three)
    coef_s, rate_s = ssm_kernel_grads(lag_s, ssm_coef.astype(F32), ssm_rate.astype(F32))
    kv_s = ring_sum(kv_held, kv_three)
    key_s = merge_columns(kv_s[0::2], core, groups)
    value_s = merge_columns(kv_s[1::2], core, groups)

    vec_grads = jnp.stack(
        [gain_one_grad, bias_one_grad, gain_two_grad, bias_two_grad, down_bias_grad]
    )
    vec_grads = vec_grads.reshape(5, ring, 2, 2, 2, rows)
    vec_keep = lax.dynamic_index_in_dim(vec_grads, core, 3, keepdims=False)
    vec_send = lax.dynamic_index_in_dim(vec_grads, 1 - core, 3, keepdims=False)
    vec_sum = (vec_keep + flip(vec_send, "c")).transpose(1, 2, 3, 0, 4)

    def flat(array):
        return array.reshape(ring, 2, 2, -1)

    small = jnp.concatenate(
        [
            flat(jnp.stack(tap_rows, axis=1)),
            flat(skip_grad),
            flat(up_bias_grad),
            flat(vec_sum),
        ],
        axis=3,
    )
    small_pad = -small.shape[3] % 1024
    small = jnp.pad(small, ((0, 0), (0, 0), (0, 0), (0, small_pad)))
    small = small.reshape(ring, 2, 2, -1, 128)

    def pick_small(x, y):
        return lax.dynamic_slice(
            small, (0, x, y, 0, 0), (ring, 1, 1) + small.shape[3:]
        ).reshape((ring,) + small.shape[3:])

    near_small = scatter_near(pick_small)
    here = lax.axis_index("r")
    small = take(near_small, 0, here)
    for distance in range(1, ring):
        small = small + shift_ring(
            take(near_small, 0, lax.rem(here + distance, ring)), distance, ring
        )
    small = small.reshape(-1)
    pieces = []
    offset = 0
    for size in (rows * tap_count, rows, up_rows, 5 * rows):
        pieces.append(small[offset : offset + size])
        offset += size
    vec_s = pieces[3].reshape(5, rows)
    return (
        mixed,
        token_grad,
        vec_s[0],
        vec_s[1],
        query_s,
        key_s,
        value_s,
        pieces[0].reshape(rows, tap_count),
        coef_s,
        rate_s,
        pieces[1],
        out_s,
        vec_s[2],
        vec_s[3],
        up_s,
        pieces[2],
        down_s,
        vec_s[4],
    )


def solution(mesh):
    dp_size, seq_size = mesh.devices.shape
    ring = dp_size // 4
    grid = Mesh(mesh.devices.reshape(ring, 2, 2, seq_size), ("r", "x", "c", "y"))
    dp = ("r", "x", "c")
    act = P(dp, "y", None)
    vec = P(dp + ("y",))
    mat = P(dp + ("y",), None)
    return jax.shard_map(
        functools.partial(body, ring),
        mesh=grid,
        in_specs=(
            act, P(dp), act, vec, vec, mat, mat, mat, mat, mat, mat, vec, mat, vec, vec, mat, vec, mat, vec,
        ),
        out_specs=(
            act, act, vec, vec, mat, mat, mat, mat, mat, mat, vec, mat, vec, vec, mat, vec, mat, vec,
        ),
        check_vma=False,
    )
```

```python
import functools
import math

import jax
import jax.numpy as jnp
from jax import lax
from jax.experimental import pallas as pl
from jax.experimental.pallas import tpu as pltpu
from jax.sharding import Mesh, PartitionSpec as P

EPS = 1e-05
BF = jnp.bfloat16
F32 = jnp.float32
SQRT_2_PI = math.sqrt(2.0 / math.pi)
MISC = ("r", "x", "y")


def flip(value, axis):
    return lax.ppermute(value, axis, [(0, 1), (1, 0)])


def ordered(mine, other, place, axis):
    first = jnp.where(place == 0, mine, other)
    second = jnp.where(place == 0, other, mine)
    return jnp.stack([first, second], axis=axis)


def swap_cy(value):
    moved = lax.ppermute(value, ("c", "y"), [(1, 2), (2, 1)])
    return jnp.where(lax.axis_index("c") == lax.axis_index("y"), value, moved)


def shift_ring(value, distance, ring):
    return lax.ppermute(value, "r", [(i, (i + distance) % ring) for i in range(ring)])


def flip_xy(value):
    return lax.ppermute(value, ("x", "y"), [(i, 3 - i) for i in range(4)])


def place(whole, part, starts):
    return lax.dynamic_update_slice(whole, part, starts)


def gather_ring(block, ring):
    here = lax.axis_index("r")
    rest = (0,) * block.ndim
    whole = jnp.zeros((ring,) + block.shape, block.dtype)
    whole = place(whole, block[None], (here,) + rest)
    for distance in range(1, ring):
        moved = shift_ring(block, distance, ring)
        whole = place(whole, moved[None], (lax.rem(here - distance + ring, ring),) + rest)
    return whole


def ring_pieces(block, ring):
    blocks = [block] + [shift_ring(block, d, ring) for d in range(1, ring)]
    return tuple(jnp.stack([part[half] for part in blocks]) for half in range(2))


def near_one(halves):
    return flip(halves[0], "y"), flip(halves[1], "x")


def near_two(halves, moved):
    first = flip(jnp.concatenate([halves[0], moved[0]]), "x")
    second = flip(jnp.concatenate([halves[1], moved[1]]), "y")
    return first, second


def chip_ids():
    return jnp.stack([lax.axis_index("r"), lax.axis_index("x"), lax.axis_index("y")]).astype(jnp.int32)


def grant(*blocks):
    total = 0
    for shape, kind in blocks:
        rows = -(-shape[-2] // 16) * 16
        total += math.prod(shape[:-2]) * rows * shape[-1] * jnp.dtype(kind).itemsize
    return pltpu.CompilerParams(vmem_limit_bytes=2 * total + (2 << 20))


def assemble_body(write, ids, *refs):
    ins, outs = refs[:8], refs[8:]
    for half in range(2):
        for index in range(4):
            x = lax.rem(ids[1] + index // 2, 2)
            y = lax.rem(ids[2] + index % 2, 2)
            write(outs, ins[4 * half + index], half, x, y)


def assemble(halves, one, two, ring, shapes, write, name):
    sources = (
        (halves[0], 0), (one[0], 0), (two[0], 0), (two[0], ring),
        (halves[1], 0), (two[1], 0), (one[1], 0), (two[1], ring),
    )
    tail = halves[0].shape[1:]
    zeros = (0,) * len(tail)
    specs = [
        pl.BlockSpec((None,) + tail, lambda i, ids, base=base: (i + base,) + zeros) for _, base in sources
    ]
    moved = 32 * math.prod(tail) * ring
    return pl.pallas_call(
        functools.partial(assemble_body, write),
        out_shape=tuple(jax.ShapeDtypeStruct(shape, halves[0].dtype) for shape in shapes),
        grid_spec=pltpu.PrefetchScalarGridSpec(
            num_scalar_prefetch=1,
            grid=(ring,),
            in_specs=specs,
            out_specs=tuple(
                pl.BlockSpec(
                    (None,) + shape[1:],
                    lambda i, ids, rank=len(shape): (lax.rem(ids[0] + ring - i, ring),) + (0,) * (rank - 1),
                )
                for shape in shapes
            ),
        ),
        compiler_params=grant(*[(tail, BF)] * 8, *[(shape[1:], BF) for shape in shapes]),
        cost_estimate=pl.CostEstimate(flops=0, bytes_accessed=moved, transcendentals=0),
        name=name,
    )(chip_ids(), *[array for array, _ in sources])


def write_heads(outs, part, half, x, y):
    outs[0][x, half, y] = part[0]


def write_up(outs, part, half, x, y):
    lanes = part.shape[-1]
    count = part.shape[0] - 1
    for index in range(count):
        outs[0][x, half, y, :, index * lanes : (index + 1) * lanes] = part[index]
    outs[1][x, y, :, half * lanes : (half + 1) * lanes] = part[count]


def here_x(i, ids):
    return ids[1]


def other_x(i, ids):
    return 1 - ids[1]


def here_y(i, ids):
    return ids[2]


def other_y(i, ids):
    return 1 - ids[2]


def step_r(i, ids):
    return i


def turn_r(ring):
    return lambda i, ids: lax.rem(ids[0] + i, ring)


def sums_body(plan, ids, *refs):
    ins, outs = refs[: len(refs) - len(plan)], refs[len(refs) - len(plan) :]
    for out, columns in zip(outs, plan):
        width = out.shape[2]
        at = 0
        for terms in columns:
            first = ins[terms[0]]
            cores, extra, _, lanes = first.shape
            index = 0
            for core in range(cores):
                for more in range(extra):
                    for low in range(0, lanes, width):
                        total = None
                        for term in terms:
                            ref = ins[term]
                            if len(ref.shape) == 4:
                                value = ref[core, more, :, low : low + width]
                            else:
                                value = ref[at + index]
                            value = value.astype(F32)
                            total = value if total is None else total + value
                        out[at + index] = total.astype(out.dtype)
                        index += 1
            at += index


def sums(ring, jobs):
    arrays, specs, plan, shapes = [], [], [], []
    for width, columns in jobs:
        pieces = 0
        numbers = []
        for terms in columns:
            mine = []
            for count, (array, picks) in enumerate(terms):
                tail = array.shape[len(picks) :]
                block = tuple(
                    size if pick is None else None for size, pick in zip(array.shape, picks)
                ) + tail

                def index_map(i, ids, picks=picks, tail=tail):
                    return tuple(0 if pick is None else pick(i, ids) for pick in picks) + (0,) * len(tail)

                if count == 0:
                    held = [size for size in block if size is not None]
                    pieces += held[0] * held[1] * (held[3] // width)
                mine.append(len(arrays))
                arrays.append(array)
                specs.append(pl.BlockSpec(block, index_map))
            numbers.append(mine)
        plan.append(numbers)
        rows = columns[0][0][0].shape[-2]
        shapes.append(jax.ShapeDtypeStruct((ring, pieces, rows, width), BF))
    moved = sum(2 * math.prod(shape.shape) * 2 for shape in shapes)
    return pl.pallas_call(
        functools.partial(sums_body, plan),
        out_shape=tuple(shapes),
        grid_spec=pltpu.PrefetchScalarGridSpec(
            num_scalar_prefetch=1,
            grid=(ring,),
            in_specs=specs,
            out_specs=tuple(
                pl.BlockSpec((None,) + shape.shape[1:], lambda i, ids: (i, 0, 0, 0)) for shape in shapes
            ),
        ),
        compiler_params=grant(
            *[
                (tuple(size for size in spec.block_shape if size is not None), BF)
                for spec in specs
            ],
            *[(shape.shape[1:], BF) for shape in shapes],
        ),
        cost_estimate=pl.CostEstimate(flops=0, bytes_accessed=2 * moved, transcendentals=0),
        name="sums",
    )(chip_ids(), *[pltpu.with_memory_space_constraint(array, pltpu.HBM) for array in arrays])


def take(parts, axis, index):
    return lax.dynamic_index_in_dim(parts, index, axis, keepdims=False)


def pair_one(y_first, x_first):
    x, y = lax.axis_index("x"), lax.axis_index("y")
    return flip(take(y_first, 3, 1 - y), "y"), flip(take(x_first, 1, 1 - x), "x")


def pair_two(y_first, x_first, moved, ring):
    one = [
        (y_first, (step_r, other_x, None, here_y)),
        (moved[0], (step_r, other_x, None)),
    ]
    two = [
        (x_first, (step_r, here_x, None, other_y)),
        (moved[1], (step_r, None, other_y)),
    ]
    send_one, send_two = sums(ring, [(y_first.shape[-1], [one]), (x_first.shape[-1], [two])])
    shape_one = (ring, y_first.shape[2]) + y_first.shape[4:]
    shape_two = (ring, x_first.shape[2]) + x_first.shape[4:]
    return flip(send_one, "x").reshape(shape_one), flip(send_two, "y").reshape(shape_two)


def pair_three(y_first, x_first, moved_one, moved_two, ring, width):
    turn = turn_r(ring)
    one = [
        (y_first, (turn, here_x, None, here_y)),
        (moved_one[0], (turn, here_x, None)),
        (moved_two[0], (turn, None)),
    ]
    two = [
        (x_first, (turn, here_x, None, here_y)),
        (moved_one[1], (turn, None, here_y)),
        (moved_two[1], (turn, None)),
    ]
    return sums(ring, [(width, [one, two])])[0]


def direct_one(arrays, ring, width):
    spots = ((here_x, other_y), (other_x, here_y), (other_x, other_y))
    along_y, along_x, across = sums(
        ring, [(width, [[(array, (step_r, x, None, y))] for array in arrays]) for x, y in spots]
    )
    return flip(along_y, "y"), flip(along_x, "x"), flip_xy(across)


def direct_two(arrays, moved, ring, width):
    turn = turn_r(ring)
    columns = [
        [(array, (turn, here_x, None, here_y))] + [(part, (turn,)) for part in moved] for array in arrays
    ]
    return sums(ring, [(width, columns)])[0]


def ring_send(held, ring):
    return tuple(shift_ring(held[distance], distance, ring) for distance in range(1, ring))


def ring_sum(held, moved):
    total = held[0].astype(F32)
    for part in moved:
        total = total + part.astype(F32)
    return total


def join(pieces):
    return jnp.concatenate([pieces[i] for i in range(pieces.shape[0])], axis=1)


def scatter_near(pick):
    x, y = lax.axis_index("x"), lax.axis_index("y")
    total = pick(x, y).astype(F32)
    total = total + flip(pick(x, 1 - y), "y").astype(F32)
    total = total + flip(pick(1 - x, y), "x").astype(F32)
    return total + flip_xy(pick(1 - x, 1 - y)).astype(F32)


def gather_quad(block):
    x, y = lax.axis_index("x"), lax.axis_index("y")
    parts = ((block, x, y), (flip(block, "y"), x, 1 - y), (flip(block, "x"), 1 - x, y), (flip_xy(block), 1 - x, 1 - y))
    full = jnp.zeros((2, 2) + block.shape, block.dtype)
    for part, at_x, at_y in parts:
        full = place(full, part[None, None], (at_x, at_y) + (0,) * block.ndim)
    return full


def fence(*values):
    return lax.optimization_barrier(values)


def merge_columns(parts, core, groups):
    keep = lax.dynamic_index_in_dim(parts, core, 0, keepdims=False)
    send = lax.dynamic_index_in_dim(parts, 1 - core, 0, keepdims=False)
    count, cols = keep.shape
    other = flip(send.astype(BF), "c").astype(F32)
    grid = ordered(
        keep.reshape(count, groups, -1), other.reshape(count, groups, -1), core, 2
    )
    return grid.reshape(count, 2 * cols)


def mm(left, right):
    return jnp.dot(left, right, preferred_element_type=F32)


def mm_tn(left, right):
    return lax.dot_general(
        left, right, (((0,), (0,)), ((), ())), preferred_element_type=F32
    )


def mm_nt(left, right):
    return lax.dot_general(
        left, right, (((1,), (1,)), ((), ())), preferred_element_type=F32
    )


def norm_stats(values):
    mean = jnp.mean(values, axis=-1, keepdims=True)
    centred = values - mean
    variance = jnp.mean(centred * centred, axis=-1, keepdims=True)
    scale = lax.rsqrt(variance + EPS)
    return centred * scale, scale


def norm_back(grad, unit, scale, gain):
    inner = grad * gain
    mean_one = jnp.mean(inner, axis=-1, keepdims=True)
    mean_two = jnp.mean(inner * unit, axis=-1, keepdims=True)
    return scale * (inner - mean_one - unit * mean_two)


def tables_body(token_ref, cos_ref, sin_ref, cos_turn_ref, sin_turn_ref):
    length = cos_ref.shape[0]
    part = 32
    blocks = length // part
    step = math.pi / (2.0 * length)
    period = 4 * length
    rows = lax.broadcasted_iota(jnp.int32, (part, length), 0)
    cols = lax.broadcasted_iota(jnp.int32, (part, length), 1)

    def turns(count):
        angle = (count & (period - 1)).astype(F32) * step
        return jnp.cos(angle), jnp.sin(angle)

    def fill(high, low, cos_out, sin_out):
        (cos_high, sin_high), (cos_low, sin_low) = turns(high), turns(low)
        for block in range(blocks):
            ch, sh = cos_high[block : block + 1], sin_high[block : block + 1]
            at = pl.ds(block * part, part)
            cos_out[at, :] = (ch * cos_low - sh * sin_low).astype(BF)
            sin_out[at, :] = (sh * cos_low + ch * sin_low).astype(BF)

    fill(2 * part * rows * cols, (2 * rows + 1) * cols, cos_ref, sin_ref)
    fill(part * rows * (2 * cols + 1), rows * (2 * cols + 1), cos_turn_ref, sin_turn_ref)


def dft_tables(length, token):
    table = jax.ShapeDtypeStruct((length, length), BF)
    return pl.pallas_call(
        tables_body,
        out_shape=(table,) * 4,
        in_specs=[pl.BlockSpec(memory_space=pl.ANY)],
        out_specs=tuple(in_vmem(4)),
        cost_estimate=pl.CostEstimate(flops=7 * 10**9, bytes_accessed=8 * length * length, transcendentals=0),
        compiler_params=pltpu.CompilerParams(vmem_limit_bytes=4 << 20),
        name="dft_tables",
    )(token)


def norm_body(core_ref, mine_ref, other_ref, vec_ref, all_ref, rows_ref):
    half = mine_ref.shape[0]
    step = 128
    for index, ref in enumerate((mine_ref, other_ref)):
        place = lax.rem(core_ref[0] + index, 2) * half
        for start in range(0, half, step):
            block = ref[start : start + step, :]
            at = pl.ds(pl.multiple_of(place + start, step), step)
            all_ref[at, :] = block
            unit, _ = norm_stats(block.astype(F32))
            rows_ref[at, :] = (unit * vec_ref[8:9, :] + vec_ref[9:10, :]).astype(BF)


def first_norm(mine, other, core, vectors):
    half, width = mine.shape
    wide = jax.ShapeDtypeStruct((2 * half, width), BF)
    return pl.pallas_call(
        norm_body,
        out_shape=(wide, wide),
        in_specs=[pl.BlockSpec(memory_space=pltpu.SMEM)] + in_vmem(3),
        out_specs=tuple(in_vmem(2)),
        cost_estimate=pl.CostEstimate(flops=3 * 10**9, bytes_accessed=4 * half * width, transcendentals=0),
        compiler_params=pltpu.CompilerParams(vmem_limit_bytes=4 << 20),
        name="first_norm",
    )(core.astype(jnp.int32).reshape(1), mine, other, vectors)


def in_vmem(count):
    return [pl.BlockSpec(memory_space=pltpu.VMEM)] * count


def kernel_body(part, coef_ref, rate_ref, out_ref, high_ref, low_ref):
    states = coef_ref.shape[0]
    length = out_ref.shape[0]
    blocks = length // part
    lanes = out_ref.shape[1]
    high_ids = lax.broadcasted_iota(jnp.int32, (blocks, lanes), 0).astype(F32) * (part / length)
    low_ids = lax.broadcasted_iota(jnp.int32, (part, lanes), 0).astype(F32) * (1.0 / length)

    def fill(state, carry):
        rate = rate_ref[pl.ds(state, 1), :]
        coef = coef_ref[pl.ds(state, 1), :] * (length ** (-0.5))
        high_ref[state] = coef * jnp.exp(-rate * high_ids)
        low_ref[state] = jnp.exp(-rate * low_ids)
        return carry

    lax.fori_loop(0, states, fill, 0)
    for start in range(0, blocks, 8):

        def add(state, sums):
            low = low_ref[state]
            return tuple(
                total + high_ref[state, pl.ds(start + index, 1), :] * low
                for index, total in enumerate(sums)
            )

        zero = jnp.zeros((part, lanes), F32)
        sums = lax.fori_loop(0, states, add, (zero,) * 8, unroll=4)
        for index, total in enumerate(sums):
            out_ref[pl.ds((start + index) * part, part), :] = total.astype(out_ref.dtype)


def spectrum_body(part, states, params_ref, cos_ref, sin_ref, re_ref, im_ref, kernel_ref, high_ref, low_ref, coef_part, rate_part):
    length, channels = kernel_ref.shape
    for start in range(0, channels, 128):
        lanes = pl.ds(start, 128)
        coef_part[...] = params_ref[0:states, lanes]
        rate_part[...] = params_ref[states : 2 * states, lanes]
        kernel_body(part, coef_part, rate_part, kernel_ref.at[:, lanes], high_ref, low_ref)
    for start in range(0, length, 256):
        rows = pl.ds(start, 256)
        re_ref[rows, :] = mm(cos_ref[rows, :], kernel_ref[...]).astype(BF)
        im_ref[rows, :] = mm(sin_ref[rows, :], kernel_ref[...]).astype(BF)


def ssm_spectrum(params, states, cos_t, sin_t, length):
    channels = params.shape[1]
    part = 32
    return pl.pallas_call(
        functools.partial(spectrum_body, part, states),
        out_shape=(jax.ShapeDtypeStruct((length, channels), BF),) * 2,
        in_specs=in_vmem(3),
        out_specs=tuple(in_vmem(2)),
        scratch_shapes=[
            pltpu.VMEM((length, channels), BF),
            pltpu.VMEM((states, length // part, 128), F32),
            pltpu.VMEM((states, part, 128), F32),
            pltpu.VMEM((states, 128), F32),
            pltpu.VMEM((states, 128), F32),
        ],
        cost_estimate=pl.CostEstimate(
            flops=600 * length * states * channels, bytes_accessed=2 * length * channels * 4, transcendentals=0
        ),
        compiler_params=pltpu.CompilerParams(vmem_limit_bytes=8 << 20),
        name="ssm_spectrum",
    )(params, cos_t, sin_t)


def conv_body(
    first, tap_count, heads_ref, kern_re_ref, kern_im_ref, params_ref, cos_ref, sin_ref, cos_turn_ref, sin_turn_ref,
    mixed_ref, conv_ref, shifted_ref, prod_re_ref, prod_im_ref,
    products_ref, low_ref, spec_re_ref, spec_im_ref,
):
    length, channels = mixed_ref.shape
    step = 128
    last = first + tap_count
    for start in range(0, length, step):
        rows = pl.ds(start, step)
        if start == 0:
            keys = heads_ref[0:step, channels : 2 * channels].astype(F32)
            keys = jnp.concatenate([jnp.zeros((8, channels), F32), keys], axis=0)
        else:
            keys = heads_ref[start - 8 : start + step, channels : 2 * channels].astype(F32)
        shifted = keys[8:] * params_ref[first : first + 1, :]
        for tap in range(1, tap_count):
            shifted = shifted + keys[8 - tap : 8 - tap + step] * params_ref[first + tap : first + tap + 1, :]
        shifted_ref[rows, :] = shifted.astype(BF)
        products = shifted * heads_ref[rows, 2 * channels : 3 * channels].astype(F32)
        products_ref[rows, :] = products
        low_ref[rows, :] = products.astype(BF)
    for start in range(0, length, 256):
        rows = pl.ds(start, 256)
        prod_re = mm(cos_ref[rows, :], low_ref[...])
        prod_im = mm(sin_ref[rows, :], low_ref[...])
        kern_re, kern_im = kern_re_ref[rows, :].astype(F32), kern_im_ref[rows, :].astype(F32)
        prod_re_ref[rows, :] = prod_re.astype(BF)
        prod_im_ref[rows, :] = prod_im.astype(BF)
        spec_re_ref[rows, :] = (prod_re * kern_re - prod_im * kern_im).astype(BF)
        spec_im_ref[rows, :] = (prod_re * kern_im + prod_im * kern_re).astype(BF)
    for start in range(0, length, 256):
        rows = pl.ds(start, 256)
        conv = mm(cos_turn_ref[rows, :], spec_re_ref[...]) + mm(sin_turn_ref[rows, :], spec_im_ref[...])
        conv = conv * (1.0 / length) + params_ref[last : last + 1, :] * products_ref[rows, :]
        conv_ref[rows, :] = conv.astype(BF)
        mixed_ref[rows, :] = (heads_ref[rows, 0:channels].astype(F32) * conv).astype(BF)


def conv_forward(heads, kern_re, kern_im, params, first, tap_count, tables):
    length, channels = kern_re.shape
    wide = jax.ShapeDtypeStruct((length, channels), BF)
    return pl.pallas_call(
        functools.partial(conv_body, first, tap_count),
        out_shape=(wide,) * 5,
        in_specs=in_vmem(8),
        out_specs=tuple(in_vmem(5)),
        scratch_shapes=[
            pltpu.VMEM((length, channels), F32),
            pltpu.VMEM((length, channels), BF),
            pltpu.VMEM((length, channels), BF),
            pltpu.VMEM((length, channels), BF),
        ],
        cost_estimate=pl.CostEstimate(
            flops=24 * length * length * channels, bytes_accessed=16 * length * channels, transcendentals=0
        ),
        compiler_params=pltpu.CompilerParams(vmem_limit_bytes=10 << 20),
        name="conv_forward",
    )(heads, kern_re, kern_im, params, *tables)


def ssm_kernel_grads(grad, coef, rate):
    length = grad.shape[1]
    times = lax.broadcasted_iota(jnp.int32, (1, 1, length), 2).astype(F32) * (1.0 / length)
    weighted = grad[:, None] * jnp.exp(-rate[:, :, None] * times)
    scale = length ** (-0.5)
    return jnp.sum(weighted, axis=2) * scale, -coef * jnp.sum(weighted * times, axis=2) * scale


def row_block(cols, kind_rows=256):
    return pl.BlockSpec((kind_rows, cols), lambda i: (i, 0))


def whole_block(rows, cols):
    return pl.BlockSpec((rows, cols), lambda i: (0, 0), pipeline_mode=pl.Buffered(1))


def turned_block(cols, steps):
    return pl.BlockSpec((256, cols), lambda i, core: (lax.rem(i + steps // 2 * (1 - core[0]), steps), 0))


def same_block(rows, cols):
    return pl.BlockSpec((rows, cols), lambda i, core: (0, 0), pipeline_mode=pl.Buffered(1))


def half_blocks(cols, steps):
    theirs = pl.BlockSpec((256, cols), lambda i, core: (jnp.minimum(i, steps // 2 - 1), 0))
    mine = pl.BlockSpec((256, cols), lambda i, core: (jnp.maximum(i - steps // 2, 0), 0))
    return theirs, mine


def put_half(theirs_ref, mine_ref, theirs, mine):
    first = pl.program_id(0) < pl.num_programs(0) // 2

    @pl.when(first)
    def _():
        theirs_ref[...] = theirs.astype(theirs_ref.dtype)

    @pl.when(jnp.logical_not(first))
    def _():
        mine_ref[...] = mine.astype(mine_ref.dtype)


def ffn_forward_body(
    core_ref, resid_ref, vec_ref, up_ref, up_bias_ref, down_ref,
    rows_ref, act_ref, slope_ref, theirs_ref, mine_ref,
):
    resid = resid_ref[...]
    unit, _ = norm_stats(resid)
    second = (unit * vec_ref[10:11, :] + vec_ref[11:12, :]).astype(BF)
    rows_ref[...] = second
    pre = mm(second, up_ref[...]) + up_bias_ref[...]
    square = pre * pre
    bend = jnp.tanh(pre * (SQRT_2_PI + SQRT_2_PI * 0.044715 * square))
    half = 0.5 * pre
    act = (half + half * bend).astype(BF)
    act_ref[...] = act
    steep = SQRT_2_PI + 3.0 * SQRT_2_PI * 0.044715 * square
    slope_ref[...] = (0.5 + 0.5 * bend + half * (1.0 - bend * bend) * steep).astype(BF)
    part = mm(act, down_ref[...])
    put_half(theirs_ref, mine_ref, part, part + resid + vec_ref[12:13, :])


def ffn_forward(core, resid, vectors, up, up_bias, down):
    length, width = resid.shape
    hidden = up.shape[1]
    steps = length // 256
    return pl.pallas_call(
        ffn_forward_body,
        out_shape=(
            jax.ShapeDtypeStruct((length, width), BF),
            jax.ShapeDtypeStruct((length, hidden), BF),
            jax.ShapeDtypeStruct((length, hidden), BF),
            jax.ShapeDtypeStruct((length // 2, width), BF),
            jax.ShapeDtypeStruct((length // 2, width), F32),
        ),
        grid_spec=pltpu.PrefetchScalarGridSpec(
            num_scalar_prefetch=1,
            grid=(steps,),
            in_specs=[
                turned_block(width, steps),
                same_block(vectors.shape[0], width),
                same_block(width, hidden),
                same_block(1, hidden),
                same_block(hidden, width),
            ],
            out_specs=(
                turned_block(width, steps),
                turned_block(hidden, steps),
                turned_block(hidden, steps),
            )
            + half_blocks(width, steps),
        ),
        compiler_params=pltpu.CompilerParams(vmem_limit_bytes=28 << 20),
        cost_estimate=pl.CostEstimate(
            flops=8 * length * width * hidden, bytes_accessed=12 * length * width, transcendentals=0
        ),
        name="ffn_forward",
    )(core, resid, vectors, up, up_bias, down)


def ffn_backward_body(core_ref, grad_ref, slope_ref, up_ref, down_ref, pre_ref, bias_ref, theirs_ref, mine_ref):
    act_grad = mm_nt(grad_ref[...], down_ref[...])
    pre = (act_grad * slope_ref[...].astype(F32)).astype(BF)
    pre_ref[...] = pre
    part = mm_nt(pre, up_ref[...])
    put_half(theirs_ref, mine_ref, part, part)

    @pl.when(pl.program_id(0) == 0)
    def _():
        bias_ref[...] = jnp.zeros_like(bias_ref)

    bias_ref[...] += jnp.sum(pre.astype(F32), axis=0, keepdims=True)


def ffn_backward(core, grad, slope, up, down):
    length, width = grad.shape
    hidden = up.shape[1]
    steps = length // 256
    return pl.pallas_call(
        ffn_backward_body,
        out_shape=(
            jax.ShapeDtypeStruct((length, hidden), BF),
            jax.ShapeDtypeStruct((1, hidden), F32),
            jax.ShapeDtypeStruct((length // 2, width), BF),
            jax.ShapeDtypeStruct((length // 2, width), F32),
        ),
        grid_spec=pltpu.PrefetchScalarGridSpec(
            num_scalar_prefetch=1,
            grid=(steps,),
            in_specs=[
                turned_block(width, steps),
                turned_block(hidden, steps),
                same_block(width, hidden),
                same_block(hidden, width),
            ],
            out_specs=(turned_block(hidden, steps), pl.BlockSpec((1, hidden), lambda i, core: (0, 0)))
            + half_blocks(width, steps),
        ),
        compiler_params=pltpu.CompilerParams(vmem_limit_bytes=24 << 20),
        cost_estimate=pl.CostEstimate(
            flops=6 * length * width * hidden, bytes_accessed=12 * length * width, transcendentals=0
        ),
        name="ffn_backward",
    )(core, grad, slope, up, down)


def body(
    ring,
    tokens,
    lengths,
    cotangent,
    norm1_gain,
    norm1_bias,
    w_query,
    w_key,
    w_value,
    shift_taps,
    ssm_coef,
    ssm_rate,
    skip_gain,
    w_out,
    norm2_gain,
    norm2_bias,
    w_up,
    up_bias,
    w_down,
    down_bias,
):
    core = lax.axis_index("c")
    groups = 2 * ring
    _, block_len, width = tokens.shape
    length = 2 * block_len
    rows = w_query.shape[0]
    up_rows = up_bias.shape[0]
    hidden = w_up.shape[1]
    states = ssm_coef.shape[1]
    tap_count = shift_taps.shape[1]
    channels = width // 2

    def columns(weight, which):
        grid = weight.reshape(rows, groups, 2, -1)
        return jnp.where(which == 0, grid[:, :, 0], grid[:, :, 1]).reshape(rows, -1)

    down_own = lax.all_gather(w_down, MISC, axis=0, tiled=True)
    matrices = (w_query, w_key, w_value, w_up)
    keep = jnp.concatenate([columns(w, core) for w in matrices], axis=1)
    send = jnp.concatenate([columns(w, 1 - core) for w in matrices], axis=1)
    norm1_gain, ssm_coef, ssm_rate, send = fence(norm1_gain, ssm_coef, ssm_rate, send)
    packed = ordered(keep, flip(send, "c"), core, 0)
    first_pack = packed[:, None, :, : 3 * channels]
    first_ring = ring_pieces(first_pack, ring)
    up_lanes = packed[:, :, 3 * channels :]
    up_pack = jnp.stack(
        [up_lanes[:, :, i * channels : (i + 1) * channels] for i in range(hidden // width)]
        + [jnp.stack([w_out[:, :channels], w_out[:, channels:]])],
        axis=1,
    )

    vectors = jnp.stack(
        [skip_gain, skip_gain, skip_gain, skip_gain, norm1_gain, norm1_bias, norm2_gain, norm2_bias, down_bias]
    )
    misc = jnp.concatenate(
        [ssm_coef, ssm_rate, shift_taps, vectors.T], axis=1
    )
    bias_row = jnp.pad(up_bias, (0, 256 - up_rows)).reshape(1, 256)
    misc = jnp.pad(misc, ((0, 0), (0, 256 - misc.shape[1])))
    misc = jnp.pad(jnp.concatenate([misc, bias_row]), ((0, -(rows + 1) % 8), (0, 0)))
    misc_near = gather_quad(misc)
    misc_near, *first_ring = fence(misc_near, *first_ring)
    misc_all = gather_ring(misc_near, ring)
    params = misc_all[..., :rows, :].reshape(channels, 256)
    side = params[:, 2 * states :]
    params = params.T.astype(F32)
    taps = params[2 * states : 2 * states + tap_count]
    skip = params[2 * states + tap_count : 2 * states + tap_count + 1]
    side = ordered(
        side.reshape(groups, 2 * rows, -1), flip(side, "c").reshape(groups, 2 * rows, -1), core, 1
    )
    vec_all = side.reshape(width, -1).T.astype(F32)
    up_bias_own = misc_all[..., rows, :up_rows].astype(F32).reshape(1, hidden // 2)

    start = lax.axis_index("y") * block_len
    valid = start + lax.broadcasted_iota(jnp.int32, (block_len, 1), 0) < lengths[0]
    masked = jnp.where(valid, cotangent[0], jnp.zeros((), BF))
    masked, first_pack = fence(masked, first_pack)
    grad_half = swap_cy(masked)

    token_half = swap_cy(tokens[0])
    token_other = flip(token_half, "c")
    tables = dft_tables(length, first_pack)
    tables, first_ring = list(tables), list(first_ring)
    *tables, first_zero, first_half = fence(*tables, *first_ring)
    first_ring = (first_zero, first_half)
    first_one = near_one(first_ring)
    params, up_pack, token_other, grad_half, *first_one = fence(
        params, up_pack, token_other, grad_half, *first_one
    )
    first_two = near_two(first_ring, first_one)
    up_ring = ring_pieces(up_pack, ring)
    kern_re, kern_im = ssm_spectrum(params, states, tables[0], tables[1], length)
    kern_re, token_half = fence(kern_re, token_half)
    token_all, first_rows = first_norm(token_half, token_other, core, vec_all)
    first_rows, *first_two = fence(first_rows, *first_two)
    inputs = token_all.astype(F32)
    grad_all = ordered(grad_half, flip(grad_half, "c"), core, 0).reshape(length, width)
    w_qkv = assemble(
        first_ring, first_one, first_two, ring, ((ring, 2, 2, 2, rows, 3 * channels),), write_heads, "place_heads"
    )[0].reshape(width, 3 * channels)
    w_qkv, *up_ring = fence(w_qkv, *up_ring)
    up_one = near_one(up_ring)

    heads = mm(first_rows, w_qkv).astype(BF)
    heads, *up_one = fence(heads, *up_one)
    up_two = near_two(up_ring, up_one)
    mixed_heads, convolved, shifted, prod_re, prod_im = conv_forward(
        heads, kern_re, kern_im, params, 2 * states, tap_count, tables
    )
    mixed_heads, *up_two = fence(mixed_heads, *up_two)
    mixed_other = flip(mixed_heads, "c")
    up_own, out_own = assemble(
        up_ring,
        up_one,
        up_two,
        ring,
        ((ring, 2, 2, 2, rows, hidden // 2), (ring, 2, 2, rows, width)),
        write_up,
        "place_up",
    )
    up_own = up_own.reshape(width, hidden // 2)
    out_own = out_own.reshape(channels, width)
    out_other = flip(out_own, "c")
    residual = inputs + mm(mixed_heads, out_own) + mm(mixed_other, out_other)
    core_id = core.astype(jnp.int32).reshape(1)
    second_rows, activated, slope, down_theirs, mixed_mine = ffn_forward(
        core_id, residual, vec_all, up_own, up_bias_own, down_own
    )

    def mine(array):
        return lax.dynamic_slice_in_dim(array, core * block_len, block_len, 0)

    def theirs(array):
        return lax.dynamic_slice_in_dim(array, (1 - core) * block_len, block_len, 0)

    down_part = mm(activated, down_own)
    slope, down_theirs = fence(slope, down_theirs)
    down_other = flip(down_theirs, "c")
    pre_grad, up_bias_grad, second_theirs, second_mine = ffn_backward(core_id, grad_all, slope, up_own, down_own)
    second_theirs, down_other = fence(second_theirs, down_other)
    second_other = flip(second_theirs, "c")
    mixed = (mixed_mine + down_other.astype(F32)).astype(BF)
    residual_half = mine(residual)
    second_other, mixed = fence(second_other, mixed)
    mixed = swap_cy(mixed)[None]
    down_sum = mm_tn(activated, grad_all).astype(BF).reshape(ring, 2, 1, 2, -1, rows, width)
    up_sum = mm_tn(second_rows, pre_grad).astype(BF).reshape(ring, 2, 2, 2, 1, rows, hidden // 2)
    down_sum, up_sum = fence(down_sum, up_sum)

    ffn_one = pair_one(down_sum, up_sum)
    second_grad = second_mine + second_other.astype(F32)
    unit_two_h, scale_two_h = norm_stats(residual_half)
    grad_half_f = grad_half.astype(F32)
    gain_two_grad = jnp.sum(second_grad * unit_two_h, axis=0)
    bias_two_grad = jnp.sum(second_grad, axis=0)
    down_bias_grad = jnp.sum(grad_half_f, axis=0)
    resid_grad = grad_half_f + norm_back(second_grad, unit_two_h, scale_two_h, vec_all[10:11])
    mix_half = resid_grad.astype(BF)
    mix_grad = ordered(mix_half, flip(mix_half, "c"), core, 0).reshape(length, width)

    cos_t, sin_t = tables[0], tables[1]
    query_f, key_f, value_f = [
        heads[:, i * channels : (i + 1) * channels].astype(F32) for i in range(3)
    ]
    padded = jnp.pad(key_f, ((tap_count - 1, 0), (0, 0)))
    convolved, shifted = convolved.astype(F32), shifted.astype(F32)
    prod_re, prod_im, kern_re, kern_im = [
        array.astype(F32) for array in (prod_re, prod_im, kern_re, kern_im)
    ]
    products = shifted * value_f
    head_grad = mm_nt(mix_grad, out_own).astype(BF).astype(F32)
    query_grad = (head_grad * convolved).astype(BF)
    conv_grad = head_grad * query_f
    conv_low = conv_grad.astype(BF)
    skip_grad = jnp.sum(conv_grad * products, axis=0)
    grad_re = mm(cos_t, conv_low)
    grad_im = mm(sin_t, conv_low)
    out_grad = mm_tn(mixed_heads, mix_grad).astype(BF)
    q_grad = mm_tn(first_rows, query_grad).astype(BF)
    back_re = (grad_re * kern_re + grad_im * kern_im).astype(BF)
    back_im = (grad_im * kern_re - grad_re * kern_im).astype(BF)
    lag_re = (grad_re * prod_re + grad_im * prod_im).astype(BF)
    lag_im = (grad_im * prod_re - grad_re * prod_im).astype(BF)
    lag_grad = (mm_tn(lag_re, cos_t) + mm_tn(lag_im, sin_t)) * (1.0 / length)
    lag_sum = lag_grad.astype(BF).reshape(ring, 2, 1, 2, 1, rows, length)
    back = (mm_tn(cos_t, back_re) + mm_tn(sin_t, back_im)) * (1.0 / length)
    product_grad = back + skip * conv_grad
    out_sum = out_grad.reshape(ring, 2, 1, 2, 1, rows, width)
    q_sum = q_grad.reshape(ring, 2, 2, 2, 1, rows, channels)
    shifted_grad = product_grad * value_f
    value_grad = (product_grad * shifted).astype(BF)
    padded_grad = jnp.pad(shifted_grad, ((0, tap_count - 1), (0, 0)))
    key_grad = jnp.zeros_like(key_f)
    tap_rows = []
    for tap in range(tap_count):
        at = tap_count - 1 - tap
        key_grad = key_grad + padded_grad[tap : tap + length] * taps[tap : tap + 1]
        tap_rows.append(jnp.sum(shifted_grad * padded[at : at + length], axis=0))
    key_grad = key_grad.astype(BF)
    kv_grad = jnp.concatenate([key_grad, value_grad], axis=1)
    kv_sum = mm_tn(first_rows, kv_grad).astype(BF).reshape(ring, 2, 2, 2, 1, rows, 2 * channels)
    kv_sum, q_sum, out_sum, lag_sum, kv_grad, *ffn_one = fence(
        kv_sum, q_sum, out_sum, lag_sum, kv_grad, *ffn_one
    )

    lag_width = length // 8
    ffn_two = pair_two(down_sum, up_sum, ffn_one, ring)
    outq_one = direct_one((q_sum, out_sum, lag_sum), ring, lag_width)
    first_part = mm_nt(jnp.concatenate([query_grad, kv_grad], axis=1), w_qkv)
    first_other = flip(theirs(first_part).astype(BF), "c").astype(F32)
    first_grad = mine(first_part) + first_other
    unit_one_h, scale_one_h = norm_stats(token_half.astype(F32))
    gain_one_grad = jnp.sum(first_grad * unit_one_h, axis=0)
    bias_one_grad = jnp.sum(first_grad, axis=0)
    token_grad = resid_grad + norm_back(first_grad, unit_one_h, scale_one_h, vec_all[8:9])
    token_grad = token_grad.astype(BF)

    vec_grads = jnp.stack(
        [gain_one_grad, bias_one_grad, gain_two_grad, bias_two_grad, down_bias_grad]
    )
    vec_grads = vec_grads.reshape(5, groups, 2, 2 * rows)
    vec_keep = lax.dynamic_index_in_dim(vec_grads, core, 2, keepdims=False)
    vec_send = lax.dynamic_index_in_dim(vec_grads, 1 - core, 2, keepdims=False)
    vec_sum = (vec_keep + flip(vec_send, "c")).reshape(5, channels)
    small = jnp.concatenate([vec_sum, jnp.stack(tap_rows), skip_grad[None]])
    small = jnp.concatenate([small.T, up_bias_grad.reshape(channels, -1)], axis=1)
    small = jnp.pad(small, ((0, 0), (0, 128 - small.shape[1]))).astype(BF)
    small_sum = small.reshape(ring, 2, 1, 2, 1, rows, 128)
    small_sum, token_grad, *ffn_two = fence(small_sum, token_grad, *ffn_two)

    ffn_held = pair_three(down_sum, up_sum, ffn_one, ffn_two, ring, width)
    ffn_three = ring_send(ffn_held, ring)
    kv_one = direct_one((kv_sum, small_sum), ring, 128)
    token_grad = swap_cy(token_grad).astype(F32)[None]
    ffn_held, *outq_one = fence(ffn_held, *outq_one)
    outq_held = direct_two((q_sum, out_sum, lag_sum), outq_one, ring, lag_width)
    outq_three = ring_send(outq_held, ring)
    outq_held, *late = fence(outq_held, *kv_one, *ffn_three)
    kv_one, ffn_three = late[:3], late[3:]
    kv_held = direct_two((kv_sum, small_sum), kv_one, ring, 128)
    kv_three = ring_send(kv_held, ring)
    ffn_s = ring_sum(ffn_held, ffn_three)
    down_pieces = up_rows // rows
    down_s = ffn_s[:down_pieces].reshape(up_rows, width)
    up_half = (ffn_s.shape[0] - down_pieces) // 2
    up_s = jnp.stack([join(ffn_s[down_pieces : down_pieces + up_half]), join(ffn_s[down_pieces + up_half :])])
    up_s = merge_columns(up_s, core, groups)
    outq_s = ring_sum(outq_held, outq_three)
    q_pieces = channels // lag_width
    query_s = merge_columns(
        jnp.stack([join(outq_s[:q_pieces]), join(outq_s[q_pieces : 2 * q_pieces])]), core, groups
    )
    out_s = join(outq_s[2 * q_pieces : 4 * q_pieces])
    lag_s = join(outq_s[4 * q_pieces :])
    up_s, down_s, query_s, out_s, lag_s, *kv_three = fence(up_s, down_s, query_s, out_s, lag_s, *kv_three)
    coef_s, rate_s = ssm_kernel_grads(lag_s, ssm_coef.astype(F32), ssm_rate.astype(F32))
    kv_s = ring_sum(kv_held, kv_three)
    pieces = channels // 128
    key_s = merge_columns(
        jnp.stack([join(kv_s[:pieces]), join(kv_s[2 * pieces : 3 * pieces])]), core, groups
    )
    value_s = merge_columns(
        jnp.stack([join(kv_s[pieces : 2 * pieces]), join(kv_s[3 * pieces : 4 * pieces])]), core, groups
    )
    small = kv_s[4 * pieces]
    vec_s = small[:, :5].T
    taps_s = small[:, 5 : 5 + tap_count]
    skip_s = small[:, 5 + tap_count]
    up_bias_s = small[:, 6 + tap_count : 6 + tap_count + up_rows // rows].reshape(up_rows)
    return (
        mixed,
        token_grad,
        vec_s[0],
        vec_s[1],
        query_s,
        key_s,
        value_s,
        taps_s,
        coef_s,
        rate_s,
        skip_s,
        out_s,
        vec_s[2],
        vec_s[3],
        up_s,
        up_bias_s,
        down_s,
        vec_s[4],
    )


def solution(mesh):
    dp_size, seq_size = mesh.devices.shape
    ring = dp_size // 4
    grid = Mesh(mesh.devices.reshape(ring, 2, 2, seq_size), ("r", "x", "c", "y"))
    dp = ("r", "x", "c")
    act = P(dp, "y", None)
    vec = P(dp + ("y",))
    mat = P(dp + ("y",), None)
    return jax.shard_map(
        functools.partial(body, ring),
        mesh=grid,
        in_specs=(
            act, P(dp), act, vec, vec, mat, mat, mat, mat, mat, mat, vec, mat, vec, vec, mat, vec, mat, vec,
        ),
        out_specs=(
            act, act, vec, vec, mat, mat, mat, mat, mat, mat, vec, mat, vec, vec, mat, vec, mat, vec,
        ),
        check_vma=False,
    )
```

```python
import functools
import math

import jax
import jax.numpy as jnp
from jax import lax
from jax.experimental import pallas as pl
from jax.experimental.pallas import tpu as pltpu
from jax.sharding import Mesh, PartitionSpec as P

EPS = 1e-05
BF = jnp.bfloat16
F32 = jnp.float32
SQRT_2_PI = math.sqrt(2.0 / math.pi)
MISC = ("r", "x", "y")


def flip(value, axis):
    return lax.ppermute(value, axis, [(0, 1), (1, 0)])


def ordered(mine, other, place, axis):
    first = jnp.where(place == 0, mine, other)
    second = jnp.where(place == 0, other, mine)
    return jnp.stack([first, second], axis=axis)


def swap_cy(value):
    moved = lax.ppermute(value, ("c", "y"), [(1, 2), (2, 1)])
    return jnp.where(lax.axis_index("c") == lax.axis_index("y"), value, moved)


def shift_ring(value, distance, ring):
    return lax.ppermute(value, "r", [(i, (i + distance) % ring) for i in range(ring)])


def flip_xy(value):
    return lax.ppermute(value, ("x", "y"), [(i, 3 - i) for i in range(4)])


def place(whole, part, starts):
    return lax.dynamic_update_slice(whole, part, starts)


def gather_ring(block, ring):
    here = lax.axis_index("r")
    rest = (0,) * block.ndim
    whole = jnp.zeros((ring,) + block.shape, block.dtype)
    whole = place(whole, block[None], (here,) + rest)
    for distance in range(1, ring):
        moved = shift_ring(block, distance, ring)
        whole = place(whole, moved[None], (lax.rem(here - distance + ring, ring),) + rest)
    return whole


def ring_pieces(block, ring):
    blocks = [block] + [shift_ring(block, d, ring) for d in range(1, ring)]
    return tuple(jnp.stack([part[half] for part in blocks]) for half in range(2))


def near_one(halves):
    return flip(halves[0], "y"), flip(halves[1], "x")


def near_two(halves, moved):
    first = flip(jnp.concatenate([halves[0], moved[0]]), "x")
    second = flip(jnp.concatenate([halves[1], moved[1]]), "y")
    return first, second


def chip_ids():
    return jnp.stack([lax.axis_index("r"), lax.axis_index("x"), lax.axis_index("y")]).astype(jnp.int32)


def grant(*blocks):
    total = 0
    for shape, kind in blocks:
        rows = -(-shape[-2] // 16) * 16
        total += math.prod(shape[:-2]) * rows * shape[-1] * jnp.dtype(kind).itemsize
    return pltpu.CompilerParams(vmem_limit_bytes=2 * total + (2 << 20))


def assemble_body(write, ids, *refs):
    ins, outs = refs[:8], refs[8:]
    for half in range(2):
        for index in range(4):
            x = lax.rem(ids[1] + index // 2, 2)
            y = lax.rem(ids[2] + index % 2, 2)
            write(outs, ins[4 * half + index], half, x, y)


def assemble(halves, one, two, ring, shapes, write, name):
    sources = (
        (halves[0], 0), (one[0], 0), (two[0], 0), (two[0], ring),
        (halves[1], 0), (two[1], 0), (one[1], 0), (two[1], ring),
    )
    tail = halves[0].shape[1:]
    zeros = (0,) * len(tail)
    specs = [
        pl.BlockSpec((None,) + tail, lambda i, ids, base=base: (i + base,) + zeros) for _, base in sources
    ]
    moved = 32 * math.prod(tail) * ring
    return pl.pallas_call(
        functools.partial(assemble_body, write),
        out_shape=tuple(jax.ShapeDtypeStruct(shape, halves[0].dtype) for shape in shapes),
        grid_spec=pltpu.PrefetchScalarGridSpec(
            num_scalar_prefetch=1,
            grid=(ring,),
            in_specs=specs,
            out_specs=tuple(
                pl.BlockSpec(
                    (None,) + shape[1:],
                    lambda i, ids, rank=len(shape): (lax.rem(ids[0] + ring - i, ring),) + (0,) * (rank - 1),
                )
                for shape in shapes
            ),
        ),
        compiler_params=grant(*[(tail, BF)] * 8, *[(shape[1:], BF) for shape in shapes]),
        cost_estimate=pl.CostEstimate(flops=0, bytes_accessed=moved, transcendentals=0),
        name=name,
    )(chip_ids(), *[array for array, _ in sources])


def write_heads(outs, part, half, x, y):
    outs[0][x, half, y] = part[0]


def write_up(outs, part, half, x, y):
    lanes = part.shape[-1]
    count = part.shape[0] - 1
    for index in range(count):
        outs[0][x, half, y, :, index * lanes : (index + 1) * lanes] = part[index]
    outs[1][x, y, :, half * lanes : (half + 1) * lanes] = part[count]


def here_x(i, ids):
    return ids[1]


def other_x(i, ids):
    return 1 - ids[1]


def here_y(i, ids):
    return ids[2]


def other_y(i, ids):
    return 1 - ids[2]


def step_r(i, ids):
    return i


def turn_r(ring):
    return lambda i, ids: lax.rem(ids[0] + i, ring)


def sums_body(plan, ids, *refs):
    ins, outs = refs[: len(refs) - len(plan)], refs[len(refs) - len(plan) :]
    for out, columns in zip(outs, plan):
        width = out.shape[2]
        at = 0
        for terms in columns:
            first = ins[terms[0]]
            cores, extra, _, lanes = first.shape
            index = 0
            for core in range(cores):
                for more in range(extra):
                    for low in range(0, lanes, width):
                        total = None
                        for term in terms:
                            ref = ins[term]
                            if len(ref.shape) == 4:
                                value = ref[core, more, :, low : low + width]
                            else:
                                value = ref[at + index]
                            value = value.astype(F32)
                            total = value if total is None else total + value
                        out[at + index] = total.astype(out.dtype)
                        index += 1
            at += index


def sums(ring, jobs):
    arrays, specs, plan, shapes = [], [], [], []
    for width, columns in jobs:
        pieces = 0
        numbers = []
        for terms in columns:
            mine = []
            for count, (array, picks) in enumerate(terms):
                tail = array.shape[len(picks) :]
                block = tuple(
                    size if pick is None else None for size, pick in zip(array.shape, picks)
                ) + tail

                def index_map(i, ids, picks=picks, tail=tail):
                    return tuple(0 if pick is None else pick(i, ids) for pick in picks) + (0,) * len(tail)

                if count == 0:
                    held = [size for size in block if size is not None]
                    pieces += held[0] * held[1] * (held[3] // width)
                mine.append(len(arrays))
                arrays.append(array)
                specs.append(pl.BlockSpec(block, index_map))
            numbers.append(mine)
        plan.append(numbers)
        rows = columns[0][0][0].shape[-2]
        shapes.append(jax.ShapeDtypeStruct((ring, pieces, rows, width), BF))
    moved = sum(2 * math.prod(shape.shape) * 2 for shape in shapes)
    return pl.pallas_call(
        functools.partial(sums_body, plan),
        out_shape=tuple(shapes),
        grid_spec=pltpu.PrefetchScalarGridSpec(
            num_scalar_prefetch=1,
            grid=(ring,),
            in_specs=specs,
            out_specs=tuple(
                pl.BlockSpec((None,) + shape.shape[1:], lambda i, ids: (i, 0, 0, 0)) for shape in shapes
            ),
        ),
        compiler_params=grant(
            *[
                (tuple(size for size in spec.block_shape if size is not None), BF)
                for spec in specs
            ],
            *[(shape.shape[1:], BF) for shape in shapes],
        ),
        cost_estimate=pl.CostEstimate(flops=0, bytes_accessed=2 * moved, transcendentals=0),
        name="sums",
    )(chip_ids(), *[pltpu.with_memory_space_constraint(array, pltpu.HBM) for array in arrays])


def take(parts, axis, index):
    return lax.dynamic_index_in_dim(parts, index, axis, keepdims=False)


def pair_one(y_first, x_first):
    x, y = lax.axis_index("x"), lax.axis_index("y")
    return flip(take(y_first, 3, 1 - y), "y"), flip(take(x_first, 1, 1 - x), "x")


def pair_two(y_first, x_first, moved, ring):
    one = [
        (y_first, (step_r, other_x, None, here_y)),
        (moved[0], (step_r, other_x, None)),
    ]
    two = [
        (x_first, (step_r, here_x, None, other_y)),
        (moved[1], (step_r, None, other_y)),
    ]
    send_one, send_two = sums(ring, [(y_first.shape[-1], [one]), (x_first.shape[-1], [two])])
    shape_one = (ring, y_first.shape[2]) + y_first.shape[4:]
    shape_two = (ring, x_first.shape[2]) + x_first.shape[4:]
    return flip(send_one, "x").reshape(shape_one), flip(send_two, "y").reshape(shape_two)


def pair_three(y_first, x_first, moved_one, moved_two, ring, width):
    turn = turn_r(ring)
    one = [
        (y_first, (turn, here_x, None, here_y)),
        (moved_one[0], (turn, here_x, None)),
        (moved_two[0], (turn, None)),
    ]
    two = [
        (x_first, (turn, here_x, None, here_y)),
        (moved_one[1], (turn, None, here_y)),
        (moved_two[1], (turn, None)),
    ]
    return sums(ring, [(width, [one, two])])[0]


def direct_one(arrays, ring, width):
    spots = ((here_x, other_y), (other_x, here_y), (other_x, other_y))
    along_y, along_x, across = sums(
        ring, [(width, [[(array, (step_r, x, None, y))] for array in arrays]) for x, y in spots]
    )
    return flip(along_y, "y"), flip(along_x, "x"), flip_xy(across)


def direct_two(arrays, moved, ring, width):
    turn = turn_r(ring)
    columns = [
        [(array, (turn, here_x, None, here_y))] + [(part, (turn,)) for part in moved] for array in arrays
    ]
    return sums(ring, [(width, columns)])[0]


def ring_send(held, ring):
    return tuple(shift_ring(held[distance], distance, ring) for distance in range(1, ring))


def ring_sum(held, moved):
    total = held[0].astype(F32)
    for part in moved:
        total = total + part.astype(F32)
    return total


def join(pieces):
    return jnp.concatenate([pieces[i] for i in range(pieces.shape[0])], axis=1)


def scatter_near(pick):
    x, y = lax.axis_index("x"), lax.axis_index("y")
    total = pick(x, y).astype(F32)
    total = total + flip(pick(x, 1 - y), "y").astype(F32)
    total = total + flip(pick(1 - x, y), "x").astype(F32)
    return total + flip_xy(pick(1 - x, 1 - y)).astype(F32)


def gather_quad(block):
    x, y = lax.axis_index("x"), lax.axis_index("y")
    parts = ((block, x, y), (flip(block, "y"), x, 1 - y), (flip(block, "x"), 1 - x, y), (flip_xy(block), 1 - x, 1 - y))
    full = jnp.zeros((2, 2) + block.shape, block.dtype)
    for part, at_x, at_y in parts:
        full = place(full, part[None, None], (at_x, at_y) + (0,) * block.ndim)
    return full


def fence(*values):
    return lax.optimization_barrier(values)


def merge_columns(parts, core, groups):
    keep = lax.dynamic_index_in_dim(parts, core, 0, keepdims=False)
    send = lax.dynamic_index_in_dim(parts, 1 - core, 0, keepdims=False)
    count, cols = keep.shape
    other = flip(send.astype(BF), "c").astype(F32)
    grid = ordered(
        keep.reshape(count, groups, -1), other.reshape(count, groups, -1), core, 2
    )
    return grid.reshape(count, 2 * cols)


def mm(left, right):
    return jnp.dot(left, right, preferred_element_type=F32)


def mm_tn(left, right):
    return lax.dot_general(
        left, right, (((0,), (0,)), ((), ())), preferred_element_type=F32
    )


def mm_nt(left, right):
    return lax.dot_general(
        left, right, (((1,), (1,)), ((), ())), preferred_element_type=F32
    )


def norm_stats(values):
    mean = jnp.mean(values, axis=-1, keepdims=True)
    centred = values - mean
    variance = jnp.mean(centred * centred, axis=-1, keepdims=True)
    scale = lax.rsqrt(variance + EPS)
    return centred * scale, scale


def norm_back(grad, unit, scale, gain):
    inner = grad * gain
    mean_one = jnp.mean(inner, axis=-1, keepdims=True)
    mean_two = jnp.mean(inner * unit, axis=-1, keepdims=True)
    return scale * (inner - mean_one - unit * mean_two)


def tables_body(token_ref, cos_ref, sin_ref, cos_turn_ref, sin_turn_ref, cos_high_ref, sin_high_ref):
    length = cos_ref.shape[0]
    part = 32
    blocks = length // part
    step = math.pi / (2.0 * length)
    period = 4 * length
    rows = lax.broadcasted_iota(jnp.int32, (part, length), 0)
    cols = lax.broadcasted_iota(jnp.int32, (part, length), 1)

    def turns(count):
        angle = (count & (period - 1)).astype(F32) * step
        return jnp.cos(angle), jnp.sin(angle)

    def fill(high, low, cos_out, sin_out):
        cos_high_ref[...], sin_high_ref[...] = turns(high)
        cos_low, sin_low = turns(low)

        def put(block, carry):
            ch, sh = cos_high_ref[pl.ds(block, 1), :], sin_high_ref[pl.ds(block, 1), :]
            at = pl.ds(pl.multiple_of(block * part, part), part)
            cos_out[at, :] = (ch * cos_low - sh * sin_low).astype(BF)
            sin_out[at, :] = (sh * cos_low + ch * sin_low).astype(BF)
            return carry

        lax.fori_loop(0, blocks, put, 0)

    fill(2 * part * rows * cols, (2 * rows + 1) * cols, cos_ref, sin_ref)
    fill(part * rows * (2 * cols + 1), rows * (2 * cols + 1), cos_turn_ref, sin_turn_ref)


def dft_tables(length, token):
    table = jax.ShapeDtypeStruct((length, length), BF)
    return pl.pallas_call(
        tables_body,
        out_shape=(table,) * 4,
        in_specs=[pl.BlockSpec(memory_space=pl.ANY)],
        out_specs=tuple(in_vmem(4)),
        scratch_shapes=[pltpu.VMEM((32, length), F32)] * 2,
        cost_estimate=pl.CostEstimate(flops=7 * 10**9, bytes_accessed=8 * length * length, transcendentals=0),
        compiler_params=pltpu.CompilerParams(vmem_limit_bytes=4 << 20),
        name="dft_tables",
    )(token)


def norm_body(core_ref, mine_ref, other_ref, vec_ref, all_ref, rows_ref):
    half = mine_ref.shape[0]
    step = 128
    for index, ref in enumerate((mine_ref, other_ref)):
        place = lax.rem(core_ref[0] + index, 2) * half

        def put(block_id, carry):
            block = ref[pl.ds(pl.multiple_of(block_id * step, step), step), :]
            at = pl.ds(pl.multiple_of(place + block_id * step, step), step)
            all_ref[at, :] = block
            unit, _ = norm_stats(block.astype(F32))
            rows_ref[at, :] = (unit * vec_ref[8:9, :] + vec_ref[9:10, :]).astype(BF)
            return carry

        lax.fori_loop(0, half // step, put, 0)


def first_norm(mine, other, core, vectors):
    half, width = mine.shape
    wide = jax.ShapeDtypeStruct((2 * half, width), BF)
    return pl.pallas_call(
        norm_body,
        out_shape=(wide, wide),
        in_specs=[pl.BlockSpec(memory_space=pltpu.SMEM)] + in_vmem(3),
        out_specs=tuple(in_vmem(2)),
        cost_estimate=pl.CostEstimate(flops=3 * 10**9, bytes_accessed=4 * half * width, transcendentals=0),
        compiler_params=pltpu.CompilerParams(vmem_limit_bytes=4 << 20),
        name="first_norm",
    )(core.astype(jnp.int32).reshape(1), mine, other, vectors)


def in_vmem(count):
    return [pl.BlockSpec(memory_space=pltpu.VMEM)] * count


def kernel_body(part, coef_ref, rate_ref, out_ref, high_ref, low_ref):
    states = coef_ref.shape[0]
    length = out_ref.shape[0]
    blocks = length // part
    lanes = out_ref.shape[1]
    high_ids = lax.broadcasted_iota(jnp.int32, (blocks, lanes), 0).astype(F32) * (part / length)
    low_ids = lax.broadcasted_iota(jnp.int32, (part, lanes), 0).astype(F32) * (1.0 / length)

    def fill(state, carry):
        rate = rate_ref[pl.ds(state, 1), :]
        coef = coef_ref[pl.ds(state, 1), :] * (length ** (-0.5))
        high_ref[state] = coef * jnp.exp(-rate * high_ids)
        low_ref[state] = jnp.exp(-rate * low_ids)
        return carry

    lax.fori_loop(0, states, fill, 0)
    for start in range(0, blocks, 8):

        def add(state, sums):
            low = low_ref[state]
            return tuple(
                total + high_ref[state, pl.ds(start + index, 1), :] * low
                for index, total in enumerate(sums)
            )

        zero = jnp.zeros((part, lanes), F32)
        sums = lax.fori_loop(0, states, add, (zero,) * 8, unroll=4)
        for index, total in enumerate(sums):
            out_ref[pl.ds((start + index) * part, part), :] = total.astype(out_ref.dtype)


def spectrum_body(part, states, params_ref, cos_ref, sin_ref, re_ref, im_ref, kernel_ref, high_ref, low_ref, coef_part, rate_part):
    length, channels = kernel_ref.shape
    for start in range(0, channels, 128):
        lanes = pl.ds(start, 128)
        coef_part[...] = params_ref[0:states, lanes]
        rate_part[...] = params_ref[states : 2 * states, lanes]
        kernel_body(part, coef_part, rate_part, kernel_ref.at[:, lanes], high_ref, low_ref)

    def put(block, carry):
        rows = pl.ds(pl.multiple_of(block * 256, 256), 256)
        re_ref[rows, :] = mm(cos_ref[rows, :], kernel_ref[...]).astype(BF)
        im_ref[rows, :] = mm(sin_ref[rows, :], kernel_ref[...]).astype(BF)
        return carry

    lax.fori_loop(0, length // 256, put, 0)


def ssm_spectrum(params, states, cos_t, sin_t, length):
    channels = params.shape[1]
    part = 32
    return pl.pallas_call(
        functools.partial(spectrum_body, part, states),
        out_shape=(jax.ShapeDtypeStruct((length, channels), BF),) * 2,
        in_specs=in_vmem(3),
        out_specs=tuple(in_vmem(2)),
        scratch_shapes=[
            pltpu.VMEM((length, channels), BF),
            pltpu.VMEM((states, length // part, 128), F32),
            pltpu.VMEM((states, part, 128), F32),
            pltpu.VMEM((states, 128), F32),
            pltpu.VMEM((states, 128), F32),
        ],
        cost_estimate=pl.CostEstimate(
            flops=600 * length * states * channels, bytes_accessed=2 * length * channels * 4, transcendentals=0
        ),
        compiler_params=pltpu.CompilerParams(vmem_limit_bytes=8 << 20),
        name="ssm_spectrum",
    )(params, cos_t, sin_t)


def conv_body(
    first, tap_count, heads_ref, kern_re_ref, kern_im_ref, params_ref, cos_ref, sin_ref, cos_turn_ref, sin_turn_ref,
    mixed_ref, conv_ref, shifted_ref, prod_re_ref, prod_im_ref,
    products_ref, low_ref, spec_re_ref, spec_im_ref,
):
    length, channels = mixed_ref.shape
    step = 128
    last = first + tap_count

    def shift(rows, keys):
        shifted = keys[8:] * params_ref[first : first + 1, :]
        for tap in range(1, tap_count):
            shifted = shifted + keys[8 - tap : 8 - tap + step] * params_ref[first + tap : first + tap + 1, :]
        shifted_ref[rows, :] = shifted.astype(BF)
        products = shifted * heads_ref[rows, 2 * channels : 3 * channels].astype(F32)
        products_ref[rows, :] = products
        low_ref[rows, :] = products.astype(BF)

    keys = heads_ref[0:step, channels : 2 * channels].astype(F32)
    shift(pl.ds(0, step), jnp.concatenate([jnp.zeros((8, channels), F32), keys], axis=0))

    def shift_block(block, carry):
        before = pl.ds(pl.multiple_of(block * step - 8, 8), step + 8)
        shift(
            pl.ds(pl.multiple_of(block * step, step), step),
            heads_ref[before, channels : 2 * channels].astype(F32),
        )
        return carry

    lax.fori_loop(1, length // step, shift_block, 0)

    def spectrum(block, carry):
        rows = pl.ds(pl.multiple_of(block * 256, 256), 256)
        prod_re = mm(cos_ref[rows, :], low_ref[...])
        prod_im = mm(sin_ref[rows, :], low_ref[...])
        kern_re, kern_im = kern_re_ref[rows, :].astype(F32), kern_im_ref[rows, :].astype(F32)
        prod_re_ref[rows, :] = prod_re.astype(BF)
        prod_im_ref[rows, :] = prod_im.astype(BF)
        spec_re_ref[rows, :] = (prod_re * kern_re - prod_im * kern_im).astype(BF)
        spec_im_ref[rows, :] = (prod_re * kern_im + prod_im * kern_re).astype(BF)
        return carry

    lax.fori_loop(0, length // 256, spectrum, 0)

    def convolve(block, carry):
        rows = pl.ds(pl.multiple_of(block * 256, 256), 256)
        conv = mm(cos_turn_ref[rows, :], spec_re_ref[...]) + mm(sin_turn_ref[rows, :], spec_im_ref[...])
        conv = conv * (1.0 / length) + params_ref[last : last + 1, :] * products_ref[rows, :]
        conv_ref[rows, :] = conv.astype(BF)
        mixed_ref[rows, :] = (heads_ref[rows, 0:channels].astype(F32) * conv).astype(BF)
        return carry

    lax.fori_loop(0, length // 256, convolve, 0)


def conv_forward(heads, kern_re, kern_im, params, first, tap_count, tables):
    length, channels = kern_re.shape
    wide = jax.ShapeDtypeStruct((length, channels), BF)
    return pl.pallas_call(
        functools.partial(conv_body, first, tap_count),
        out_shape=(wide,) * 5,
        in_specs=in_vmem(8),
        out_specs=tuple(in_vmem(5)),
        scratch_shapes=[
            pltpu.VMEM((length, channels), F32),
            pltpu.VMEM((length, channels), BF),
            pltpu.VMEM((length, channels), BF),
            pltpu.VMEM((length, channels), BF),
        ],
        cost_estimate=pl.CostEstimate(
            flops=24 * length * length * channels, bytes_accessed=16 * length * channels, transcendentals=0
        ),
        compiler_params=pltpu.CompilerParams(vmem_limit_bytes=10 << 20),
        name="conv_forward",
    )(heads, kern_re, kern_im, params, *tables)


def ssm_kernel_grads(grad, coef, rate):
    length = grad.shape[1]
    times = lax.broadcasted_iota(jnp.int32, (1, 1, length), 2).astype(F32) * (1.0 / length)
    weighted = grad[:, None] * jnp.exp(-rate[:, :, None] * times)
    scale = length ** (-0.5)
    return jnp.sum(weighted, axis=2) * scale, -coef * jnp.sum(weighted * times, axis=2) * scale


def row_block(cols, kind_rows=256):
    return pl.BlockSpec((kind_rows, cols), lambda i: (i, 0))


def whole_block(rows, cols):
    return pl.BlockSpec((rows, cols), lambda i: (0, 0), pipeline_mode=pl.Buffered(1))


def turned_block(cols, steps):
    return pl.BlockSpec((256, cols), lambda i, core: (lax.rem(i + steps // 2 * (1 - core[0]), steps), 0))


def same_block(rows, cols):
    return pl.BlockSpec((rows, cols), lambda i, core: (0, 0), pipeline_mode=pl.Buffered(1))


def half_blocks(cols, steps):
    theirs = pl.BlockSpec((256, cols), lambda i, core: (jnp.minimum(i, steps // 2 - 1), 0))
    mine = pl.BlockSpec((256, cols), lambda i, core: (jnp.maximum(i - steps // 2, 0), 0))
    return theirs, mine


def put_half(theirs_ref, mine_ref, theirs, mine):
    first = pl.program_id(0) < pl.num_programs(0) // 2

    @pl.when(first)
    def _():
        theirs_ref[...] = theirs.astype(theirs_ref.dtype)

    @pl.when(jnp.logical_not(first))
    def _():
        mine_ref[...] = mine.astype(mine_ref.dtype)


def ffn_forward_body(
    core_ref, resid_ref, vec_ref, up_ref, up_bias_ref, down_ref,
    rows_ref, act_ref, slope_ref, theirs_ref, mine_ref,
):
    resid = resid_ref[...]
    unit, _ = norm_stats(resid)
    second = (unit * vec_ref[10:11, :] + vec_ref[11:12, :]).astype(BF)
    rows_ref[...] = second
    pre = mm(second, up_ref[...]) + up_bias_ref[...]
    square = pre * pre
    bend = jnp.tanh(pre * (SQRT_2_PI + SQRT_2_PI * 0.044715 * square))
    half = 0.5 * pre
    act = (half + half * bend).astype(BF)
    act_ref[...] = act
    steep = SQRT_2_PI + 3.0 * SQRT_2_PI * 0.044715 * square
    slope_ref[...] = (0.5 + 0.5 * bend + half * (1.0 - bend * bend) * steep).astype(BF)
    part = mm(act, down_ref[...])
    put_half(theirs_ref, mine_ref, part, part + resid + vec_ref[12:13, :])


def ffn_forward(core, resid, vectors, up, up_bias, down):
    length, width = resid.shape
    hidden = up.shape[1]
    steps = length // 256
    return pl.pallas_call(
        ffn_forward_body,
        out_shape=(
            jax.ShapeDtypeStruct((length, width), BF),
            jax.ShapeDtypeStruct((length, hidden), BF),
            jax.ShapeDtypeStruct((length, hidden), BF),
            jax.ShapeDtypeStruct((length // 2, width), BF),
            jax.ShapeDtypeStruct((length // 2, width), F32),
        ),
        grid_spec=pltpu.PrefetchScalarGridSpec(
            num_scalar_prefetch=1,
            grid=(steps,),
            in_specs=[
                turned_block(width, steps),
                same_block(vectors.shape[0], width),
                same_block(width, hidden),
                same_block(1, hidden),
                same_block(hidden, width),
            ],
            out_specs=(
                turned_block(width, steps),
                turned_block(hidden, steps),
                turned_block(hidden, steps),
            )
            + half_blocks(width, steps),
        ),
        compiler_params=pltpu.CompilerParams(vmem_limit_bytes=28 << 20),
        cost_estimate=pl.CostEstimate(
            flops=8 * length * width * hidden, bytes_accessed=12 * length * width, transcendentals=0
        ),
        name="ffn_forward",
    )(core, resid, vectors, up, up_bias, down)


def ffn_backward_body(core_ref, grad_ref, slope_ref, up_ref, down_ref, pre_ref, bias_ref, theirs_ref, mine_ref):
    act_grad = mm_nt(grad_ref[...], down_ref[...])
    pre = (act_grad * slope_ref[...].astype(F32)).astype(BF)
    pre_ref[...] = pre
    part = mm_nt(pre, up_ref[...])
    put_half(theirs_ref, mine_ref, part, part)

    @pl.when(pl.program_id(0) == 0)
    def _():
        bias_ref[...] = jnp.zeros_like(bias_ref)

    bias_ref[...] += jnp.sum(pre.astype(F32), axis=0, keepdims=True)


def ffn_backward(core, grad, slope, up, down):
    length, width = grad.shape
    hidden = up.shape[1]
    steps = length // 256
    return pl.pallas_call(
        ffn_backward_body,
        out_shape=(
            jax.ShapeDtypeStruct((length, hidden), BF),
            jax.ShapeDtypeStruct((1, hidden), F32),
            jax.ShapeDtypeStruct((length // 2, width), BF),
            jax.ShapeDtypeStruct((length // 2, width), F32),
        ),
        grid_spec=pltpu.PrefetchScalarGridSpec(
            num_scalar_prefetch=1,
            grid=(steps,),
            in_specs=[
                turned_block(width, steps),
                turned_block(hidden, steps),
                same_block(width, hidden),
                same_block(hidden, width),
            ],
            out_specs=(turned_block(hidden, steps), pl.BlockSpec((1, hidden), lambda i, core: (0, 0)))
            + half_blocks(width, steps),
        ),
        compiler_params=pltpu.CompilerParams(vmem_limit_bytes=24 << 20),
        cost_estimate=pl.CostEstimate(
            flops=6 * length * width * hidden, bytes_accessed=12 * length * width, transcendentals=0
        ),
        name="ffn_backward",
    )(core, grad, slope, up, down)


def body(
    ring,
    tokens,
    lengths,
    cotangent,
    norm1_gain,
    norm1_bias,
    w_query,
    w_key,
    w_value,
    shift_taps,
    ssm_coef,
    ssm_rate,
    skip_gain,
    w_out,
    norm2_gain,
    norm2_bias,
    w_up,
    up_bias,
    w_down,
    down_bias,
):
    core = lax.axis_index("c")
    groups = 2 * ring
    _, block_len, width = tokens.shape
    length = 2 * block_len
    rows = w_query.shape[0]
    up_rows = up_bias.shape[0]
    hidden = w_up.shape[1]
    states = ssm_coef.shape[1]
    tap_count = shift_taps.shape[1]
    channels = width // 2

    def columns(weight, which):
        grid = weight.reshape(rows, groups, 2, -1)
        return jnp.where(which == 0, grid[:, :, 0], grid[:, :, 1]).reshape(rows, -1)

    down_own = lax.all_gather(w_down, MISC, axis=0, tiled=True)
    matrices = (w_query, w_key, w_value, w_up)
    keep = jnp.concatenate([columns(w, core) for w in matrices], axis=1)
    send = jnp.concatenate([columns(w, 1 - core) for w in matrices], axis=1)
    norm1_gain, ssm_coef, ssm_rate, send = fence(norm1_gain, ssm_coef, ssm_rate, send)
    packed = ordered(keep, flip(send, "c"), core, 0)
    first_pack = packed[:, None, :, : 3 * channels]
    first_ring = ring_pieces(first_pack, ring)
    up_lanes = packed[:, :, 3 * channels :]
    up_pack = jnp.stack(
        [up_lanes[:, :, i * channels : (i + 1) * channels] for i in range(hidden // width)]
        + [jnp.stack([w_out[:, :channels], w_out[:, channels:]])],
        axis=1,
    )

    vectors = jnp.stack(
        [skip_gain, skip_gain, skip_gain, skip_gain, norm1_gain, norm1_bias, norm2_gain, norm2_bias, down_bias]
    )
    misc = jnp.concatenate(
        [ssm_coef, ssm_rate, shift_taps, vectors.T], axis=1
    )
    bias_row = jnp.pad(up_bias, (0, 256 - up_rows)).reshape(1, 256)
    misc = jnp.pad(misc, ((0, 0), (0, 256 - misc.shape[1])))
    misc = jnp.pad(jnp.concatenate([misc, bias_row]), ((0, -(rows + 1) % 8), (0, 0)))
    misc_near = gather_quad(misc)
    misc_near, *first_ring = fence(misc_near, *first_ring)
    misc_all = gather_ring(misc_near, ring)
    params = misc_all[..., :rows, :].reshape(channels, 256)
    side = params[:, 2 * states :]
    params = params.T.astype(F32)
    taps = params[2 * states : 2 * states + tap_count]
    skip = params[2 * states + tap_count : 2 * states + tap_count + 1]
    side = ordered(
        side.reshape(groups, 2 * rows, -1), flip(side, "c").reshape(groups, 2 * rows, -1), core, 1
    )
    vec_all = side.reshape(width, -1).T.astype(F32)
    up_bias_own = misc_all[..., rows, :up_rows].astype(F32).reshape(1, hidden // 2)

    start = lax.axis_index("y") * block_len
    valid = start + lax.broadcasted_iota(jnp.int32, (block_len, 1), 0) < lengths[0]
    masked = jnp.where(valid, cotangent[0], jnp.zeros((), BF))
    masked, first_pack = fence(masked, first_pack)
    grad_half = swap_cy(masked)

    token_half = swap_cy(tokens[0])
    token_other = flip(token_half, "c")
    tables = dft_tables(length, first_pack)
    tables, first_ring = list(tables), list(first_ring)
    *tables, first_zero, first_half = fence(*tables, *first_ring)
    first_ring = (first_zero, first_half)
    first_one = near_one(first_ring)
    params, up_pack, token_other, grad_half, *first_one = fence(
        params, up_pack, token_other, grad_half, *first_one
    )
    first_two = near_two(first_ring, first_one)
    up_ring = ring_pieces(up_pack, ring)
    kern_re, kern_im = ssm_spectrum(params, states, tables[0], tables[1], length)
    kern_re, token_half = fence(kern_re, token_half)
    token_all, first_rows = first_norm(token_half, token_other, core, vec_all)
    first_rows, *first_two = fence(first_rows, *first_two)
    inputs = token_all.astype(F32)
    grad_all = ordered(grad_half, flip(grad_half, "c"), core, 0).reshape(length, width)
    w_qkv = assemble(
        first_ring, first_one, first_two, ring, ((ring, 2, 2, 2, rows, 3 * channels),), write_heads, "place_heads"
    )[0].reshape(width, 3 * channels)
    w_qkv, *up_ring = fence(w_qkv, *up_ring)
    up_one = near_one(up_ring)

    heads = mm(first_rows, w_qkv).astype(BF)
    heads, *up_one = fence(heads, *up_one)
    up_two = near_two(up_ring, up_one)
    mixed_heads, convolved, shifted, prod_re, prod_im = conv_forward(
        heads, kern_re, kern_im, params, 2 * states, tap_count, tables
    )
    mixed_heads, *up_two = fence(mixed_heads, *up_two)
    mixed_other = flip(mixed_heads, "c")
    up_own, out_own = assemble(
        up_ring,
        up_one,
        up_two,
        ring,
        ((ring, 2, 2, 2, rows, hidden // 2), (ring, 2, 2, rows, width)),
        write_up,
        "place_up",
    )
    up_own = up_own.reshape(width, hidden // 2)
    out_own = out_own.reshape(channels, width)
    out_other = flip(out_own, "c")
    residual = inputs + mm(mixed_heads, out_own) + mm(mixed_other, out_other)
    core_id = core.astype(jnp.int32).reshape(1)
    second_rows, activated, slope, down_theirs, mixed_mine = ffn_forward(
        core_id, residual, vec_all, up_own, up_bias_own, down_own
    )

    def mine(array):
        return lax.dynamic_slice_in_dim(array, core * block_len, block_len, 0)

    def theirs(array):
        return lax.dynamic_slice_in_dim(array, (1 - core) * block_len, block_len, 0)

    down_part = mm(activated, down_own)
    slope, down_theirs = fence(slope, down_theirs)
    down_other = flip(down_theirs, "c")
    pre_grad, up_bias_grad, second_theirs, second_mine = ffn_backward(core_id, grad_all, slope, up_own, down_own)
    second_theirs, down_other = fence(second_theirs, down_other)
    second_other = flip(second_theirs, "c")
    mixed = (mixed_mine + down_other.astype(F32)).astype(BF)
    residual_half = mine(residual)
    second_other, mixed = fence(second_other, mixed)
    mixed = swap_cy(mixed)[None]
    down_sum = mm_tn(activated, grad_all).astype(BF).reshape(ring, 2, 1, 2, -1, rows, width)
    up_sum = mm_tn(second_rows, pre_grad).astype(BF).reshape(ring, 2, 2, 2, 1, rows, hidden // 2)
    down_sum, up_sum = fence(down_sum, up_sum)

    ffn_one = pair_one(down_sum, up_sum)
    second_grad = second_mine + second_other.astype(F32)
    unit_two_h, scale_two_h = norm_stats(residual_half)
    grad_half_f = grad_half.astype(F32)
    gain_two_grad = jnp.sum(second_grad * unit_two_h, axis=0)
    bias_two_grad = jnp.sum(second_grad, axis=0)
    down_bias_grad = jnp.sum(grad_half_f, axis=0)
    resid_grad = grad_half_f + norm_back(second_grad, unit_two_h, scale_two_h, vec_all[10:11])
    mix_half = resid_grad.astype(BF)
    mix_grad = ordered(mix_half, flip(mix_half, "c"), core, 0).reshape(length, width)

    cos_t, sin_t = tables[0], tables[1]
    query_f, key_f, value_f = [
        heads[:, i * channels : (i + 1) * channels].astype(F32) for i in range(3)
    ]
    padded = jnp.pad(key_f, ((tap_count - 1, 0), (0, 0)))
    convolved, shifted = convolved.astype(F32), shifted.astype(F32)
    prod_re, prod_im, kern_re, kern_im = [
        array.astype(F32) for array in (prod_re, prod_im, kern_re, kern_im)
    ]
    products = shifted * value_f
    head_grad = mm_nt(mix_grad, out_own).astype(BF).astype(F32)
    query_grad = (head_grad * convolved).astype(BF)
    conv_grad = head_grad * query_f
    conv_low = conv_grad.astype(BF)
    skip_grad = jnp.sum(conv_grad * products, axis=0)
    grad_re = mm(cos_t, conv_low)
    grad_im = mm(sin_t, conv_low)
    out_grad = mm_tn(mixed_heads, mix_grad).astype(BF)
    q_grad = mm_tn(first_rows, query_grad).astype(BF)
    back_re = (grad_re * kern_re + grad_im * kern_im).astype(BF)
    back_im = (grad_im * kern_re - grad_re * kern_im).astype(BF)
    lag_re = (grad_re * prod_re + grad_im * prod_im).astype(BF)
    lag_im = (grad_im * prod_re - grad_re * prod_im).astype(BF)
    lag_grad = (mm_tn(lag_re, cos_t) + mm_tn(lag_im, sin_t)) * (1.0 / length)
    lag_sum = lag_grad.astype(BF).reshape(ring, 2, 1, 2, 1, rows, length)
    back = (mm_tn(cos_t, back_re) + mm_tn(sin_t, back_im)) * (1.0 / length)
    product_grad = back + skip * conv_grad
    out_sum = out_grad.reshape(ring, 2, 1, 2, 1, rows, width)
    q_sum = q_grad.reshape(ring, 2, 2, 2, 1, rows, channels)
    shifted_grad = product_grad * value_f
    value_grad = (product_grad * shifted).astype(BF)
    padded_grad = jnp.pad(shifted_grad, ((0, tap_count - 1), (0, 0)))
    key_grad = jnp.zeros_like(key_f)
    tap_rows = []
    for tap in range(tap_count):
        at = tap_count - 1 - tap
        key_grad = key_grad + padded_grad[tap : tap + length] * taps[tap : tap + 1]
        tap_rows.append(jnp.sum(shifted_grad * padded[at : at + length], axis=0))
    key_grad = key_grad.astype(BF)
    kv_grad = jnp.concatenate([key_grad, value_grad], axis=1)
    kv_sum = mm_tn(first_rows, kv_grad).astype(BF).reshape(ring, 2, 2, 2, 1, rows, 2 * channels)
    kv_sum, q_sum, out_sum, lag_sum, kv_grad, *ffn_one = fence(
        kv_sum, q_sum, out_sum, lag_sum, kv_grad, *ffn_one
    )

    lag_width = length // 8
    ffn_two = pair_two(down_sum, up_sum, ffn_one, ring)
    outq_one = direct_one((q_sum, out_sum, lag_sum), ring, lag_width)
    first_part = mm_nt(jnp.concatenate([query_grad, kv_grad], axis=1), w_qkv)
    first_other = flip(theirs(first_part).astype(BF), "c").astype(F32)
    first_grad = mine(first_part) + first_other
    unit_one_h, scale_one_h = norm_stats(token_half.astype(F32))
    gain_one_grad = jnp.sum(first_grad * unit_one_h, axis=0)
    bias_one_grad = jnp.sum(first_grad, axis=0)
    token_grad = resid_grad + norm_back(first_grad, unit_one_h, scale_one_h, vec_all[8:9])
    token_grad = token_grad.astype(BF)

    vec_grads = jnp.stack(
        [gain_one_grad, bias_one_grad, gain_two_grad, bias_two_grad, down_bias_grad]
    )
    vec_grads = vec_grads.reshape(5, groups, 2, 2 * rows)
    vec_keep = lax.dynamic_index_in_dim(vec_grads, core, 2, keepdims=False)
    vec_send = lax.dynamic_index_in_dim(vec_grads, 1 - core, 2, keepdims=False)
    vec_sum = (vec_keep + flip(vec_send, "c")).reshape(5, channels)
    small = jnp.concatenate([vec_sum, jnp.stack(tap_rows), skip_grad[None]])
    small = jnp.concatenate([small.T, up_bias_grad.reshape(channels, -1)], axis=1)
    small = jnp.pad(small, ((0, 0), (0, 128 - small.shape[1]))).astype(BF)
    small_sum = small.reshape(ring, 2, 1, 2, 1, rows, 128)
    small_sum, token_grad, *ffn_two = fence(small_sum, token_grad, *ffn_two)

    ffn_held = pair_three(down_sum, up_sum, ffn_one, ffn_two, ring, width)
    ffn_three = ring_send(ffn_held, ring)
    kv_one = direct_one((kv_sum, small_sum), ring, 128)
    token_grad = swap_cy(token_grad).astype(F32)[None]
    ffn_held, *outq_one = fence(ffn_held, *outq_one)
    outq_held = direct_two((q_sum, out_sum, lag_sum), outq_one, ring, lag_width)
    outq_three = ring_send(outq_held, ring)
    outq_held, *late = fence(outq_held, *kv_one, *ffn_three)
    kv_one, ffn_three = late[:3], late[3:]
    kv_held = direct_two((kv_sum, small_sum), kv_one, ring, 128)
    kv_three = ring_send(kv_held, ring)
    ffn_s = ring_sum(ffn_held, ffn_three)
    down_pieces = up_rows // rows
    down_s = ffn_s[:down_pieces].reshape(up_rows, width)
    up_half = (ffn_s.shape[0] - down_pieces) // 2
    up_s = jnp.stack([join(ffn_s[down_pieces : down_pieces + up_half]), join(ffn_s[down_pieces + up_half :])])
    up_s = merge_columns(up_s, core, groups)
    outq_s = ring_sum(outq_held, outq_three)
    q_pieces = channels // lag_width
    query_s = merge_columns(
        jnp.stack([join(outq_s[:q_pieces]), join(outq_s[q_pieces : 2 * q_pieces])]), core, groups
    )
    out_s = join(outq_s[2 * q_pieces : 4 * q_pieces])
    lag_s = join(outq_s[4 * q_pieces :])
    coef_s, rate_s = ssm_kernel_grads(lag_s, ssm_coef.astype(F32), ssm_rate.astype(F32))
    up_s, down_s, query_s, out_s, coef_s, rate_s, token_grad, *kv_three = fence(
        up_s, down_s, query_s, out_s, coef_s, rate_s, token_grad, *kv_three
    )
    kv_s = ring_sum(kv_held, kv_three)
    pieces = channels // 128

    def heads_of(first):
        both = [join(kv_s[(first + i) * pieces : (first + i + 1) * pieces]) for i in range(2)]
        return jnp.concatenate(both, axis=0)

    heads_s = merge_columns(jnp.stack([heads_of(0), heads_of(2)]), core, groups)
    key_s, value_s = heads_s[:rows], heads_s[rows:]
    small = kv_s[4 * pieces]
    vec_s = small[:, :5].T
    taps_s = small[:, 5 : 5 + tap_count]
    skip_s = small[:, 5 + tap_count]
    up_bias_s = small[:, 6 + tap_count : 6 + tap_count + up_rows // rows].reshape(up_rows)
    return (
        mixed,
        token_grad,
        vec_s[0],
        vec_s[1],
        query_s,
        key_s,
        value_s,
        taps_s,
        coef_s,
        rate_s,
        skip_s,
        out_s,
        vec_s[2],
        vec_s[3],
        up_s,
        up_bias_s,
        down_s,
        vec_s[4],
    )


def solution(mesh):
    dp_size, seq_size = mesh.devices.shape
    ring = dp_size // 4
    grid = Mesh(mesh.devices.reshape(ring, 2, 2, seq_size), ("r", "x", "c", "y"))
    dp = ("r", "x", "c")
    act = P(dp, "y", None)
    vec = P(dp + ("y",))
    mat = P(dp + ("y",), None)
    return jax.shard_map(
        functools.partial(body, ring),
        mesh=grid,
        in_specs=(
            act, P(dp), act, vec, vec, mat, mat, mat, mat, mat, mat, vec, mat, vec, vec, mat, vec, mat, vec,
        ),
        out_specs=(
            act, act, vec, vec, mat, mat, mat, mat, mat, mat, vec, mat, vec, vec, mat, vec, mat, vec,
        ),
        check_vma=False,
    )
```

```python
import functools
import math

import jax
import jax.numpy as jnp
from jax import lax
from jax.experimental import pallas as pl
from jax.experimental.pallas import tpu as pltpu
from jax.sharding import Mesh, PartitionSpec as P

EPS = 1e-05
BF = jnp.bfloat16
F32 = jnp.float32
SQRT_2_PI = math.sqrt(2.0 / math.pi)
MISC = ("r", "x", "y")


def flip(value, axis):
    return lax.ppermute(value, axis, [(0, 1), (1, 0)])


def ordered(mine, other, place, axis):
    first = jnp.where(place == 0, mine, other)
    second = jnp.where(place == 0, other, mine)
    return jnp.stack([first, second], axis=axis)


def swap_cy(value):
    moved = lax.ppermute(value, ("c", "y"), [(1, 2), (2, 1)])
    return jnp.where(lax.axis_index("c") == lax.axis_index("y"), value, moved)


def shift_ring(value, distance, ring):
    return lax.ppermute(value, "r", [(i, (i + distance) % ring) for i in range(ring)])


def flip_xy(value):
    return lax.ppermute(value, ("x", "y"), [(i, 3 - i) for i in range(4)])


def place(whole, part, starts):
    return lax.dynamic_update_slice(whole, part, starts)


def gather_ring(block, ring):
    here = lax.axis_index("r")
    rest = (0,) * block.ndim
    whole = jnp.zeros((ring,) + block.shape, block.dtype)
    whole = place(whole, block[None], (here,) + rest)
    for distance in range(1, ring):
        moved = shift_ring(block, distance, ring)
        whole = place(whole, moved[None], (lax.rem(here - distance + ring, ring),) + rest)
    return whole


def ring_pieces(block, ring):
    blocks = [block] + [shift_ring(block, d, ring) for d in range(1, ring)]
    return tuple(jnp.stack([part[half] for part in blocks]) for half in range(2))


def near_one(halves):
    return flip(halves[0], "y"), flip(halves[1], "x")


def near_two(halves, moved):
    first = flip(jnp.concatenate([halves[0], moved[0]]), "x")
    second = flip(jnp.concatenate([halves[1], moved[1]]), "y")
    return first, second


def chip_ids():
    return jnp.stack([lax.axis_index("r"), lax.axis_index("x"), lax.axis_index("y")]).astype(jnp.int32)


def grant(*blocks):
    total = 0
    for shape, kind in blocks:
        rows = -(-shape[-2] // 16) * 16
        total += math.prod(shape[:-2]) * rows * shape[-1] * jnp.dtype(kind).itemsize
    return pltpu.CompilerParams(vmem_limit_bytes=2 * total + (2 << 20))


def assemble_body(write, ids, *refs):
    ins, outs = refs[:8], refs[8:]
    for half in range(2):
        for index in range(4):
            x = lax.rem(ids[1] + index // 2, 2)
            y = lax.rem(ids[2] + index % 2, 2)
            write(outs, ins[4 * half + index], half, x, y)


def assemble(halves, one, two, ring, shapes, write, name):
    sources = (
        (halves[0], 0), (one[0], 0), (two[0], 0), (two[0], ring),
        (halves[1], 0), (two[1], 0), (one[1], 0), (two[1], ring),
    )
    tail = halves[0].shape[1:]
    zeros = (0,) * len(tail)
    specs = [
        pl.BlockSpec((None,) + tail, lambda i, ids, base=base: (i + base,) + zeros) for _, base in sources
    ]
    moved = 32 * math.prod(tail) * ring
    return pl.pallas_call(
        functools.partial(assemble_body, write),
        out_shape=tuple(jax.ShapeDtypeStruct(shape, halves[0].dtype) for shape in shapes),
        grid_spec=pltpu.PrefetchScalarGridSpec(
            num_scalar_prefetch=1,
            grid=(ring,),
            in_specs=specs,
            out_specs=tuple(
                pl.BlockSpec(
                    (None,) + shape[1:],
                    lambda i, ids, rank=len(shape): (lax.rem(ids[0] + ring - i, ring),) + (0,) * (rank - 1),
                )
                for shape in shapes
            ),
        ),
        compiler_params=grant(*[(tail, BF)] * 8, *[(shape[1:], BF) for shape in shapes]),
        cost_estimate=pl.CostEstimate(flops=0, bytes_accessed=moved, transcendentals=0),
        name=name,
    )(chip_ids(), *[array for array, _ in sources])


def write_heads(outs, part, half, x, y):
    outs[0][x, half, y] = part[0]


def write_up(outs, part, half, x, y):
    lanes = part.shape[-1]
    count = part.shape[0] - 1
    for index in range(count):
        outs[0][x, half, y, :, index * lanes : (index + 1) * lanes] = part[index]
    outs[1][x, y, :, half * lanes : (half + 1) * lanes] = part[count]


def here_x(i, ids):
    return ids[1]


def other_x(i, ids):
    return 1 - ids[1]


def here_y(i, ids):
    return ids[2]


def other_y(i, ids):
    return 1 - ids[2]


def step_r(i, ids):
    return i


def turn_r(ring):
    return lambda i, ids: lax.rem(ids[0] + i, ring)


def sums_body(plan, ids, *refs):
    ins, outs = refs[: len(refs) - len(plan)], refs[len(refs) - len(plan) :]
    for out, columns in zip(outs, plan):
        width = out.shape[2]
        at = 0
        for terms in columns:
            first = ins[terms[0]]
            cores, extra, _, lanes = first.shape
            index = 0
            for core in range(cores):
                for more in range(extra):
                    for low in range(0, lanes, width):
                        total = None
                        for term in terms:
                            ref = ins[term]
                            if len(ref.shape) == 4:
                                value = ref[core, more, :, low : low + width]
                            else:
                                value = ref[at + index]
                            value = value.astype(F32)
                            total = value if total is None else total + value
                        out[at + index] = total.astype(out.dtype)
                        index += 1
            at += index


def sums(ring, jobs):
    arrays, specs, plan, shapes = [], [], [], []
    for width, columns in jobs:
        pieces = 0
        numbers = []
        for terms in columns:
            mine = []
            for count, (array, picks) in enumerate(terms):
                tail = array.shape[len(picks) :]
                block = tuple(
                    size if pick is None else None for size, pick in zip(array.shape, picks)
                ) + tail

                def index_map(i, ids, picks=picks, tail=tail):
                    return tuple(0 if pick is None else pick(i, ids) for pick in picks) + (0,) * len(tail)

                if count == 0:
                    held = [size for size in block if size is not None]
                    pieces += held[0] * held[1] * (held[3] // width)
                mine.append(len(arrays))
                arrays.append(array)
                specs.append(pl.BlockSpec(block, index_map))
            numbers.append(mine)
        plan.append(numbers)
        rows = columns[0][0][0].shape[-2]
        shapes.append(jax.ShapeDtypeStruct((ring, pieces, rows, width), BF))
    moved = sum(2 * math.prod(shape.shape) * 2 for shape in shapes)
    return pl.pallas_call(
        functools.partial(sums_body, plan),
        out_shape=tuple(shapes),
        grid_spec=pltpu.PrefetchScalarGridSpec(
            num_scalar_prefetch=1,
            grid=(ring,),
            in_specs=specs,
            out_specs=tuple(
                pl.BlockSpec((None,) + shape.shape[1:], lambda i, ids: (i, 0, 0, 0)) for shape in shapes
            ),
        ),
        compiler_params=grant(
            *[
                (tuple(size for size in spec.block_shape if size is not None), BF)
                for spec in specs
            ],
            *[(shape.shape[1:], BF) for shape in shapes],
        ),
        cost_estimate=pl.CostEstimate(flops=0, bytes_accessed=2 * moved, transcendentals=0),
        name="sums",
    )(chip_ids(), *[pltpu.with_memory_space_constraint(array, pltpu.HBM) for array in arrays])


def take(parts, axis, index):
    return lax.dynamic_index_in_dim(parts, index, axis, keepdims=False)


def pair_one(y_first, x_first):
    x, y = lax.axis_index("x"), lax.axis_index("y")
    return flip(take(y_first, 3, 1 - y), "y"), flip(take(x_first, 1, 1 - x), "x")


def pair_two(y_first, x_first, moved, ring):
    one = [
        (y_first, (step_r, other_x, None, here_y)),
        (moved[0], (step_r, other_x, None)),
    ]
    two = [
        (x_first, (step_r, here_x, None, other_y)),
        (moved[1], (step_r, None, other_y)),
    ]
    send_one, send_two = sums(ring, [(y_first.shape[-1], [one]), (x_first.shape[-1], [two])])
    shape_one = (ring, y_first.shape[2]) + y_first.shape[4:]
    shape_two = (ring, x_first.shape[2]) + x_first.shape[4:]
    return flip(send_one, "x").reshape(shape_one), flip(send_two, "y").reshape(shape_two)


def pair_three(y_first, x_first, moved_one, moved_two, ring, width):
    turn = turn_r(ring)
    one = [
        (y_first, (turn, here_x, None, here_y)),
        (moved_one[0], (turn, here_x, None)),
        (moved_two[0], (turn, None)),
    ]
    two = [
        (x_first, (turn, here_x, None, here_y)),
        (moved_one[1], (turn, None, here_y)),
        (moved_two[1], (turn, None)),
    ]
    return sums(ring, [(width, [one, two])])[0]


def direct_one(arrays, ring, width):
    spots = ((here_x, other_y), (other_x, here_y), (other_x, other_y))
    along_y, along_x, across = sums(
        ring, [(width, [[(array, (step_r, x, None, y))] for array in arrays]) for x, y in spots]
    )
    return flip(along_y, "y"), flip(along_x, "x"), flip_xy(across)


def direct_two(arrays, moved, ring, width):
    turn = turn_r(ring)
    columns = [
        [(array, (turn, here_x, None, here_y))] + [(part, (turn,)) for part in moved] for array in arrays
    ]
    return sums(ring, [(width, columns)])[0]


def ring_send(held, ring):
    return tuple(shift_ring(held[distance], distance, ring) for distance in range(1, ring))


def ring_sum(held, moved):
    total = held[0].astype(F32)
    for part in moved:
        total = total + part.astype(F32)
    return total


def join(pieces):
    return jnp.concatenate([pieces[i] for i in range(pieces.shape[0])], axis=1)


def scatter_near(pick):
    x, y = lax.axis_index("x"), lax.axis_index("y")
    total = pick(x, y).astype(F32)
    total = total + flip(pick(x, 1 - y), "y").astype(F32)
    total = total + flip(pick(1 - x, y), "x").astype(F32)
    return total + flip_xy(pick(1 - x, 1 - y)).astype(F32)


def gather_quad(block):
    x, y = lax.axis_index("x"), lax.axis_index("y")
    parts = ((block, x, y), (flip(block, "y"), x, 1 - y), (flip(block, "x"), 1 - x, y), (flip_xy(block), 1 - x, 1 - y))
    full = jnp.zeros((2, 2) + block.shape, block.dtype)
    for part, at_x, at_y in parts:
        full = place(full, part[None, None], (at_x, at_y) + (0,) * block.ndim)
    return full


def fence(*values):
    return lax.optimization_barrier(values)


def merge_columns(parts, core, groups):
    keep = lax.dynamic_index_in_dim(parts, core, 0, keepdims=False)
    send = lax.dynamic_index_in_dim(parts, 1 - core, 0, keepdims=False)
    count, cols = keep.shape
    other = flip(send.astype(BF), "c").astype(F32)
    grid = ordered(
        keep.reshape(count, groups, -1), other.reshape(count, groups, -1), core, 2
    )
    return grid.reshape(count, 2 * cols)


def mm(left, right):
    return jnp.dot(left, right, preferred_element_type=F32)


def mm_tn(left, right):
    return lax.dot_general(
        left, right, (((0,), (0,)), ((), ())), preferred_element_type=F32
    )


def mm_nt(left, right):
    return lax.dot_general(
        left, right, (((1,), (1,)), ((), ())), preferred_element_type=F32
    )


def norm_stats(values):
    mean = jnp.mean(values, axis=-1, keepdims=True)
    centred = values - mean
    variance = jnp.mean(centred * centred, axis=-1, keepdims=True)
    scale = lax.rsqrt(variance + EPS)
    return centred * scale, scale


def norm_back(grad, unit, scale, gain):
    inner = grad * gain
    mean_one = jnp.mean(inner, axis=-1, keepdims=True)
    mean_two = jnp.mean(inner * unit, axis=-1, keepdims=True)
    return scale * (inner - mean_one - unit * mean_two)


def tables_body(token_ref, cos_ref, sin_ref, cos_turn_ref, sin_turn_ref, cos_high_ref, sin_high_ref):
    length = cos_ref.shape[0]
    part = 32
    blocks = length // part
    step = math.pi / (2.0 * length)
    period = 4 * length
    rows = lax.broadcasted_iota(jnp.int32, (part, length), 0)
    cols = lax.broadcasted_iota(jnp.int32, (part, length), 1)

    def turns(count):
        angle = (count & (period - 1)).astype(F32) * step
        return jnp.cos(angle), jnp.sin(angle)

    def fill(high, low, cos_out, sin_out):
        cos_high_ref[...], sin_high_ref[...] = turns(high)
        cos_low, sin_low = turns(low)

        def put(block, carry):
            ch, sh = cos_high_ref[pl.ds(block, 1), :], sin_high_ref[pl.ds(block, 1), :]
            at = pl.ds(pl.multiple_of(block * part, part), part)
            cos_out[at, :] = (ch * cos_low - sh * sin_low).astype(BF)
            sin_out[at, :] = (sh * cos_low + ch * sin_low).astype(BF)
            return carry

        lax.fori_loop(0, blocks, put, 0)

    fill(2 * part * rows * cols, (2 * rows + 1) * cols, cos_ref, sin_ref)
    fill(part * rows * (2 * cols + 1), rows * (2 * cols + 1), cos_turn_ref, sin_turn_ref)


def dft_tables(length, token):
    table = jax.ShapeDtypeStruct((length, length), BF)
    return pl.pallas_call(
        tables_body,
        out_shape=(table,) * 4,
        in_specs=[pl.BlockSpec(memory_space=pl.ANY)],
        out_specs=tuple(in_vmem(4)),
        scratch_shapes=[pltpu.VMEM((32, length), F32)] * 2,
        cost_estimate=pl.CostEstimate(flops=7 * 10**9, bytes_accessed=8 * length * length, transcendentals=0),
        compiler_params=pltpu.CompilerParams(vmem_limit_bytes=4 << 20),
        name="dft_tables",
    )(token)


def norm_body(core_ref, mine_ref, other_ref, vec_ref, all_ref, rows_ref):
    half = mine_ref.shape[0]
    step = 128
    for index, ref in enumerate((mine_ref, other_ref)):
        place = lax.rem(core_ref[0] + index, 2) * half

        def put(block_id, carry):
            block = ref[pl.ds(pl.multiple_of(block_id * step, step), step), :]
            at = pl.ds(pl.multiple_of(place + block_id * step, step), step)
            all_ref[at, :] = block
            unit, _ = norm_stats(block.astype(F32))
            rows_ref[at, :] = (unit * vec_ref[8:9, :] + vec_ref[9:10, :]).astype(BF)
            return carry

        lax.fori_loop(0, half // step, put, 0)


def first_norm(mine, other, core, vectors):
    half, width = mine.shape
    wide = jax.ShapeDtypeStruct((2 * half, width), BF)
    return pl.pallas_call(
        norm_body,
        out_shape=(wide, wide),
        in_specs=[pl.BlockSpec(memory_space=pltpu.SMEM)] + in_vmem(3),
        out_specs=tuple(in_vmem(2)),
        cost_estimate=pl.CostEstimate(flops=3 * 10**9, bytes_accessed=4 * half * width, transcendentals=0),
        compiler_params=pltpu.CompilerParams(vmem_limit_bytes=4 << 20),
        name="first_norm",
    )(core.astype(jnp.int32).reshape(1), mine, other, vectors)


def in_vmem(count):
    return [pl.BlockSpec(memory_space=pltpu.VMEM)] * count


def kernel_body(part, coef_ref, rate_ref, out_ref, high_ref, low_ref):
    states = coef_ref.shape[0]
    length = out_ref.shape[0]
    blocks = length // part
    lanes = out_ref.shape[1]
    high_ids = lax.broadcasted_iota(jnp.int32, (blocks, lanes), 0).astype(F32) * (part / length)
    low_ids = lax.broadcasted_iota(jnp.int32, (part, lanes), 0).astype(F32) * (1.0 / length)

    def fill(state, carry):
        rate = rate_ref[pl.ds(state, 1), :]
        coef = coef_ref[pl.ds(state, 1), :] * (length ** (-0.5))
        high_ref[state] = coef * jnp.exp(-rate * high_ids)
        low_ref[state] = jnp.exp(-rate * low_ids)
        return carry

    lax.fori_loop(0, states, fill, 0)
    for start in range(0, blocks, 8):

        def add(state, sums):
            low = low_ref[state]
            return tuple(
                total + high_ref[state, pl.ds(start + index, 1), :] * low
                for index, total in enumerate(sums)
            )

        zero = jnp.zeros((part, lanes), F32)
        sums = lax.fori_loop(0, states, add, (zero,) * 8, unroll=4)
        for index, total in enumerate(sums):
            out_ref[pl.ds((start + index) * part, part), :] = total.astype(out_ref.dtype)


def spectrum_body(part, states, params_ref, cos_ref, sin_ref, re_ref, im_ref, kernel_ref, high_ref, low_ref, coef_part, rate_part):
    length, channels = kernel_ref.shape
    for start in range(0, channels, 128):
        lanes = pl.ds(start, 128)
        coef_part[...] = params_ref[0:states, lanes]
        rate_part[...] = params_ref[states : 2 * states, lanes]
        kernel_body(part, coef_part, rate_part, kernel_ref.at[:, lanes], high_ref, low_ref)

    def put(block, carry):
        rows = pl.ds(pl.multiple_of(block * 256, 256), 256)
        re_ref[rows, :] = mm(cos_ref[rows, :], kernel_ref[...]).astype(BF)
        im_ref[rows, :] = mm(sin_ref[rows, :], kernel_ref[...]).astype(BF)
        return carry

    lax.fori_loop(0, length // 256, put, 0)


def ssm_spectrum(params, states, cos_t, sin_t, length):
    channels = params.shape[1]
    part = 32
    return pl.pallas_call(
        functools.partial(spectrum_body, part, states),
        out_shape=(jax.ShapeDtypeStruct((length, channels), BF),) * 2,
        in_specs=in_vmem(3),
        out_specs=tuple(in_vmem(2)),
        scratch_shapes=[
            pltpu.VMEM((length, channels), BF),
            pltpu.VMEM((states, length // part, 128), F32),
            pltpu.VMEM((states, part, 128), F32),
            pltpu.VMEM((states, 128), F32),
            pltpu.VMEM((states, 128), F32),
        ],
        cost_estimate=pl.CostEstimate(
            flops=600 * length * states * channels, bytes_accessed=2 * length * channels * 4, transcendentals=0
        ),
        compiler_params=pltpu.CompilerParams(vmem_limit_bytes=8 << 20),
        name="ssm_spectrum",
    )(params, cos_t, sin_t)


def conv_body(
    first, tap_count, heads_ref, kern_re_ref, kern_im_ref, params_ref, cos_ref, sin_ref, cos_turn_ref, sin_turn_ref,
    mixed_ref, conv_ref, shifted_ref, prod_re_ref, prod_im_ref,
    products_ref, low_ref, spec_re_ref, spec_im_ref,
):
    length, channels = mixed_ref.shape
    step = 128
    last = first + tap_count

    def shift(rows, keys):
        shifted = keys[8:] * params_ref[first : first + 1, :]
        for tap in range(1, tap_count):
            shifted = shifted + keys[8 - tap : 8 - tap + step] * params_ref[first + tap : first + tap + 1, :]
        shifted_ref[rows, :] = shifted.astype(BF)
        products = shifted * heads_ref[rows, 2 * channels : 3 * channels].astype(F32)
        products_ref[rows, :] = products
        low_ref[rows, :] = products.astype(BF)

    keys = heads_ref[0:step, channels : 2 * channels].astype(F32)
    shift(pl.ds(0, step), jnp.concatenate([jnp.zeros((8, channels), F32), keys], axis=0))

    def shift_block(block, carry):
        before = pl.ds(pl.multiple_of(block * step - 8, 8), step + 8)
        shift(
            pl.ds(pl.multiple_of(block * step, step), step),
            heads_ref[before, channels : 2 * channels].astype(F32),
        )
        return carry

    lax.fori_loop(1, length // step, shift_block, 0)

    def spectrum(block, carry):
        rows = pl.ds(pl.multiple_of(block * 256, 256), 256)
        prod_re = mm(cos_ref[rows, :], low_ref[...])
        prod_im = mm(sin_ref[rows, :], low_ref[...])
        kern_re, kern_im = kern_re_ref[rows, :].astype(F32), kern_im_ref[rows, :].astype(F32)
        prod_re_ref[rows, :] = prod_re.astype(BF)
        prod_im_ref[rows, :] = prod_im.astype(BF)
        spec_re_ref[rows, :] = (prod_re * kern_re - prod_im * kern_im).astype(BF)
        spec_im_ref[rows, :] = (prod_re * kern_im + prod_im * kern_re).astype(BF)
        return carry

    lax.fori_loop(0, length // 256, spectrum, 0)

    def convolve(block, carry):
        rows = pl.ds(pl.multiple_of(block * 256, 256), 256)
        conv = mm(cos_turn_ref[rows, :], spec_re_ref[...]) + mm(sin_turn_ref[rows, :], spec_im_ref[...])
        conv = conv * (1.0 / length) + params_ref[last : last + 1, :] * products_ref[rows, :]
        conv_ref[rows, :] = conv.astype(BF)
        mixed_ref[rows, :] = (heads_ref[rows, 0:channels].astype(F32) * conv).astype(BF)
        return carry

    lax.fori_loop(0, length // 256, convolve, 0)


def conv_forward(heads, kern_re, kern_im, params, first, tap_count, tables):
    length, channels = kern_re.shape
    wide = jax.ShapeDtypeStruct((length, channels), BF)
    return pl.pallas_call(
        functools.partial(conv_body, first, tap_count),
        out_shape=(wide,) * 5,
        in_specs=in_vmem(8),
        out_specs=tuple(in_vmem(5)),
        scratch_shapes=[
            pltpu.VMEM((length, channels), F32),
            pltpu.VMEM((length, channels), BF),
            pltpu.VMEM((length, channels), BF),
            pltpu.VMEM((length, channels), BF),
        ],
        cost_estimate=pl.CostEstimate(
            flops=24 * length * length * channels, bytes_accessed=16 * length * channels, transcendentals=0
        ),
        compiler_params=pltpu.CompilerParams(vmem_limit_bytes=10 << 20),
        name="conv_forward",
    )(heads, kern_re, kern_im, params, *tables)


def ssm_kernel_grads(grad, coef, rate):
    length = grad.shape[1]
    times = lax.broadcasted_iota(jnp.int32, (1, 1, length), 2).astype(F32) * (1.0 / length)
    weighted = grad[:, None] * jnp.exp(-rate[:, :, None] * times)
    scale = length ** (-0.5)
    return jnp.sum(weighted, axis=2) * scale, -coef * jnp.sum(weighted * times, axis=2) * scale


def row_block(cols, kind_rows=256):
    return pl.BlockSpec((kind_rows, cols), lambda i: (i, 0))


def whole_block(rows, cols):
    return pl.BlockSpec((rows, cols), lambda i: (0, 0), pipeline_mode=pl.Buffered(1))


def turned_block(cols, steps):
    return pl.BlockSpec((256, cols), lambda i, core: (lax.rem(i + steps // 2 * (1 - core[0]), steps), 0))


def same_block(rows, cols):
    return pl.BlockSpec((rows, cols), lambda i, core: (0, 0), pipeline_mode=pl.Buffered(1))


def half_blocks(cols, steps):
    theirs = pl.BlockSpec((256, cols), lambda i, core: (jnp.minimum(i, steps // 2 - 1), 0))
    mine = pl.BlockSpec((256, cols), lambda i, core: (jnp.maximum(i - steps // 2, 0), 0))
    return theirs, mine


def put_half(theirs_ref, mine_ref, theirs, mine):
    first = pl.program_id(0) < pl.num_programs(0) // 2

    @pl.when(first)
    def _():
        theirs_ref[...] = theirs.astype(theirs_ref.dtype)

    @pl.when(jnp.logical_not(first))
    def _():
        mine_ref[...] = mine.astype(mine_ref.dtype)


def ffn_forward_body(
    core_ref, resid_ref, vec_ref, up_ref, up_bias_ref, down_ref,
    rows_ref, act_ref, slope_ref, theirs_ref, mine_ref,
):
    resid = resid_ref[...]
    unit, _ = norm_stats(resid)
    second = (unit * vec_ref[10:11, :] + vec_ref[11:12, :]).astype(BF)
    rows_ref[...] = second
    pre = mm(second, up_ref[...]) + up_bias_ref[...]
    square = pre * pre
    bend = jnp.tanh(pre * (SQRT_2_PI + SQRT_2_PI * 0.044715 * square))
    half = 0.5 * pre
    act = (half + half * bend).astype(BF)
    act_ref[...] = act
    steep = SQRT_2_PI + 3.0 * SQRT_2_PI * 0.044715 * square
    slope_ref[...] = (0.5 + 0.5 * bend + half * (1.0 - bend * bend) * steep).astype(BF)
    part = mm(act, down_ref[...])
    put_half(theirs_ref, mine_ref, part, part + resid + vec_ref[12:13, :])


def ffn_forward(core, resid, vectors, up, up_bias, down):
    length, width = resid.shape
    hidden = up.shape[1]
    steps = length // 256
    return pl.pallas_call(
        ffn_forward_body,
        out_shape=(
            jax.ShapeDtypeStruct((length, width), BF),
            jax.ShapeDtypeStruct((length, hidden), BF),
            jax.ShapeDtypeStruct((length, hidden), BF),
            jax.ShapeDtypeStruct((length // 2, width), BF),
            jax.ShapeDtypeStruct((length // 2, width), F32),
        ),
        grid_spec=pltpu.PrefetchScalarGridSpec(
            num_scalar_prefetch=1,
            grid=(steps,),
            in_specs=[
                turned_block(width, steps),
                same_block(vectors.shape[0], width),
                same_block(width, hidden),
                same_block(1, hidden),
                same_block(hidden, width),
            ],
            out_specs=(
                turned_block(width, steps),
                turned_block(hidden, steps),
                turned_block(hidden, steps),
            )
            + half_blocks(width, steps),
        ),
        compiler_params=pltpu.CompilerParams(vmem_limit_bytes=28 << 20),
        cost_estimate=pl.CostEstimate(
            flops=8 * length * width * hidden, bytes_accessed=12 * length * width, transcendentals=0
        ),
        name="ffn_forward",
    )(core, resid, vectors, up, up_bias, down)


def ffn_backward_body(core_ref, grad_ref, slope_ref, up_ref, down_ref, pre_ref, bias_ref, theirs_ref, mine_ref):
    act_grad = mm_nt(grad_ref[...], down_ref[...])
    pre = (act_grad * slope_ref[...].astype(F32)).astype(BF)
    pre_ref[...] = pre
    part = mm_nt(pre, up_ref[...])
    put_half(theirs_ref, mine_ref, part, part)

    @pl.when(pl.program_id(0) == 0)
    def _():
        bias_ref[...] = jnp.zeros_like(bias_ref)

    bias_ref[...] += jnp.sum(pre.astype(F32), axis=0, keepdims=True)


def ffn_backward(core, grad, slope, up, down):
    length, width = grad.shape
    hidden = up.shape[1]
    steps = length // 256
    return pl.pallas_call(
        ffn_backward_body,
        out_shape=(
            jax.ShapeDtypeStruct((length, hidden), BF),
            jax.ShapeDtypeStruct((1, hidden), F32),
            jax.ShapeDtypeStruct((length // 2, width), BF),
            jax.ShapeDtypeStruct((length // 2, width), F32),
        ),
        grid_spec=pltpu.PrefetchScalarGridSpec(
            num_scalar_prefetch=1,
            grid=(steps,),
            in_specs=[
                turned_block(width, steps),
                turned_block(hidden, steps),
                same_block(width, hidden),
                same_block(hidden, width),
            ],
            out_specs=(turned_block(hidden, steps), pl.BlockSpec((1, hidden), lambda i, core: (0, 0)))
            + half_blocks(width, steps),
        ),
        compiler_params=pltpu.CompilerParams(vmem_limit_bytes=24 << 20),
        cost_estimate=pl.CostEstimate(
            flops=6 * length * width * hidden, bytes_accessed=12 * length * width, transcendentals=0
        ),
        name="ffn_backward",
    )(core, grad, slope, up, down)


def body(
    ring,
    tokens,
    lengths,
    cotangent,
    norm1_gain,
    norm1_bias,
    w_query,
    w_key,
    w_value,
    shift_taps,
    ssm_coef,
    ssm_rate,
    skip_gain,
    w_out,
    norm2_gain,
    norm2_bias,
    w_up,
    up_bias,
    w_down,
    down_bias,
):
    core = lax.axis_index("c")
    groups = 2 * ring
    _, block_len, width = tokens.shape
    length = 2 * block_len
    rows = w_query.shape[0]
    up_rows = up_bias.shape[0]
    hidden = w_up.shape[1]
    states = ssm_coef.shape[1]
    tap_count = shift_taps.shape[1]
    channels = width // 2

    def columns(weight, which):
        grid = weight.reshape(rows, groups, 2, -1)
        return jnp.where(which == 0, grid[:, :, 0], grid[:, :, 1]).reshape(rows, -1)

    down_own = lax.all_gather(w_down, MISC, axis=0, tiled=True)
    matrices = (w_query, w_key, w_value, w_up)
    keep = jnp.concatenate([columns(w, core) for w in matrices], axis=1)
    send = jnp.concatenate([columns(w, 1 - core) for w in matrices], axis=1)
    norm1_gain, ssm_coef, ssm_rate, send = fence(norm1_gain, ssm_coef, ssm_rate, send)
    packed = ordered(keep, flip(send, "c"), core, 0)
    first_pack = packed[:, None, :, : 3 * channels]
    first_ring = ring_pieces(first_pack, ring)
    up_lanes = packed[:, :, 3 * channels :]
    up_pack = jnp.stack(
        [up_lanes[:, :, i * channels : (i + 1) * channels] for i in range(hidden // width)]
        + [jnp.stack([w_out[:, :channels], w_out[:, channels:]])],
        axis=1,
    )

    vectors = jnp.stack(
        [skip_gain, skip_gain, skip_gain, skip_gain, norm1_gain, norm1_bias, norm2_gain, norm2_bias, down_bias]
    )
    misc = jnp.concatenate(
        [ssm_coef, ssm_rate, shift_taps, vectors.T], axis=1
    )
    bias_row = jnp.pad(up_bias, (0, 256 - up_rows)).reshape(1, 256)
    misc = jnp.pad(misc, ((0, 0), (0, 256 - misc.shape[1])))
    misc = jnp.pad(jnp.concatenate([misc, bias_row]), ((0, -(rows + 1) % 8), (0, 0)))
    misc_near = gather_quad(misc)
    misc_near, *first_ring = fence(misc_near, *first_ring)
    misc_all = gather_ring(misc_near, ring)
    params = misc_all[..., :rows, :].reshape(channels, 256)
    side = params[:, 2 * states :]
    params = params.T.astype(F32)
    taps = params[2 * states : 2 * states + tap_count]
    skip = params[2 * states + tap_count : 2 * states + tap_count + 1]
    side = ordered(
        side.reshape(groups, 2 * rows, -1), flip(side, "c").reshape(groups, 2 * rows, -1), core, 1
    )
    vec_all = side.reshape(width, -1).T.astype(F32)
    up_bias_own = misc_all[..., rows, :up_rows].astype(F32).reshape(1, hidden // 2)

    start = lax.axis_index("y") * block_len
    valid = start + lax.broadcasted_iota(jnp.int32, (block_len, 1), 0) < lengths[0]
    masked = jnp.where(valid, cotangent[0], jnp.zeros((), BF))
    masked, first_pack = fence(masked, first_pack)
    grad_half = swap_cy(masked)

    token_half = swap_cy(tokens[0])
    token_other = flip(token_half, "c")
    tables = dft_tables(length, first_pack)
    tables, first_ring = list(tables), list(first_ring)
    *tables, first_zero, first_half = fence(*tables, *first_ring)
    first_ring = (first_zero, first_half)
    first_one = near_one(first_ring)
    params, up_pack, token_other, grad_half, *first_one = fence(
        params, up_pack, token_other, grad_half, *first_one
    )
    first_two = near_two(first_ring, first_one)
    up_ring = ring_pieces(up_pack, ring)
    kern_re, kern_im = ssm_spectrum(params, states, tables[0], tables[1], length)
    kern_re, token_half = fence(kern_re, token_half)
    token_all, first_rows = first_norm(token_half, token_other, core, vec_all)
    first_rows, *first_two = fence(first_rows, *first_two)
    inputs = token_all.astype(F32)
    grad_all = ordered(grad_half, flip(grad_half, "c"), core, 0).reshape(length, width)
    w_qkv = assemble(
        first_ring, first_one, first_two, ring, ((ring, 2, 2, 2, rows, 3 * channels),), write_heads, "place_heads"
    )[0].reshape(width, 3 * channels)
    w_qkv, *up_ring = fence(w_qkv, *up_ring)
    up_one = near_one(up_ring)

    heads = mm(first_rows, w_qkv).astype(BF)
    heads, *up_one = fence(heads, *up_one)
    up_two = near_two(up_ring, up_one)
    mixed_heads, convolved, shifted, prod_re, prod_im = conv_forward(
        heads, kern_re, kern_im, params, 2 * states, tap_count, tables
    )
    mixed_heads, down_own, *up_two = fence(mixed_heads, down_own, *up_two)
    mixed_other = flip(mixed_heads, "c")
    up_own, out_own = assemble(
        up_ring,
        up_one,
        up_two,
        ring,
        ((ring, 2, 2, 2, rows, hidden // 2), (ring, 2, 2, rows, width)),
        write_up,
        "place_up",
    )
    up_own = up_own.reshape(width, hidden // 2)
    out_own = out_own.reshape(channels, width)
    out_other = flip(out_own, "c")
    residual = inputs + mm(mixed_heads, out_own) + mm(mixed_other, out_other)
    core_id = core.astype(jnp.int32).reshape(1)
    second_rows, activated, slope, down_theirs, mixed_mine = ffn_forward(
        core_id, residual, vec_all, up_own, up_bias_own, down_own
    )

    def mine(array):
        return lax.dynamic_slice_in_dim(array, core * block_len, block_len, 0)

    def theirs(array):
        return lax.dynamic_slice_in_dim(array, (1 - core) * block_len, block_len, 0)

    down_part = mm(activated, down_own)
    slope, down_theirs = fence(slope, down_theirs)
    down_other = flip(down_theirs, "c")
    pre_grad, up_bias_grad, second_theirs, second_mine = ffn_backward(core_id, grad_all, slope, up_own, down_own)
    second_theirs, down_other = fence(second_theirs, down_other)
    second_other = flip(second_theirs, "c")
    mixed = (mixed_mine + down_other.astype(F32)).astype(BF)
    residual_half = mine(residual)
    second_other, mixed = fence(second_other, mixed)
    mixed = swap_cy(mixed)[None]
    down_sum = mm_tn(activated, grad_all).astype(BF).reshape(ring, 2, 1, 2, -1, rows, width)
    up_sum = mm_tn(second_rows, pre_grad).astype(BF).reshape(ring, 2, 2, 2, 1, rows, hidden // 2)
    down_sum, up_sum = fence(down_sum, up_sum)

    ffn_one = pair_one(down_sum, up_sum)
    second_grad = second_mine + second_other.astype(F32)
    unit_two_h, scale_two_h = norm_stats(residual_half)
    grad_half_f = grad_half.astype(F32)
    gain_two_grad = jnp.sum(second_grad * unit_two_h, axis=0)
    bias_two_grad = jnp.sum(second_grad, axis=0)
    down_bias_grad = jnp.sum(grad_half_f, axis=0)
    resid_grad = grad_half_f + norm_back(second_grad, unit_two_h, scale_two_h, vec_all[10:11])
    mix_half = resid_grad.astype(BF)
    mix_grad = ordered(mix_half, flip(mix_half, "c"), core, 0).reshape(length, width)

    cos_t, sin_t = tables[0], tables[1]
    query_f, key_f, value_f = [
        heads[:, i * channels : (i + 1) * channels].astype(F32) for i in range(3)
    ]
    padded = jnp.pad(key_f, ((tap_count - 1, 0), (0, 0)))
    convolved, shifted = convolved.astype(F32), shifted.astype(F32)
    prod_re, prod_im, kern_re, kern_im = [
        array.astype(F32) for array in (prod_re, prod_im, kern_re, kern_im)
    ]
    products = shifted * value_f
    head_grad = mm_nt(mix_grad, out_own).astype(BF).astype(F32)
    query_grad = (head_grad * convolved).astype(BF)
    conv_grad = head_grad * query_f
    conv_low = conv_grad.astype(BF)
    skip_grad = jnp.sum(conv_grad * products, axis=0)
    grad_re = mm(cos_t, conv_low)
    grad_im = mm(sin_t, conv_low)
    out_grad = mm_tn(mixed_heads, mix_grad).astype(BF)
    q_grad = mm_tn(first_rows, query_grad).astype(BF)
    back_re = (grad_re * kern_re + grad_im * kern_im).astype(BF)
    back_im = (grad_im * kern_re - grad_re * kern_im).astype(BF)
    lag_re = (grad_re * prod_re + grad_im * prod_im).astype(BF)
    lag_im = (grad_im * prod_re - grad_re * prod_im).astype(BF)
    lag_grad = (mm_tn(lag_re, cos_t) + mm_tn(lag_im, sin_t)) * (1.0 / length)
    lag_sum = lag_grad.astype(BF).reshape(ring, 2, 1, 2, 1, rows, length)
    back = (mm_tn(cos_t, back_re) + mm_tn(sin_t, back_im)) * (1.0 / length)
    product_grad = back + skip * conv_grad
    out_sum = out_grad.reshape(ring, 2, 1, 2, 1, rows, width)
    q_sum = q_grad.reshape(ring, 2, 2, 2, 1, rows, channels)
    shifted_grad = product_grad * value_f
    value_grad = (product_grad * shifted).astype(BF)
    padded_grad = jnp.pad(shifted_grad, ((0, tap_count - 1), (0, 0)))
    key_grad = jnp.zeros_like(key_f)
    tap_rows = []
    for tap in range(tap_count):
        at = tap_count - 1 - tap
        key_grad = key_grad + padded_grad[tap : tap + length] * taps[tap : tap + 1]
        tap_rows.append(jnp.sum(shifted_grad * padded[at : at + length], axis=0))
    key_grad = key_grad.astype(BF)
    kv_grad = jnp.concatenate([key_grad, value_grad], axis=1)
    kv_sum = mm_tn(first_rows, kv_grad).astype(BF).reshape(ring, 2, 2, 2, 1, rows, 2 * channels)
    kv_sum, q_sum, out_sum, lag_sum, kv_grad, *ffn_one = fence(
        kv_sum, q_sum, out_sum, lag_sum, kv_grad, *ffn_one
    )

    lag_width = length // 8
    ffn_two = pair_two(down_sum, up_sum, ffn_one, ring)
    outq_one = direct_one((q_sum, out_sum, lag_sum), ring, lag_width)
    first_part = mm_nt(jnp.concatenate([query_grad, kv_grad], axis=1), w_qkv)
    first_other = flip(theirs(first_part).astype(BF), "c").astype(F32)
    first_grad = mine(first_part) + first_other
    unit_one_h, scale_one_h = norm_stats(token_half.astype(F32))
    gain_one_grad = jnp.sum(first_grad * unit_one_h, axis=0)
    bias_one_grad = jnp.sum(first_grad, axis=0)
    token_grad = resid_grad + norm_back(first_grad, unit_one_h, scale_one_h, vec_all[8:9])
    token_grad = token_grad.astype(BF)

    vec_grads = jnp.stack(
        [gain_one_grad, bias_one_grad, gain_two_grad, bias_two_grad, down_bias_grad]
    )
    vec_grads = vec_grads.reshape(5, groups, 2, 2 * rows)
    vec_keep = lax.dynamic_index_in_dim(vec_grads, core, 2, keepdims=False)
    vec_send = lax.dynamic_index_in_dim(vec_grads, 1 - core, 2, keepdims=False)
    vec_sum = (vec_keep + flip(vec_send, "c")).reshape(5, channels)
    small = jnp.concatenate([vec_sum, jnp.stack(tap_rows), skip_grad[None]])
    small = jnp.concatenate([small.T, up_bias_grad.reshape(channels, -1)], axis=1)
    small = jnp.pad(small, ((0, 0), (0, 128 - small.shape[1]))).astype(BF)
    small_sum = small.reshape(ring, 2, 1, 2, 1, rows, 128)
    small_sum, token_grad, *ffn_two = fence(small_sum, token_grad, *ffn_two)

    ffn_held = pair_three(down_sum, up_sum, ffn_one, ffn_two, ring, width)
    ffn_three = ring_send(ffn_held, ring)
    kv_one = direct_one((kv_sum, small_sum), ring, 128)
    token_grad = swap_cy(token_grad).astype(F32)[None]
    ffn_held, *outq_one = fence(ffn_held, *outq_one)
    outq_held = direct_two((q_sum, out_sum, lag_sum), outq_one, ring, lag_width)
    outq_three = ring_send(outq_held, ring)
    outq_held, *late = fence(outq_held, *kv_one, *ffn_three)
    kv_one, ffn_three = late[:3], late[3:]
    kv_held = direct_two((kv_sum, small_sum), kv_one, ring, 128)
    kv_three = ring_send(kv_held, ring)
    ffn_s = ring_sum(ffn_held, ffn_three)
    down_pieces = up_rows // rows
    down_s = ffn_s[:down_pieces].reshape(up_rows, width)
    up_half = (ffn_s.shape[0] - down_pieces) // 2
    up_s = jnp.stack([join(ffn_s[down_pieces : down_pieces + up_half]), join(ffn_s[down_pieces + up_half :])])
    up_s = merge_columns(up_s, core, groups)
    outq_s = ring_sum(outq_held, outq_three)
    q_pieces = channels // lag_width
    query_s = merge_columns(
        jnp.stack([join(outq_s[:q_pieces]), join(outq_s[q_pieces : 2 * q_pieces])]), core, groups
    )
    out_s = join(outq_s[2 * q_pieces : 4 * q_pieces])
    lag_s = join(outq_s[4 * q_pieces :])
    coef_s, rate_s = ssm_kernel_grads(lag_s, ssm_coef.astype(F32), ssm_rate.astype(F32))
    up_s, down_s, query_s, out_s, coef_s, rate_s, token_grad, *kv_three = fence(
        up_s, down_s, query_s, out_s, coef_s, rate_s, token_grad, *kv_three
    )
    kv_s = ring_sum(kv_held, kv_three)
    pieces = channels // 128

    def heads_of(first):
        both = [join(kv_s[(first + i) * pieces : (first + i + 1) * pieces]) for i in range(2)]
        return jnp.concatenate(both, axis=0)

    heads_s = merge_columns(jnp.stack([heads_of(0), heads_of(2)]), core, groups)
    key_s, value_s = heads_s[:rows], heads_s[rows:]
    small = kv_s[4 * pieces]
    vec_s = small[:, :5].T
    taps_s = small[:, 5 : 5 + tap_count]
    skip_s = small[:, 5 + tap_count]
    up_bias_s = small[:, 6 + tap_count : 6 + tap_count + up_rows // rows].reshape(up_rows)
    return (
        mixed,
        token_grad,
        vec_s[0],
        vec_s[1],
        query_s,
        key_s,
        value_s,
        taps_s,
        coef_s,
        rate_s,
        skip_s,
        out_s,
        vec_s[2],
        vec_s[3],
        up_s,
        up_bias_s,
        down_s,
        vec_s[4],
    )


def solution(mesh):
    dp_size, seq_size = mesh.devices.shape
    ring = dp_size // 4
    grid = Mesh(mesh.devices.reshape(ring, 2, 2, seq_size), ("r", "x", "c", "y"))
    dp = ("r", "x", "c")
    act = P(dp, "y", None)
    vec = P(dp + ("y",))
    mat = P(dp + ("y",), None)
    return jax.shard_map(
        functools.partial(body, ring),
        mesh=grid,
        in_specs=(
            act, P(dp), act, vec, vec, mat, mat, mat, mat, mat, mat, vec, mat, vec, vec, mat, vec, mat, vec,
        ),
        out_specs=(
            act, act, vec, vec, mat, mat, mat, mat, mat, mat, vec, mat, vec, vec, mat, vec, mat, vec,
        ),
        check_vma=False,
    )
```

```python
import functools
import math

import jax
import jax.numpy as jnp
from jax import lax
from jax.experimental import pallas as pl
from jax.experimental.pallas import tpu as pltpu
from jax.sharding import Mesh, PartitionSpec as P

EPS = 1e-05
BF = jnp.bfloat16
F32 = jnp.float32
SQRT_2_PI = math.sqrt(2.0 / math.pi)
MISC = ("r", "x", "y")


def flip(value, axis):
    return lax.ppermute(value, axis, [(0, 1), (1, 0)])


def ordered(mine, other, place, axis):
    first = jnp.where(place == 0, mine, other)
    second = jnp.where(place == 0, other, mine)
    return jnp.stack([first, second], axis=axis)


def swap_cy(value):
    moved = lax.ppermute(value, ("c", "y"), [(1, 2), (2, 1)])
    return jnp.where(lax.axis_index("c") == lax.axis_index("y"), value, moved)


def shift_ring(value, distance, ring):
    return lax.ppermute(value, "r", [(i, (i + distance) % ring) for i in range(ring)])


def flip_xy(value):
    return lax.ppermute(value, ("x", "y"), [(i, 3 - i) for i in range(4)])


def place(whole, part, starts):
    return lax.dynamic_update_slice(whole, part, starts)


def gather_ring(block, ring):
    here = lax.axis_index("r")
    rest = (0,) * block.ndim
    whole = jnp.zeros((ring,) + block.shape, block.dtype)
    whole = place(whole, block[None], (here,) + rest)
    for distance in range(1, ring):
        moved = shift_ring(block, distance, ring)
        whole = place(whole, moved[None], (lax.rem(here - distance + ring, ring),) + rest)
    return whole


def ring_pieces(block, ring):
    blocks = [block] + [shift_ring(block, d, ring) for d in range(1, ring)]
    return tuple(jnp.stack([part[half] for part in blocks]) for half in range(2))


def near_one(halves):
    return flip(halves[0], "y"), flip(halves[1], "x")


def near_two(halves, moved):
    first = flip(jnp.concatenate([halves[0], moved[0]]), "x")
    second = flip(jnp.concatenate([halves[1], moved[1]]), "y")
    return first, second


def chip_ids():
    return jnp.stack([lax.axis_index("r"), lax.axis_index("x"), lax.axis_index("y")]).astype(jnp.int32)


def grant(*blocks):
    total = 0
    for shape, kind in blocks:
        rows = -(-shape[-2] // 16) * 16
        total += math.prod(shape[:-2]) * rows * shape[-1] * jnp.dtype(kind).itemsize
    return pltpu.CompilerParams(vmem_limit_bytes=2 * total + (2 << 20))


def assemble_body(write, ids, *refs):
    ins, outs = refs[:8], refs[8:]
    for half in range(2):
        for index in range(4):
            x = lax.rem(ids[1] + index // 2, 2)
            y = lax.rem(ids[2] + index % 2, 2)
            write(outs, ins[4 * half + index], half, x, y)


def assemble(halves, one, two, ring, shapes, write, name):
    sources = (
        (halves[0], 0), (one[0], 0), (two[0], 0), (two[0], ring),
        (halves[1], 0), (two[1], 0), (one[1], 0), (two[1], ring),
    )
    tail = halves[0].shape[1:]
    zeros = (0,) * len(tail)
    specs = [
        pl.BlockSpec((None,) + tail, lambda i, ids, base=base: (i + base,) + zeros) for _, base in sources
    ]
    moved = 32 * math.prod(tail) * ring
    return pl.pallas_call(
        functools.partial(assemble_body, write),
        out_shape=tuple(jax.ShapeDtypeStruct(shape, halves[0].dtype) for shape in shapes),
        grid_spec=pltpu.PrefetchScalarGridSpec(
            num_scalar_prefetch=1,
            grid=(ring,),
            in_specs=specs,
            out_specs=tuple(
                pl.BlockSpec(
                    (None,) + shape[1:],
                    lambda i, ids, rank=len(shape): (lax.rem(ids[0] + ring - i, ring),) + (0,) * (rank - 1),
                )
                for shape in shapes
            ),
        ),
        compiler_params=grant(*[(tail, BF)] * 8, *[(shape[1:], BF) for shape in shapes]),
        cost_estimate=pl.CostEstimate(flops=0, bytes_accessed=moved, transcendentals=0),
        name=name,
    )(chip_ids(), *[array for array, _ in sources])


def write_heads(outs, part, half, x, y):
    outs[0][x, half, y] = part[0]


def write_up(outs, part, half, x, y):
    lanes = part.shape[-1]
    count = part.shape[0] - 1
    for index in range(count):
        outs[0][x, half, y, :, index * lanes : (index + 1) * lanes] = part[index]
    outs[1][x, y, :, half * lanes : (half + 1) * lanes] = part[count]


def here_x(i, ids):
    return ids[1]


def other_x(i, ids):
    return 1 - ids[1]


def here_y(i, ids):
    return ids[2]


def other_y(i, ids):
    return 1 - ids[2]


def step_r(i, ids):
    return i


def turn_r(ring):
    return lambda i, ids: lax.rem(ids[0] + i, ring)


def sums_body(plan, ids, *refs):
    ins, outs = refs[: len(refs) - len(plan)], refs[len(refs) - len(plan) :]
    for out, columns in zip(outs, plan):
        width = out.shape[2]
        at = 0
        for terms in columns:
            first = ins[terms[0]]
            cores, extra, _, lanes = first.shape
            index = 0
            for core in range(cores):
                for more in range(extra):
                    for low in range(0, lanes, width):
                        total = None
                        for term in terms:
                            ref = ins[term]
                            if len(ref.shape) == 4:
                                value = ref[core, more, :, low : low + width]
                            else:
                                value = ref[at + index]
                            value = value.astype(F32)
                            total = value if total is None else total + value
                        out[at + index] = total.astype(out.dtype)
                        index += 1
            at += index


def sums(ring, jobs):
    arrays, specs, plan, shapes = [], [], [], []
    for width, columns in jobs:
        pieces = 0
        numbers = []
        for terms in columns:
            mine = []
            for count, (array, picks) in enumerate(terms):
                tail = array.shape[len(picks) :]
                block = tuple(
                    size if pick is None else None for size, pick in zip(array.shape, picks)
                ) + tail

                def index_map(i, ids, picks=picks, tail=tail):
                    return tuple(0 if pick is None else pick(i, ids) for pick in picks) + (0,) * len(tail)

                if count == 0:
                    held = [size for size in block if size is not None]
                    pieces += held[0] * held[1] * (held[3] // width)
                mine.append(len(arrays))
                arrays.append(array)
                specs.append(pl.BlockSpec(block, index_map))
            numbers.append(mine)
        plan.append(numbers)
        rows = columns[0][0][0].shape[-2]
        shapes.append(jax.ShapeDtypeStruct((ring, pieces, rows, width), BF))
    moved = sum(2 * math.prod(shape.shape) * 2 for shape in shapes)
    return pl.pallas_call(
        functools.partial(sums_body, plan),
        out_shape=tuple(shapes),
        grid_spec=pltpu.PrefetchScalarGridSpec(
            num_scalar_prefetch=1,
            grid=(ring,),
            in_specs=specs,
            out_specs=tuple(
                pl.BlockSpec((None,) + shape.shape[1:], lambda i, ids: (i, 0, 0, 0)) for shape in shapes
            ),
        ),
        compiler_params=grant(
            *[
                (tuple(size for size in spec.block_shape if size is not None), BF)
                for spec in specs
            ],
            *[(shape.shape[1:], BF) for shape in shapes],
        ),
        cost_estimate=pl.CostEstimate(flops=0, bytes_accessed=2 * moved, transcendentals=0),
        name="sums",
    )(chip_ids(), *[pltpu.with_memory_space_constraint(array, pltpu.HBM) for array in arrays])


def take(parts, axis, index):
    return lax.dynamic_index_in_dim(parts, index, axis, keepdims=False)


def pair_one(y_first, x_first):
    x, y = lax.axis_index("x"), lax.axis_index("y")
    return flip(take(y_first, 3, 1 - y), "y"), flip(take(x_first, 1, 1 - x), "x")


def pair_two(y_first, x_first, moved, ring):
    one = [
        (y_first, (step_r, other_x, None, here_y)),
        (moved[0], (step_r, other_x, None)),
    ]
    two = [
        (x_first, (step_r, here_x, None, other_y)),
        (moved[1], (step_r, None, other_y)),
    ]
    send_one, send_two = sums(ring, [(y_first.shape[-1], [one]), (x_first.shape[-1], [two])])
    shape_one = (ring, y_first.shape[2]) + y_first.shape[4:]
    shape_two = (ring, x_first.shape[2]) + x_first.shape[4:]
    return flip(send_one, "x").reshape(shape_one), flip(send_two, "y").reshape(shape_two)


def pair_three(y_first, x_first, moved_one, moved_two, ring, width):
    turn = turn_r(ring)
    one = [
        (y_first, (turn, here_x, None, here_y)),
        (moved_one[0], (turn, here_x, None)),
        (moved_two[0], (turn, None)),
    ]
    two = [
        (x_first, (turn, here_x, None, here_y)),
        (moved_one[1], (turn, None, here_y)),
        (moved_two[1], (turn, None)),
    ]
    return sums(ring, [(width, [one, two])])[0]


def direct_one(arrays, ring, width):
    spots = ((here_x, other_y), (other_x, here_y), (other_x, other_y))
    along_y, along_x, across = sums(
        ring, [(width, [[(array, (step_r, x, None, y))] for array in arrays]) for x, y in spots]
    )
    return flip(along_y, "y"), flip(along_x, "x"), flip_xy(across)


def direct_two(arrays, moved, ring, width):
    turn = turn_r(ring)
    columns = [
        [(array, (turn, here_x, None, here_y))] + [(part, (turn,)) for part in moved] for array in arrays
    ]
    return sums(ring, [(width, columns)])[0]


def ring_send(held, ring):
    return tuple(shift_ring(held[distance], distance, ring) for distance in range(1, ring))


def ring_sum(held, moved):
    total = held[0].astype(F32)
    for part in moved:
        total = total + part.astype(F32)
    return total


def join(pieces):
    return jnp.concatenate([pieces[i] for i in range(pieces.shape[0])], axis=1)


def scatter_near(pick):
    x, y = lax.axis_index("x"), lax.axis_index("y")
    total = pick(x, y).astype(F32)
    total = total + flip(pick(x, 1 - y), "y").astype(F32)
    total = total + flip(pick(1 - x, y), "x").astype(F32)
    return total + flip_xy(pick(1 - x, 1 - y)).astype(F32)


def gather_quad(block):
    x, y = lax.axis_index("x"), lax.axis_index("y")
    parts = ((block, x, y), (flip(block, "y"), x, 1 - y), (flip(block, "x"), 1 - x, y), (flip_xy(block), 1 - x, 1 - y))
    full = jnp.zeros((2, 2) + block.shape, block.dtype)
    for part, at_x, at_y in parts:
        full = place(full, part[None, None], (at_x, at_y) + (0,) * block.ndim)
    return full


def fence(*values):
    return lax.optimization_barrier(values)


def merge_columns(parts, core, groups):
    keep = lax.dynamic_index_in_dim(parts, core, 0, keepdims=False)
    send = lax.dynamic_index_in_dim(parts, 1 - core, 0, keepdims=False)
    count, cols = keep.shape
    other = flip(send.astype(BF), "c").astype(F32)
    grid = ordered(
        keep.reshape(count, groups, -1), other.reshape(count, groups, -1), core, 2
    )
    return grid.reshape(count, 2 * cols)


def mm(left, right):
    return jnp.dot(left, right, preferred_element_type=F32)


def mm_tn(left, right):
    return lax.dot_general(
        left, right, (((0,), (0,)), ((), ())), preferred_element_type=F32
    )


def mm_nt(left, right):
    return lax.dot_general(
        left, right, (((1,), (1,)), ((), ())), preferred_element_type=F32
    )


def norm_stats(values):
    mean = jnp.mean(values, axis=-1, keepdims=True)
    centred = values - mean
    variance = jnp.mean(centred * centred, axis=-1, keepdims=True)
    scale = lax.rsqrt(variance + EPS)
    return centred * scale, scale


def norm_back(grad, unit, scale, gain):
    inner = grad * gain
    mean_one = jnp.mean(inner, axis=-1, keepdims=True)
    mean_two = jnp.mean(inner * unit, axis=-1, keepdims=True)
    return scale * (inner - mean_one - unit * mean_two)


def tables_body(token_ref, cos_ref, sin_ref, cos_turn_ref, sin_turn_ref, cos_high_ref, sin_high_ref):
    length = cos_ref.shape[0]
    part = 32
    blocks = length // part
    step = math.pi / (2.0 * length)
    period = 4 * length
    rows = lax.broadcasted_iota(jnp.int32, (part, length), 0)
    cols = lax.broadcasted_iota(jnp.int32, (part, length), 1)

    def turns(count):
        angle = (count & (period - 1)).astype(F32) * step
        return jnp.cos(angle), jnp.sin(angle)

    def fill(high, low, cos_out, sin_out):
        cos_high_ref[...], sin_high_ref[...] = turns(high)
        cos_low, sin_low = turns(low)

        def put(block, carry):
            ch, sh = cos_high_ref[pl.ds(block, 1), :], sin_high_ref[pl.ds(block, 1), :]
            at = pl.ds(pl.multiple_of(block * part, part), part)
            cos_out[at, :] = (ch * cos_low - sh * sin_low).astype(BF)
            sin_out[at, :] = (sh * cos_low + ch * sin_low).astype(BF)
            return carry

        lax.fori_loop(0, blocks, put, 0)

    fill(2 * part * rows * cols, (2 * rows + 1) * cols, cos_ref, sin_ref)
    fill(part * rows * (2 * cols + 1), rows * (2 * cols + 1), cos_turn_ref, sin_turn_ref)


def dft_tables(length, token):
    table = jax.ShapeDtypeStruct((length, length), BF)
    return pl.pallas_call(
        tables_body,
        out_shape=(table,) * 4,
        in_specs=[pl.BlockSpec(memory_space=pl.ANY)],
        out_specs=tuple(in_vmem(4)),
        scratch_shapes=[pltpu.VMEM((32, length), F32)] * 2,
        cost_estimate=pl.CostEstimate(flops=7 * 10**9, bytes_accessed=8 * length * length, transcendentals=0),
        compiler_params=pltpu.CompilerParams(vmem_limit_bytes=4 << 20),
        name="dft_tables",
    )(token)


def norm_body(core_ref, mine_ref, other_ref, vec_ref, all_ref, rows_ref):
    half = mine_ref.shape[0]
    step = 128
    for index, ref in enumerate((mine_ref, other_ref)):
        place = lax.rem(core_ref[0] + index, 2) * half

        def put(block_id, carry):
            block = ref[pl.ds(pl.multiple_of(block_id * step, step), step), :]
            at = pl.ds(pl.multiple_of(place + block_id * step, step), step)
            all_ref[at, :] = block
            unit, _ = norm_stats(block.astype(F32))
            rows_ref[at, :] = (unit * vec_ref[8:9, :] + vec_ref[9:10, :]).astype(BF)
            return carry

        lax.fori_loop(0, half // step, put, 0)


def first_norm(mine, other, core, vectors):
    half, width = mine.shape
    wide = jax.ShapeDtypeStruct((2 * half, width), BF)
    return pl.pallas_call(
        norm_body,
        out_shape=(wide, wide),
        in_specs=[pl.BlockSpec(memory_space=pltpu.SMEM)] + in_vmem(3),
        out_specs=tuple(in_vmem(2)),
        cost_estimate=pl.CostEstimate(flops=3 * 10**9, bytes_accessed=4 * half * width, transcendentals=0),
        compiler_params=pltpu.CompilerParams(vmem_limit_bytes=4 << 20),
        name="first_norm",
    )(core.astype(jnp.int32).reshape(1), mine, other, vectors)


def in_vmem(count):
    return [pl.BlockSpec(memory_space=pltpu.VMEM)] * count


def kernel_body(part, coef_ref, rate_ref, out_ref, high_ref, low_ref):
    states = coef_ref.shape[0]
    length = out_ref.shape[0]
    blocks = length // part
    lanes = out_ref.shape[1]
    high_ids = lax.broadcasted_iota(jnp.int32, (blocks, lanes), 0).astype(F32) * (part / length)
    low_ids = lax.broadcasted_iota(jnp.int32, (part, lanes), 0).astype(F32) * (1.0 / length)

    def fill(state, carry):
        rate = rate_ref[pl.ds(state, 1), :]
        coef = coef_ref[pl.ds(state, 1), :] * (length ** (-0.5))
        high_ref[state] = coef * jnp.exp(-rate * high_ids)
        low_ref[state] = jnp.exp(-rate * low_ids)
        return carry

    lax.fori_loop(0, states, fill, 0)
    for start in range(0, blocks, 8):

        def add(state, sums):
            low = low_ref[state]
            return tuple(
                total + high_ref[state, pl.ds(start + index, 1), :] * low
                for index, total in enumerate(sums)
            )

        zero = jnp.zeros((part, lanes), F32)
        sums = lax.fori_loop(0, states, add, (zero,) * 8, unroll=4)
        for index, total in enumerate(sums):
            out_ref[pl.ds((start + index) * part, part), :] = total.astype(out_ref.dtype)


def spectrum_body(part, states, params_ref, cos_ref, sin_ref, re_ref, im_ref, kernel_ref, high_ref, low_ref, coef_part, rate_part):
    length, channels = kernel_ref.shape
    for start in range(0, channels, 128):
        lanes = pl.ds(start, 128)
        coef_part[...] = params_ref[0:states, lanes]
        rate_part[...] = params_ref[states : 2 * states, lanes]
        kernel_body(part, coef_part, rate_part, kernel_ref.at[:, lanes], high_ref, low_ref)

    def put(block, carry):
        rows = pl.ds(pl.multiple_of(block * 256, 256), 256)
        re_ref[rows, :] = mm(cos_ref[rows, :], kernel_ref[...]).astype(BF)
        im_ref[rows, :] = mm(sin_ref[rows, :], kernel_ref[...]).astype(BF)
        return carry

    lax.fori_loop(0, length // 256, put, 0)


def ssm_spectrum(params, states, cos_t, sin_t, length):
    channels = params.shape[1]
    part = 32
    return pl.pallas_call(
        functools.partial(spectrum_body, part, states),
        out_shape=(jax.ShapeDtypeStruct((length, channels), BF),) * 2,
        in_specs=in_vmem(3),
        out_specs=tuple(in_vmem(2)),
        scratch_shapes=[
            pltpu.VMEM((length, channels), BF),
            pltpu.VMEM((states, length // part, 128), F32),
            pltpu.VMEM((states, part, 128), F32),
            pltpu.VMEM((states, 128), F32),
            pltpu.VMEM((states, 128), F32),
        ],
        cost_estimate=pl.CostEstimate(
            flops=600 * length * states * channels, bytes_accessed=2 * length * channels * 4, transcendentals=0
        ),
        compiler_params=pltpu.CompilerParams(vmem_limit_bytes=8 << 20),
        name="ssm_spectrum",
    )(params, cos_t, sin_t)


def conv_body(
    first, tap_count, heads_ref, kern_re_ref, kern_im_ref, params_ref, cos_ref, sin_ref, cos_turn_ref, sin_turn_ref,
    mixed_ref, conv_ref, shifted_ref, prod_re_ref, prod_im_ref,
    products_ref, low_ref, spec_re_ref, spec_im_ref,
):
    length, channels = mixed_ref.shape
    step = 128
    last = first + tap_count

    def shift(rows, keys):
        shifted = keys[8:] * params_ref[first : first + 1, :]
        for tap in range(1, tap_count):
            shifted = shifted + keys[8 - tap : 8 - tap + step] * params_ref[first + tap : first + tap + 1, :]
        shifted_ref[rows, :] = shifted.astype(BF)
        products = shifted * heads_ref[rows, 2 * channels : 3 * channels].astype(F32)
        products_ref[rows, :] = products
        low_ref[rows, :] = products.astype(BF)

    keys = heads_ref[0:step, channels : 2 * channels].astype(F32)
    shift(pl.ds(0, step), jnp.concatenate([jnp.zeros((8, channels), F32), keys], axis=0))

    def shift_block(block, carry):
        before = pl.ds(pl.multiple_of(block * step - 8, 8), step + 8)
        shift(
            pl.ds(pl.multiple_of(block * step, step), step),
            heads_ref[before, channels : 2 * channels].astype(F32),
        )
        return carry

    lax.fori_loop(1, length // step, shift_block, 0)

    def spectrum(block, carry):
        rows = pl.ds(pl.multiple_of(block * 256, 256), 256)
        prod_re = mm(cos_ref[rows, :], low_ref[...])
        prod_im = mm(sin_ref[rows, :], low_ref[...])
        kern_re, kern_im = kern_re_ref[rows, :].astype(F32), kern_im_ref[rows, :].astype(F32)
        prod_re_ref[rows, :] = prod_re.astype(BF)
        prod_im_ref[rows, :] = prod_im.astype(BF)
        spec_re_ref[rows, :] = (prod_re * kern_re - prod_im * kern_im).astype(BF)
        spec_im_ref[rows, :] = (prod_re * kern_im + prod_im * kern_re).astype(BF)
        return carry

    lax.fori_loop(0, length // 256, spectrum, 0)

    def convolve(block, carry):
        rows = pl.ds(pl.multiple_of(block * 256, 256), 256)
        conv = mm(cos_turn_ref[rows, :], spec_re_ref[...]) + mm(sin_turn_ref[rows, :], spec_im_ref[...])
        conv = conv * (1.0 / length) + params_ref[last : last + 1, :] * products_ref[rows, :]
        conv_ref[rows, :] = conv.astype(BF)
        mixed_ref[rows, :] = (heads_ref[rows, 0:channels].astype(F32) * conv).astype(BF)
        return carry

    lax.fori_loop(0, length // 256, convolve, 0)


def conv_forward(heads, kern_re, kern_im, params, first, tap_count, tables):
    length, channels = kern_re.shape
    wide = jax.ShapeDtypeStruct((length, channels), BF)
    return pl.pallas_call(
        functools.partial(conv_body, first, tap_count),
        out_shape=(wide,) * 5,
        in_specs=in_vmem(8),
        out_specs=tuple(in_vmem(5)),
        scratch_shapes=[
            pltpu.VMEM((length, channels), F32),
            pltpu.VMEM((length, channels), BF),
            pltpu.VMEM((length, channels), BF),
            pltpu.VMEM((length, channels), BF),
        ],
        cost_estimate=pl.CostEstimate(
            flops=24 * length * length * channels, bytes_accessed=16 * length * channels, transcendentals=0
        ),
        compiler_params=pltpu.CompilerParams(vmem_limit_bytes=10 << 20),
        name="conv_forward",
    )(heads, kern_re, kern_im, params, *tables)


def ssm_kernel_grads(grad, coef, rate):
    length = grad.shape[1]
    times = lax.broadcasted_iota(jnp.int32, (1, 1, length), 2).astype(F32) * (1.0 / length)
    weighted = grad[:, None] * jnp.exp(-rate[:, :, None] * times)
    scale = length ** (-0.5)
    return jnp.sum(weighted, axis=2) * scale, -coef * jnp.sum(weighted * times, axis=2) * scale


def row_block(cols, kind_rows=256):
    return pl.BlockSpec((kind_rows, cols), lambda i: (i, 0))


def whole_block(rows, cols):
    return pl.BlockSpec((rows, cols), lambda i: (0, 0), pipeline_mode=pl.Buffered(1))


def turned_block(cols, steps):
    return pl.BlockSpec((256, cols), lambda i, core: (lax.rem(i + steps // 2 * (1 - core[0]), steps), 0))


def same_block(rows, cols):
    return pl.BlockSpec((rows, cols), lambda i, core: (0, 0), pipeline_mode=pl.Buffered(1))


def half_blocks(cols, steps):
    theirs = pl.BlockSpec((256, cols), lambda i, core: (jnp.minimum(i, steps // 2 - 1), 0))
    mine = pl.BlockSpec((256, cols), lambda i, core: (jnp.maximum(i - steps // 2, 0), 0))
    return theirs, mine


def put_half(theirs_ref, mine_ref, theirs, mine):
    first = pl.program_id(0) < pl.num_programs(0) // 2

    @pl.when(first)
    def _():
        theirs_ref[...] = theirs.astype(theirs_ref.dtype)

    @pl.when(jnp.logical_not(first))
    def _():
        mine_ref[...] = mine.astype(mine_ref.dtype)


def ffn_forward_body(
    core_ref, resid_ref, vec_ref, up_ref, up_bias_ref, down_ref,
    rows_ref, act_ref, slope_ref, theirs_ref, mine_ref,
):
    resid = resid_ref[...]
    unit, _ = norm_stats(resid)
    second = (unit * vec_ref[10:11, :] + vec_ref[11:12, :]).astype(BF)
    rows_ref[...] = second
    pre = mm(second, up_ref[...]) + up_bias_ref[...]
    square = pre * pre
    bend = jnp.tanh(pre * (SQRT_2_PI + SQRT_2_PI * 0.044715 * square))
    half = 0.5 * pre
    act = (half + half * bend).astype(BF)
    act_ref[...] = act
    steep = SQRT_2_PI + 3.0 * SQRT_2_PI * 0.044715 * square
    slope_ref[...] = (0.5 + 0.5 * bend + half * (1.0 - bend * bend) * steep).astype(BF)
    part = mm(act, down_ref[...])
    put_half(theirs_ref, mine_ref, part, part + resid + vec_ref[12:13, :])


def ffn_forward(core, resid, vectors, up, up_bias, down):
    length, width = resid.shape
    hidden = up.shape[1]
    steps = length // 256
    return pl.pallas_call(
        ffn_forward_body,
        out_shape=(
            jax.ShapeDtypeStruct((length, width), BF),
            jax.ShapeDtypeStruct((length, hidden), BF),
            jax.ShapeDtypeStruct((length, hidden), BF),
            jax.ShapeDtypeStruct((length // 2, width), BF),
            jax.ShapeDtypeStruct((length // 2, width), F32),
        ),
        grid_spec=pltpu.PrefetchScalarGridSpec(
            num_scalar_prefetch=1,
            grid=(steps,),
            in_specs=[
                turned_block(width, steps),
                same_block(vectors.shape[0], width),
                same_block(width, hidden),
                same_block(1, hidden),
                same_block(hidden, width),
            ],
            out_specs=(
                turned_block(width, steps),
                turned_block(hidden, steps),
                turned_block(hidden, steps),
            )
            + half_blocks(width, steps),
        ),
        compiler_params=pltpu.CompilerParams(vmem_limit_bytes=28 << 20),
        cost_estimate=pl.CostEstimate(
            flops=8 * length * width * hidden, bytes_accessed=12 * length * width, transcendentals=0
        ),
        name="ffn_forward",
    )(core, resid, vectors, up, up_bias, down)


def ffn_backward_body(core_ref, grad_ref, slope_ref, up_ref, down_ref, pre_ref, bias_ref, theirs_ref, mine_ref):
    act_grad = mm_nt(grad_ref[...], down_ref[...])
    pre = (act_grad * slope_ref[...].astype(F32)).astype(BF)
    pre_ref[...] = pre
    part = mm_nt(pre, up_ref[...])
    put_half(theirs_ref, mine_ref, part, part)

    @pl.when(pl.program_id(0) == 0)
    def _():
        bias_ref[...] = jnp.zeros_like(bias_ref)

    bias_ref[...] += jnp.sum(pre.astype(F32), axis=0, keepdims=True)


def ffn_backward(core, grad, slope, up, down):
    length, width = grad.shape
    hidden = up.shape[1]
    steps = length // 256
    return pl.pallas_call(
        ffn_backward_body,
        out_shape=(
            jax.ShapeDtypeStruct((length, hidden), BF),
            jax.ShapeDtypeStruct((1, hidden), F32),
            jax.ShapeDtypeStruct((length // 2, width), BF),
            jax.ShapeDtypeStruct((length // 2, width), F32),
        ),
        grid_spec=pltpu.PrefetchScalarGridSpec(
            num_scalar_prefetch=1,
            grid=(steps,),
            in_specs=[
                turned_block(width, steps),
                turned_block(hidden, steps),
                same_block(width, hidden),
                same_block(hidden, width),
            ],
            out_specs=(turned_block(hidden, steps), pl.BlockSpec((1, hidden), lambda i, core: (0, 0)))
            + half_blocks(width, steps),
        ),
        compiler_params=pltpu.CompilerParams(vmem_limit_bytes=24 << 20),
        cost_estimate=pl.CostEstimate(
            flops=6 * length * width * hidden, bytes_accessed=12 * length * width, transcendentals=0
        ),
        name="ffn_backward",
    )(core, grad, slope, up, down)


def body(
    ring,
    tokens,
    lengths,
    cotangent,
    norm1_gain,
    norm1_bias,
    w_query,
    w_key,
    w_value,
    shift_taps,
    ssm_coef,
    ssm_rate,
    skip_gain,
    w_out,
    norm2_gain,
    norm2_bias,
    w_up,
    up_bias,
    w_down,
    down_bias,
):
    core = lax.axis_index("c")
    groups = 2 * ring
    _, block_len, width = tokens.shape
    length = 2 * block_len
    rows = w_query.shape[0]
    up_rows = up_bias.shape[0]
    hidden = w_up.shape[1]
    states = ssm_coef.shape[1]
    tap_count = shift_taps.shape[1]
    channels = width // 2

    def columns(weight, which):
        grid = weight.reshape(rows, groups, 2, -1)
        return jnp.where(which == 0, grid[:, :, 0], grid[:, :, 1]).reshape(rows, -1)

    down_own = lax.all_gather(w_down, MISC, axis=0, tiled=True)
    matrices = (w_query, w_key, w_value, w_up)
    keep = jnp.concatenate([columns(w, core) for w in matrices], axis=1)
    send = jnp.concatenate([columns(w, 1 - core) for w in matrices], axis=1)
    norm1_gain, ssm_coef, ssm_rate, send = fence(norm1_gain, ssm_coef, ssm_rate, send)
    packed = ordered(keep, flip(send, "c"), core, 0)
    first_pack = packed[:, None, :, : 3 * channels]
    first_ring = ring_pieces(first_pack, ring)
    up_lanes = packed[:, :, 3 * channels :]
    up_pack = jnp.stack(
        [up_lanes[:, :, i * channels : (i + 1) * channels] for i in range(hidden // width)]
        + [jnp.stack([w_out[:, :channels], w_out[:, channels:]])],
        axis=1,
    )

    vectors = jnp.stack(
        [skip_gain, skip_gain, skip_gain, skip_gain, norm1_gain, norm1_bias, norm2_gain, norm2_bias, down_bias]
    )
    misc = jnp.concatenate(
        [ssm_coef, ssm_rate, shift_taps, vectors.T], axis=1
    )
    bias_row = jnp.pad(up_bias, (0, 256 - up_rows)).reshape(1, 256)
    misc = jnp.pad(misc, ((0, 0), (0, 256 - misc.shape[1])))
    misc = jnp.pad(jnp.concatenate([misc, bias_row]), ((0, -(rows + 1) % 8), (0, 0)))
    misc_near = gather_quad(misc)
    misc_near, *first_ring = fence(misc_near, *first_ring)
    misc_all = gather_ring(misc_near, ring)
    params = misc_all[..., :rows, :].reshape(channels, 256)
    side = params[:, 2 * states :]
    params = params.T.astype(F32)
    taps = params[2 * states : 2 * states + tap_count]
    skip = params[2 * states + tap_count : 2 * states + tap_count + 1]
    side = ordered(
        side.reshape(groups, 2 * rows, -1), flip(side, "c").reshape(groups, 2 * rows, -1), core, 1
    )
    vec_all = side.reshape(width, -1).T.astype(F32)
    up_bias_own = misc_all[..., rows, :up_rows].astype(F32).reshape(1, hidden // 2)

    start = lax.axis_index("y") * block_len
    valid = start + lax.broadcasted_iota(jnp.int32, (block_len, 1), 0) < lengths[0]
    masked = jnp.where(valid, cotangent[0], jnp.zeros((), BF))
    masked, first_pack = fence(masked, first_pack)
    grad_half = swap_cy(masked)

    token_half = swap_cy(tokens[0])
    token_other = flip(token_half, "c")
    tables = dft_tables(length, first_pack)
    tables, first_ring = list(tables), list(first_ring)
    *tables, first_zero, first_half = fence(*tables, *first_ring)
    first_ring = (first_zero, first_half)
    first_one = near_one(first_ring)
    params, up_pack, token_other, grad_half, *first_one = fence(
        params, up_pack, token_other, grad_half, *first_one
    )
    first_two = near_two(first_ring, first_one)
    up_ring = ring_pieces(up_pack, ring)
    kern_re, kern_im = ssm_spectrum(params, states, tables[0], tables[1], length)
    kern_re, token_half = fence(kern_re, token_half)
    token_all, first_rows = first_norm(token_half, token_other, core, vec_all)
    first_rows, *first_two = fence(first_rows, *first_two)
    inputs = token_all.astype(F32)
    grad_all = ordered(grad_half, flip(grad_half, "c"), core, 0).reshape(length, width)
    w_qkv = assemble(
        first_ring, first_one, first_two, ring, ((ring, 2, 2, 2, rows, 3 * channels),), write_heads, "place_heads"
    )[0].reshape(width, 3 * channels)
    w_qkv, *up_ring = fence(w_qkv, *up_ring)
    up_one = near_one(up_ring)

    heads = mm(first_rows, w_qkv).astype(BF)
    heads, *up_one = fence(heads, *up_one)
    up_two = near_two(up_ring, up_one)
    mixed_heads, convolved, shifted, prod_re, prod_im = conv_forward(
        heads, kern_re, kern_im, params, 2 * states, tap_count, tables
    )
    mixed_heads, down_own, *up_two = fence(mixed_heads, down_own, *up_two)
    mixed_other = flip(mixed_heads, "c")
    up_own, out_own = assemble(
        up_ring,
        up_one,
        up_two,
        ring,
        ((ring, 2, 2, 2, rows, hidden // 2), (ring, 2, 2, rows, width)),
        write_up,
        "place_up",
    )
    up_own = up_own.reshape(width, hidden // 2)
    out_own = out_own.reshape(channels, width)
    out_other = flip(out_own, "c")
    residual = inputs + mm(mixed_heads, out_own) + mm(mixed_other, out_other)
    core_id = core.astype(jnp.int32).reshape(1)
    second_rows, activated, slope, down_theirs, mixed_mine = ffn_forward(
        core_id, residual, vec_all, up_own, up_bias_own, down_own
    )

    def mine(array):
        return lax.dynamic_slice_in_dim(array, core * block_len, block_len, 0)

    def theirs(array):
        return lax.dynamic_slice_in_dim(array, (1 - core) * block_len, block_len, 0)

    down_part = mm(activated, down_own)
    slope, down_theirs = fence(slope, down_theirs)
    down_other = flip(down_theirs, "c")
    pre_grad, up_bias_grad, second_theirs, second_mine = ffn_backward(core_id, grad_all, slope, up_own, down_own)
    second_theirs, down_other = fence(second_theirs, down_other)
    second_other = flip(second_theirs, "c")
    mixed = (mixed_mine + down_other.astype(F32)).astype(BF)
    residual_half = mine(residual)
    second_other, mixed = fence(second_other, mixed)
    down_sum = mm_tn(activated, grad_all).astype(BF).reshape(ring, 2, 1, 2, -1, rows, width)
    up_sum = mm_tn(second_rows, pre_grad).astype(BF).reshape(ring, 2, 2, 2, 1, rows, hidden // 2)
    down_sum, up_sum = fence(down_sum, up_sum)

    ffn_one = pair_one(down_sum, up_sum)
    second_grad = second_mine + second_other.astype(F32)
    unit_two_h, scale_two_h = norm_stats(residual_half)
    grad_half_f = grad_half.astype(F32)
    gain_two_grad = jnp.sum(second_grad * unit_two_h, axis=0)
    bias_two_grad = jnp.sum(second_grad, axis=0)
    down_bias_grad = jnp.sum(grad_half_f, axis=0)
    resid_grad = grad_half_f + norm_back(second_grad, unit_two_h, scale_two_h, vec_all[10:11])
    mix_half = resid_grad.astype(BF)
    mix_grad = ordered(mix_half, flip(mix_half, "c"), core, 0).reshape(length, width)

    cos_t, sin_t = tables[0], tables[1]
    query_f, key_f, value_f = [
        heads[:, i * channels : (i + 1) * channels].astype(F32) for i in range(3)
    ]
    padded = jnp.pad(key_f, ((tap_count - 1, 0), (0, 0)))
    convolved, shifted = convolved.astype(F32), shifted.astype(F32)
    prod_re, prod_im, kern_re, kern_im = [
        array.astype(F32) for array in (prod_re, prod_im, kern_re, kern_im)
    ]
    products = shifted * value_f
    head_grad = mm_nt(mix_grad, out_own).astype(BF).astype(F32)
    query_grad = (head_grad * convolved).astype(BF)
    conv_grad = head_grad * query_f
    conv_low = conv_grad.astype(BF)
    skip_grad = jnp.sum(conv_grad * products, axis=0)
    grad_re = mm(cos_t, conv_low)
    grad_im = mm(sin_t, conv_low)
    out_grad = mm_tn(mixed_heads, mix_grad).astype(BF)
    q_grad = mm_tn(first_rows, query_grad).astype(BF)
    back_re = (grad_re * kern_re + grad_im * kern_im).astype(BF)
    back_im = (grad_im * kern_re - grad_re * kern_im).astype(BF)
    lag_re = (grad_re * prod_re + grad_im * prod_im).astype(BF)
    lag_im = (grad_im * prod_re - grad_re * prod_im).astype(BF)
    lag_grad = (mm_tn(lag_re, cos_t) + mm_tn(lag_im, sin_t)) * (1.0 / length)
    lag_sum = lag_grad.astype(BF).reshape(ring, 2, 1, 2, 1, rows, length)
    back = (mm_tn(cos_t, back_re) + mm_tn(sin_t, back_im)) * (1.0 / length)
    product_grad = back + skip * conv_grad
    out_sum = out_grad.reshape(ring, 2, 1, 2, 1, rows, width)
    q_sum = q_grad.reshape(ring, 2, 2, 2, 1, rows, channels)
    shifted_grad = product_grad * value_f
    value_grad = (product_grad * shifted).astype(BF)
    padded_grad = jnp.pad(shifted_grad, ((0, tap_count - 1), (0, 0)))
    key_grad = jnp.zeros_like(key_f)
    tap_rows = []
    for tap in range(tap_count):
        at = tap_count - 1 - tap
        key_grad = key_grad + padded_grad[tap : tap + length] * taps[tap : tap + 1]
        tap_rows.append(jnp.sum(shifted_grad * padded[at : at + length], axis=0))
    key_grad = key_grad.astype(BF)
    kv_grad = jnp.concatenate([key_grad, value_grad], axis=1)
    kv_sum = mm_tn(first_rows, kv_grad).astype(BF).reshape(ring, 2, 2, 2, 1, rows, 2 * channels)
    kv_sum, q_sum, out_sum, lag_sum, kv_grad, *ffn_one = fence(
        kv_sum, q_sum, out_sum, lag_sum, kv_grad, *ffn_one
    )

    lag_width = length // 8
    ffn_two = pair_two(down_sum, up_sum, ffn_one, ring)
    outq_one = direct_one((q_sum, out_sum, lag_sum), ring, lag_width)
    first_part = mm_nt(jnp.concatenate([query_grad, kv_grad], axis=1), w_qkv)
    first_other = flip(theirs(first_part).astype(BF), "c").astype(F32)
    first_grad = mine(first_part) + first_other
    unit_one_h, scale_one_h = norm_stats(token_half.astype(F32))
    gain_one_grad = jnp.sum(first_grad * unit_one_h, axis=0)
    bias_one_grad = jnp.sum(first_grad, axis=0)
    token_grad = resid_grad + norm_back(first_grad, unit_one_h, scale_one_h, vec_all[8:9])
    token_grad = token_grad.astype(BF)

    vec_grads = jnp.stack(
        [gain_one_grad, bias_one_grad, gain_two_grad, bias_two_grad, down_bias_grad]
    )
    vec_grads = vec_grads.reshape(5, groups, 2, 2 * rows)
    vec_keep = lax.dynamic_index_in_dim(vec_grads, core, 2, keepdims=False)
    vec_send = lax.dynamic_index_in_dim(vec_grads, 1 - core, 2, keepdims=False)
    vec_sum = (vec_keep + flip(vec_send, "c")).reshape(5, channels)
    small = jnp.concatenate([vec_sum, jnp.stack(tap_rows), skip_grad[None]])
    small = jnp.concatenate([small.T, up_bias_grad.reshape(channels, -1)], axis=1)
    small = jnp.pad(small, ((0, 0), (0, 128 - small.shape[1]))).astype(BF)
    small_sum = small.reshape(ring, 2, 1, 2, 1, rows, 128)
    small_sum, token_grad, *ffn_two = fence(small_sum, token_grad, *ffn_two)

    ffn_held = pair_three(down_sum, up_sum, ffn_one, ffn_two, ring, width)
    ffn_three = ring_send(ffn_held, ring)
    kv_one = direct_one((kv_sum, small_sum), ring, 128)
    token_grad = swap_cy(token_grad).astype(F32)[None]
    ffn_held, *outq_one = fence(ffn_held, *outq_one)
    outq_held = direct_two((q_sum, out_sum, lag_sum), outq_one, ring, lag_width)
    outq_three = ring_send(outq_held, ring)
    outq_held, *late = fence(outq_held, *kv_one, *ffn_three)
    kv_one, ffn_three = late[:3], late[3:]
    kv_held = direct_two((kv_sum, small_sum), kv_one, ring, 128)
    kv_held, mixed = fence(kv_held, mixed)
    mixed = swap_cy(mixed)[None]
    kv_three = ring_send(kv_held, ring)
    ffn_s = ring_sum(ffn_held, ffn_three)
    down_pieces = up_rows // rows
    down_s = ffn_s[:down_pieces].reshape(up_rows, width)
    up_half = (ffn_s.shape[0] - down_pieces) // 2
    up_s = jnp.stack([join(ffn_s[down_pieces : down_pieces + up_half]), join(ffn_s[down_pieces + up_half :])])
    up_s = merge_columns(up_s, core, groups)
    outq_s = ring_sum(outq_held, outq_three)
    q_pieces = channels // lag_width
    query_s = merge_columns(
        jnp.stack([join(outq_s[:q_pieces]), join(outq_s[q_pieces : 2 * q_pieces])]), core, groups
    )
    out_s = join(outq_s[2 * q_pieces : 4 * q_pieces])
    lag_s = join(outq_s[4 * q_pieces :])
    coef_s, rate_s = ssm_kernel_grads(lag_s, ssm_coef.astype(F32), ssm_rate.astype(F32))
    up_s, down_s, query_s, out_s, coef_s, rate_s, token_grad, *kv_three = fence(
        up_s, down_s, query_s, out_s, coef_s, rate_s, token_grad, *kv_three
    )
    kv_s = ring_sum(kv_held, kv_three)
    pieces = channels // 128

    def heads_of(first):
        both = [join(kv_s[(first + i) * pieces : (first + i + 1) * pieces]) for i in range(2)]
        return jnp.concatenate(both, axis=0)

    heads_s = merge_columns(jnp.stack([heads_of(0), heads_of(2)]), core, groups)
    key_s, value_s = heads_s[:rows], heads_s[rows:]
    small = kv_s[4 * pieces]
    vec_s = small[:, :5].T
    taps_s = small[:, 5 : 5 + tap_count]
    skip_s = small[:, 5 + tap_count]
    up_bias_s = small[:, 6 + tap_count : 6 + tap_count + up_rows // rows].reshape(up_rows)
    return (
        mixed,
        token_grad,
        vec_s[0],
        vec_s[1],
        query_s,
        key_s,
        value_s,
        taps_s,
        coef_s,
        rate_s,
        skip_s,
        out_s,
        vec_s[2],
        vec_s[3],
        up_s,
        up_bias_s,
        down_s,
        vec_s[4],
    )


def solution(mesh):
    dp_size, seq_size = mesh.devices.shape
    ring = dp_size // 4
    grid = Mesh(mesh.devices.reshape(ring, 2, 2, seq_size), ("r", "x", "c", "y"))
    dp = ("r", "x", "c")
    act = P(dp, "y", None)
    vec = P(dp + ("y",))
    mat = P(dp + ("y",), None)
    return jax.shard_map(
        functools.partial(body, ring),
        mesh=grid,
        in_specs=(
            act, P(dp), act, vec, vec, mat, mat, mat, mat, mat, mat, vec, mat, vec, vec, mat, vec, mat, vec,
        ),
        out_specs=(
            act, act, vec, vec, mat, mat, mat, mat, mat, mat, vec, mat, vec, vec, mat, vec, mat, vec,
        ),
        check_vma=False,
    )
```
